32 devices in a mesh: groups: 2 (over y), ctx: 4 (over z), head: 2 (over x), sec: 2 (over core).
Axes of the slice: x: 2, y: 2, z: 4, core: 2. Of those that a mesh axis runs over, the one named last changes fastest.
Arguments:
- queries: bfloat16 [256, 8192], P(('groups', 'ctx'), ('head', 'sec')), parts along dimension 0, may hold values from -128 to 128
- key_cache: bfloat16 [16384, 1024], P(('groups', 'ctx'), ('head', 'sec')), parts along dimension 0, may hold values from -4.5 to 4.5
- value_cache: bfloat16 [16384, 1024], P(('groups', 'ctx'), ('head', 'sec')), parts along dimension 0, may hold values from -6 to 6
- block_index: int32 [2, 8], P('groups'), parts along dimension 0, may hold values from 0 to 63, as said below
- stream: bfloat16 [256, 8192], P(('groups', 'head', 'sec'), 'ctx'), parts along dimension 0, may hold values from -6 to 6
- out_weight: bfloat16 [8192, 8192], P(('head', 'sec'), 'ctx'), may hold values from -0.0625 to 0.0625
- norm_gain: float32 [8192], replicated, may hold values from 0.5 to 1.5
- gate_weight: bfloat16 [8192, 14336], P(('head', 'sec'), 'ctx'), may hold values from -0.0625 to 0.0625
- up_weight: bfloat16 [8192, 14336], P(('head', 'sec'), 'ctx'), may hold values from -0.0625 to 0.0625
- down_weight: bfloat16 [14336, 8192], P('ctx', ('head', 'sec')), may hold values from -0.046875 to 0.046875
Outputs:
- layer_out: bfloat16 [256, 8192], P(('groups', 'ctx'), ('head', 'sec')), parts along dimension 0
The draws below stay inside these ranges and needn't reach their ends.
There are 2 independent parts, one for each index of `groups`. The reference program is written for one: setup_inputs(seed, part) draws one part's arguments, and reference() takes and returns one part's arrays. A program takes and returns all parts, laid end to end along the dimension named above; an argument that names none is the same for every part. Nothing has to cross between parts.
Inputs may be any that keep to these rules, and one draw needn't show every extreme that they name: `block_index`: row b lists 8 distinct key blocks in increasing order, none after the block 63 + b, and includes that block and block 0. Of the aligned runs of 16 key blocks (k * 16 to (k + 1) * 16 - 1), each holds at least one of a row's blocks and at most 4, and in every row some run holds exactly 4.
All inputs are finite; a program needn't handle non-finite values.
Results may differ from the reference program's by a relative error of at most 0.014.
Values may be sent and summed in bfloat16 or wider, within the bound.
No kernel may reach another device: no remote copies, remote signals or barrier semaphores. Data moves between devices by JAX's collectives and lax.ppermute only.
A program may use at most 128 MiB of HBM per device.

```python
import math
from functools import partial
import jax
import jax.numpy as jnp
from jax import lax

D = 8192
HQ = 64
KVH = 8
DH = 128
FF = 14336
KB = 128
MOST = 4
TOK = 128
KB_DEV = 16
QB = 1
NKB = 64
CTX = 8192
SEL = 8


def draw_queries(key, part):
    base_draw = jnp.clip(2.0 * jax.random.normal(jax.random.fold_in(key, 5), (TOK, HQ * DH), jnp.float32), -9.0, 9.0)
    return base_draw.astype(jnp.bfloat16)


def draw_key_cache(key, part):
    base_draw = jnp.clip(jax.random.normal(jax.random.fold_in(key, 6), (CTX, KVH * DH), jnp.float32), -4.5, 4.5)
    return base_draw.astype(jnp.bfloat16)


def draw_block_index(key, part):
    base_key = jax.random.fold_in(key, 31)
    shards = NKB // KB_DEV
    spare = SEL - MOST - 1 - (shards - 2)

    def one_row(row_num):
        row_key = jax.random.fold_in(base_key, row_num)
        hot_shard = jax.random.randint(jax.random.fold_in(row_key, 1), (), 0, shards - 1, dtype=jnp.int32)
        order = jax.random.permutation(jax.random.fold_in(row_key, 2), shards - 2).astype(jnp.int32)
        others = jnp.arange(shards - 2, dtype=jnp.int32)
        others = others + (others >= hot_shard).astype(jnp.int32)
        extra = spare // (shards - 2) + (jnp.arange(shards - 2, dtype=jnp.int32) < spare % (shards - 2)).astype(jnp.int32)
        counts = jnp.zeros((shards,), jnp.int32).at[others[order]].set(1 + extra)
        counts = counts.at[hot_shard].set(MOST).at[shards - 1].set(1)
        local = jnp.arange(KB_DEV, dtype=jnp.int32)
        scores = jax.random.randint(jax.random.fold_in(row_key, 3), (shards, KB_DEV), 0, 1 << 20, dtype=jnp.int32) * KB_DEV + local[None, :]
        own_local = KB_DEV - QB + row_num
        last_scores = jnp.where(local == own_local, -1, jnp.where(local > own_local, 1 << 30, scores[shards - 1]))
        scores = scores.at[shards - 1].set(last_scores.astype(jnp.int32))
        scores = scores.at[0, 0].set(-1)
        ranked = jnp.argsort(scores, axis=1).astype(jnp.int32)
        picked = jnp.arange(shards, dtype=jnp.int32)[:, None] * KB_DEV + ranked
        chosen = local[None, :] < counts[:, None]
        flat = jnp.where(chosen, picked, NKB + picked).reshape(-1)
        return jnp.sort(flat)[:SEL]
    return jax.vmap(one_row)(jnp.arange(QB, dtype=jnp.int32)).astype(jnp.int32)


def draw_stream(key, part):
    row_scale = jnp.exp(jax.random.uniform(jax.random.fold_in(key, 1), (TOK, 1), jnp.float32, math.log(0.1), 0.0))
    col_scale = jnp.exp(jax.random.uniform(jax.random.fold_in(key, 2), (1, D), jnp.float32, math.log(0.3), 0.0))
    col_scale = col_scale * (0.5 + 1.5 * jnp.arange(D, dtype=jnp.float32)[None, :] / D)
    noise = jax.random.normal(jax.random.fold_in(key, 3), (TOK, D), jnp.float32)
    return jnp.clip(1.5 * noise * row_scale * col_scale, -6.0, 6.0).astype(jnp.bfloat16)


def block_scale(key, shape, split, low, top_value):
    def one(axis_at, blocks):
        steps = jax.random.uniform(jax.random.fold_in(jax.random.fold_in(key, 6), axis_at), (blocks,), jnp.float32, low / len(split), top_value / len(split))
        return jnp.repeat(jnp.exp(steps), shape[axis_at] // blocks).reshape((-1,) + (1,) * (len(shape) - axis_at - 1))

    factor_of = one(*split[0])
    for cut in split[1:]:
        factor_of = factor_of * one(*cut)
    return factor_of


def bell_draw(stream_key, shape, width, limit, pieces=(), held_as=jnp.bfloat16):
    values = jax.random.normal(stream_key, shape, jnp.float32) * width
    if len(pieces) > 0:
        values = block_scale(stream_key, shape, pieces, -0.22, 0.18) * values
    return jnp.clip(values, min=-limit, max=limit).astype(held_as)


def setup_inputs(seed: int = 0, part: int = 0) -> dict:
    seeds = jax.random.split(jax.random.key(seed), 11)
    part_keys = jax.random.split(jax.random.fold_in(seeds[10], part), 11)
    return {
        "queries": draw_queries(jax.random.fold_in(jax.random.fold_in(seeds[10], part), 71), part),
        "key_cache": draw_key_cache(jax.random.fold_in(jax.random.fold_in(seeds[10], part), 71), part),
        "value_cache": bell_draw(part_keys[2], (CTX, KVH * DH), 1.0, 6.0, ((0, 4), (1, 4))),
        "block_index": draw_block_index(jax.random.fold_in(jax.random.fold_in(seeds[10], part), 71), part),
        "stream": draw_stream(jax.random.fold_in(jax.random.fold_in(seeds[10], part), 71), part),
        "out_weight": bell_draw(seeds[5], (HQ * DH, D), (HQ * DH) ** -0.5, 0.0625, ((0, 4), (1, 4))),
        "norm_gain": jnp.clip(1.0 + 0.1 * jax.random.normal(seeds[6], (D,), jnp.float32), 0.5, 1.5),
        "gate_weight": bell_draw(seeds[7], (D, FF), D ** -0.5, 0.0625, ((0, 4), (1, 4))),
        "up_weight": bell_draw(seeds[8], (D, FF), D ** -0.5, 0.0625, ((0, 4), (1, 4))),
        "down_weight": bell_draw(seeds[9], (FF, D), FF ** -0.5, 0.046875, ((0, 4), (1, 4))),
    }


def attend_block(queries, key_cache, value_cache, block_index, block_num):
    group_size = HQ // KVH
    chosen = block_index[block_num]
    key_pos = (chosen[:, None] * KB + jnp.arange(KB, dtype=jnp.int32)[None, :]).reshape(-1).astype(jnp.int32)
    picked_keys = key_cache[key_pos].astype(jnp.float32).reshape(-1, KVH, DH)
    picked_values = value_cache[key_pos].astype(jnp.float32).reshape(-1, KVH, DH)
    query_block = lax.dynamic_slice_in_dim(queries, (block_num * KB).astype(jnp.int32), KB, 0)
    query_block = query_block.astype(jnp.float32).reshape(KB, KVH, group_size, DH)
    scores = jnp.einsum('qhgd,phd->hgqp', query_block, picked_keys) / math.sqrt(DH)
    query_pos = (CTX - TOK + block_num * KB + jnp.arange(KB, dtype=jnp.int32)).astype(jnp.int32)
    allowed = key_pos[None, :] <= query_pos[:, None]
    scores = jnp.where(allowed[None, None], scores, -jnp.inf)
    peak_score = lax.optimization_barrier(jnp.max(scores, axis=-1, keepdims=True))
    unnormed = jnp.exp(scores - peak_score)
    row_total = lax.optimization_barrier(jnp.sum(unnormed, axis=-1))
    rounded = lax.optimization_barrier(unnormed.astype(jnp.bfloat16)).astype(jnp.float32)
    mixture = jnp.einsum('hgqp,phd->qhgd', rounded, picked_values)
    result = mixture / jnp.transpose(row_total, (2, 0, 1))[..., None]
    return result.reshape(KB, HQ * DH).astype(jnp.bfloat16)

def reference(queries, key_cache, value_cache, block_index, stream, out_weight, norm_gain, gate_weight, up_weight, down_weight):
    attention = lax.map(partial(attend_block, queries, key_cache, value_cache, block_index), jnp.arange(QB, dtype=jnp.int32)).reshape(TOK, HQ * DH)
    projected = jnp.dot(attention, out_weight, preferred_element_type=jnp.float32)
    middle = lax.optimization_barrier((stream.astype(jnp.float32) + projected).astype(jnp.bfloat16))
    middle_wide = middle.astype(jnp.float32)
    mean_square = lax.optimization_barrier(jnp.mean(middle_wide * middle_wide, axis=-1, keepdims=True))
    normed = (middle_wide * lax.rsqrt(mean_square + 1e-05) * norm_gain).astype(jnp.bfloat16)
    gate_val = jnp.dot(normed, gate_weight, preferred_element_type=jnp.float32)
    up_val = jnp.dot(normed, up_weight, preferred_element_type=jnp.float32)
    hidden = (jax.nn.silu(gate_val) * up_val).astype(jnp.bfloat16)
    down_part = jnp.dot(hidden, down_weight, preferred_element_type=jnp.float32)
    return (middle_wide + down_part).astype(jnp.bfloat16)
```

```python
import functools
import math

import jax
import jax.numpy as jnp
from jax import lax
from jax.experimental import pallas as pl
from jax.experimental.pallas import tpu as pltpu
from jax.sharding import PartitionSpec as P

HQ = 64
KVH = 8
DH = 128
KB = 128
MOST = 4
LANES = 128
EPS = 1e-05
HS = ("head", "sec")
ALL = ("ctx", "head", "sec")


VM = pl.BlockSpec(memory_space=pltpu.VMEM)
SM = pl.BlockSpec(memory_space=pltpu.SMEM)
ANY = pl.BlockSpec(memory_space=pl.ANY)
F32 = jnp.float32
BF16 = jnp.bfloat16


def struct(shape, dtype):
    return jax.ShapeDtypeStruct(shape, dtype)


def call(kernel, out, in_specs, args, flops=0, scratch=(), vmem=8, name=None):
    outs = out if isinstance(out, (tuple, list)) else (out,)
    nbytes = sum(math.prod(a.shape) * a.dtype.itemsize for a in args)
    nbytes += sum(math.prod(o.shape) * o.dtype.itemsize for o in outs)
    return pl.pallas_call(
        kernel,
        out_shape=out,
        in_specs=in_specs,
        out_specs=jax.tree.map(lambda _: VM, out),
        scratch_shapes=scratch,
        compiler_params=pltpu.CompilerParams(vmem_limit_bytes=vmem << 20),
        cost_estimate=pl.CostEstimate(flops=flops, bytes_accessed=nbytes, transcendentals=0),
        name=name,
    )(*args)


def in_vmem(x):
    return pltpu.with_memory_space_constraint(x, pltpu.VMEM)


def slots(index_ref, shard, blocks):
    first = jnp.int32(0)
    count = jnp.int32(0)
    for n in range(index_ref.shape[1]):
        block = index_ref[0, n]
        first += (block < shard * blocks).astype(jnp.int32)
        count += (block < (shard + 1) * blocks).astype(jnp.int32)
    return first, count - first


def slot_block(index_ref, first, count, slot, shard, blocks):
    entry = jnp.minimum(first + slot, index_ref.shape[1] - 1)
    local = jnp.clip(index_ref[0, entry] - shard * blocks, 0, blocks - 1)
    return local, slot < count


def pick_kernel(index_ref, meta_ref, key_ref, value_ref, key_out, value_out, sems):
    blocks = key_ref.shape[0] // KB
    shard = meta_ref[0]
    first, count = slots(index_ref, shard, blocks)
    copies = []
    for slot in range(MOST):
        local, _ = slot_block(index_ref, first, count, slot, shard, blocks)
        rows = pl.ds(pl.multiple_of(local * KB, KB), KB)
        for n, (src, dst) in enumerate(((key_ref, key_out), (value_ref, value_out))):
            copy = pltpu.make_async_copy(
                src.at[rows, :], dst.at[slot * KB : (slot + 1) * KB, :], sems.at[n, slot]
            )
            copy.start()
            copies.append(copy)
    for copy in copies:
        copy.wait()


def attend_kernel(offset, blocks, context_len, total, index_ref, meta_ref, q_ref, key_ref, value_ref, out_ref):
    rows = q_ref.shape[0]
    heads = q_ref.shape[1] // DH
    kv_dev = key_ref.shape[1] // DH
    group = heads // kv_dev
    shard = meta_ref[0]
    token0 = context_len - total + (shard ^ offset) * rows
    first, count = slots(index_ref, shard, blocks)
    limits = []
    for slot in range(MOST):
        local, valid = slot_block(index_ref, first, count, slot, shard, blocks)
        limit = token0 - (shard * blocks + local) * KB
        limits.append(jnp.where(valid, limit, jnp.int32(-(1 << 20))))
    row = lax.broadcasted_iota(jnp.int32, (group * rows, KB), 0) % rows
    lane = lax.broadcasted_iota(jnp.int32, (group * rows, KB), 1)
    ahead = lane - row
    head_lane = lax.broadcasted_iota(jnp.int32, (rows, LANES), 1)
    lse_tile = jnp.zeros((rows, LANES), F32)
    for kv in range(kv_dev):
        stacked = jnp.concatenate(
            [q_ref[:, (kv * group + h) * DH : (kv * group + h + 1) * DH] for h in range(group)], axis=0
        )
        scores = lax.dot_general(
            stacked,
            key_ref[:, kv * DH : (kv + 1) * DH],
            (((1,), (1,)), ((), ())),
            preferred_element_type=F32,
        ) * (1.0 / math.sqrt(DH))
        parts = [
            jnp.where(ahead <= limits[slot], scores[:, slot * KB : (slot + 1) * KB], -1e30)
            for slot in range(MOST)
        ]
        peak = functools.reduce(jnp.maximum, parts)
        peak = jnp.max(peak, axis=1, keepdims=True)
        parts = [jnp.exp(p - peak) for p in parts]
        row_total = jnp.sum(functools.reduce(jnp.add, parts), axis=1, keepdims=True)
        weights = jnp.concatenate([p.astype(BF16) for p in parts], axis=1)
        mixture = jnp.dot(
            weights, value_ref[:, kv * DH : (kv + 1) * DH], preferred_element_type=F32
        )
        mixture = (mixture / row_total).astype(BF16)
        lse = peak + jnp.log(row_total)
        for h in range(group):
            head = kv * group + h
            span = slice(h * rows, (h + 1) * rows)
            out_ref[:, head * DH : (head + 1) * DH] = mixture[span]
            lse_tile = jnp.where(head_lane == head, lse[span], lse_tile)
    high = lse_tile.astype(BF16).astype(F32)
    rest = lse_tile - high
    mid = rest.astype(BF16).astype(F32)
    low = rest - mid
    tile = high + pltpu.roll(mid, heads, 1) + pltpu.roll(low, 2 * heads, 1)
    out_ref[:, heads * DH :] = tile.astype(BF16)


def blend_kernel(*refs):
    out_ref = refs[-1]
    parts = refs[:-1]
    heads = out_ref.shape[1] // DH
    logs = []
    for part in parts:
        tile = part[:, heads * DH :].astype(F32)
        logs.append(
            tile + pltpu.roll(tile, LANES - heads, 1) + pltpu.roll(tile, LANES - 2 * heads, 1)
        )
    peak = functools.reduce(jnp.maximum, logs)
    shares = [jnp.exp(log - peak) for log in logs]
    total = functools.reduce(jnp.add, shares)
    shares = [share / total for share in shares]
    for head in range(heads):
        span = slice(head * DH, (head + 1) * DH)
        out_ref[:, span] = functools.reduce(
            jnp.add,
            [share[:, head : head + 1] * part[:, span].astype(F32) for share, part in zip(shares, parts)],
        ).astype(BF16)


def project_kernel(n_sec, tile, meta_ref, *refs):
    pieces, (weight_ref, keep_ref, send_ref, rows_ref) = refs[:-4], refs[-4:]
    rows = pieces[0].shape[0]
    shard, sec = meta_ref[0], meta_ref[2]
    for n, piece in enumerate(pieces):
        rows_ref[n * rows : (n + 1) * rows, :] = piece[...]

    @pl.loop(0, weight_ref.shape[1] // tile)
    def _(step):
        columns = pl.ds(pl.multiple_of(step * tile, tile), tile)
        part = jnp.dot(rows_ref[...], weight_ref[:, columns], preferred_element_type=F32)
        for n in range(len(pieces)):
            owner = shard ^ n
            block = part[n * rows : (n + 1) * rows]

            @pl.when(owner % n_sec == sec)
            def _():
                keep_ref[owner // n_sec, :, columns] = block

            @pl.when(owner % n_sec != sec)
            def _():
                send_ref[owner // n_sec, :, columns] = block.astype(BF16)


def fold_kernel(meta_ref, keep_ref, got_ref, keep_out, send_out):
    head = meta_ref[1]
    keep_out[...] = keep_ref[head] + got_ref[head].astype(F32)
    send_out[...] = (keep_ref[1 - head] + got_ref[1 - head].astype(F32)).astype(BF16)


def middle_kernel(stream_ref, keep_ref, got_ref, out_ref):
    out_ref[...] = (
        stream_ref[...].astype(F32) + (keep_ref[...] + got_ref[...].astype(F32))
    ).astype(BF16)


def put_exact(ref, index, value):
    high = value.astype(BF16)
    ref[index + (slice(0, LANES),)] = high
    ref[index + (slice(LANES, 2 * LANES),)] = (value - high.astype(F32)).astype(BF16)


def take_exact(tile):
    return tile[:, :LANES].astype(F32) + tile[:, LANES:].astype(F32)


def gate_kernel(n_sec, start, width, tile, with_norm, meta_ref, *refs):
    pieces = refs[:4]
    gain_ref, gate_ref, up_ref = refs[4:7]
    outs, rows_ref = refs[7:-1], refs[-1]
    keep_ref, send_ref = outs[:2]
    rows = pieces[0].shape[0]
    shard, sec = meta_ref[0], meta_ref[2]
    for n, piece in enumerate(pieces):
        wide = piece[...].astype(F32)
        rows_ref[n * rows : (n + 1) * rows, :] = (wide * gain_ref[...]).astype(BF16)
        if with_norm:
            square = jnp.broadcast_to(jnp.sum(wide * wide, axis=1, keepdims=True), (rows, LANES))
            owner = shard ^ n

            @pl.when(owner % n_sec == sec)
            def _():
                outs[2][owner // n_sec] = square

            @pl.when(owner % n_sec != sec)
            def _():
                put_exact(outs[3], (owner // n_sec, slice(None)), square)

    @pl.loop(0, width // tile)
    def _(step):
        for base, weight_ref in ((0, gate_ref), (width, up_ref)):
            source = pl.ds(pl.multiple_of(start + step * tile, tile), tile)
            target = pl.ds(pl.multiple_of(base + step * tile, tile), tile)
            part = jnp.dot(rows_ref[...], weight_ref[:, source], preferred_element_type=F32)
            for n in range(len(pieces)):
                owner = shard ^ n
                block = part[n * rows : (n + 1) * rows]

                @pl.when(owner % n_sec == sec)
                def _():
                    keep_ref[owner // n_sec, :, target] = block

                @pl.when(owner % n_sec != sec)
                def _():
                    send_ref[owner // n_sec, :, target] = block.astype(BF16)


def fold_norm_kernel(meta_ref, keep_ref, got_ref, keep_out, send_out):
    head = meta_ref[1]
    keep_out[...] = keep_ref[head] + take_exact(got_ref[head])
    put_exact(send_out, (slice(None),), keep_ref[1 - head] + take_exact(got_ref[1 - head]))


def hidden_kernel(model, keep_ref, got_ref, square_ref, square_got_ref, out_ref):
    width = out_ref.shape[1]
    square = square_ref[...] + take_exact(square_got_ref[...])
    scale = lax.rsqrt(square / model + EPS)
    for at in range(0, width, LANES):
        gate = keep_ref[:, at : at + LANES] + got_ref[:, at : at + LANES].astype(F32)
        up = keep_ref[:, width + at : width + at + LANES] + got_ref[
            :, width + at : width + at + LANES
        ].astype(F32)
        gate = gate * scale
        out_ref[:, at : at + LANES] = (
            gate / (1.0 + jnp.exp(-gate)) * (up * scale)
        ).astype(BF16)


def down_kernel(n_chunk, tile, meta_ref, *refs):
    pieces = refs[: 4 * n_chunk]
    weight_ref, own_ref = refs[4 * n_chunk : 4 * n_chunk + 2]
    sends, rows_ref = refs[4 * n_chunk + 2 : -1], refs[-1]
    rows = pieces[0].shape[0]
    width = pieces[0].shape[1]
    shard, place = meta_ref[0], meta_ref[3]
    for n in range(4):
        at = pl.ds(pl.multiple_of((shard ^ place ^ n) * rows, rows), rows)
        for c in range(n_chunk):
            rows_ref[at, c * width : (c + 1) * width] = pieces[n * n_chunk + c][...]

    @pl.loop(0, weight_ref.shape[1] // tile)
    def _(step):
        columns = pl.ds(pl.multiple_of(step * tile, tile), tile)
        part = jnp.dot(rows_ref[...], weight_ref[:, columns], preferred_element_type=F32)
        own_ref[:, columns] = part[:rows]
        for n, send in enumerate(sends):
            send[:, columns] = part[(n + 1) * rows : (n + 2) * rows].astype(BF16)


def final_kernel(middle_ref, own_ref, *refs):
    parts, out_ref = refs[:-1], refs[-1]
    total = own_ref[...]
    for part in parts:
        total = total + part[...].astype(F32)
    out_ref[...] = (middle_ref[...].astype(F32) + total).astype(BF16)


def swap(x, axis):
    return lax.ppermute(x, axis, [(0, 1), (1, 0)])


def turn(x, axis, n, offset):
    return lax.ppermute(x, axis, [(i, i ^ offset) for i in range(n)])


def direct_body(
    queries,
    key_cache,
    value_cache,
    block_index,
    stream,
    out_weight,
    norm_gain,
    gate_weight,
    up_weight,
    down_weight,
):
    n_context, n_head, n_sec = (lax.axis_size(a) for a in ALL)
    shard, head, sec = (lax.axis_index(a) for a in ALL)
    place = head * n_sec + sec
    meta = jnp.stack([shard, head, sec, place]).astype(jnp.int32)
    rows, heads_width = queries.shape
    context_len = key_cache.shape[0] * n_context
    model = norm_gain.shape[0]
    total = rows * n_context
    blocks = key_cache.shape[0] // KB
    kv_width = key_cache.shape[1]
    order = (3, 1, 2)

    got_q = {m: turn(queries, "ctx", n_context, m) for m in order}
    got_q[0] = queries
    picked = struct((MOST * KB, kv_width), BF16)
    keys, values = call(
        pick_kernel,
        (picked, picked),
        [SM, SM, ANY, ANY],
        (block_index, meta, key_cache, value_cache),
        scratch=[pltpu.SemaphoreType.DMA((2, MOST))],
        name="pick",
    )
    partial = {}
    for m in (0,) + order:
        partial[m] = call(
            functools.partial(attend_kernel, m, blocks, context_len, total),
            struct((rows, heads_width + LANES), BF16),
            [SM, SM, VM, VM, VM],
            (block_index, meta, got_q[m], keys, values),
            flops=4 * rows * heads_width * MOST * KB,
            name=f"attend{m}",
        )
    back = {m: turn(partial[m], "ctx", n_context, m) for m in order}
    back[0] = partial[0]
    blended = call(
        blend_kernel,
        struct((rows, heads_width), BF16),
        [VM] * 4,
        tuple(back[m] for m in range(4)),
        name="blend",
    )

    attention = {m: turn(blended, "ctx", n_context, m) for m in order}
    attention[0] = blended
    width = out_weight.shape[1]
    keep, send = call(
        functools.partial(project_kernel, n_sec, 512),
        (struct((n_head, rows, width), F32), struct((n_head, rows, width), BF16)),
        [SM] + [VM] * 5,
        (meta,) + tuple(attention[m] for m in range(4)) + (in_vmem(out_weight),),
        flops=2 * total * heads_width * width,
        scratch=[pltpu.VMEM((total, heads_width), BF16)],
        name="project",
    )
    got = swap(send, "sec")
    keep, send = call(
        fold_kernel,
        (struct((rows, width), F32), struct((rows, width), BF16)),
        [SM, VM, VM],
        (meta, keep, got),
        name="fold",
    )
    got = swap(send, "head")
    middle = call(
        middle_kernel, struct((rows, width), BF16), [VM] * 3, (stream, keep, got), name="middle"
    )

    middle = lax.ppermute(
        middle,
        ALL,
        [(a * n_context + b, b * n_context + a) for a in range(n_context) for b in range(n_context)],
    )
    all_middle = {m: turn(middle, "ctx", n_context, m) for m in order}
    all_middle[0] = middle
    gain = lax.dynamic_slice_in_dim(norm_gain, place * width, width, 0)[None]
    hidden_width = gate_weight.shape[1]
    n_chunk = 2
    chunk = hidden_width // n_chunk
    hidden = []
    gate_vmem, up_vmem = in_vmem(gate_weight), in_vmem(up_weight)
    square = None
    for c in range(n_chunk):
        out = [struct((n_head, rows, 2 * chunk), F32), struct((n_head, rows, 2 * chunk), BF16)]
        if c == 0:
            out += [struct((n_head, rows, LANES), F32), struct((n_head, rows, 2 * LANES), BF16)]
        res = call(
            functools.partial(gate_kernel, n_sec, c * chunk, chunk, 256, c == 0),
            tuple(out),
            [SM] + [VM] * 7,
            (meta,) + tuple(all_middle[m] for m in range(4)) + (gain, gate_vmem, up_vmem),
            flops=4 * total * width * chunk,
            scratch=[pltpu.VMEM((total, width), BF16)],
            name=f"gate{c}",
        )
        keep, send = res[:2]
        if c == 0:
            square_keep, square_send = call(
                fold_norm_kernel,
                (struct((rows, LANES), F32), struct((rows, 2 * LANES), BF16)),
                [SM, VM, VM],
                (meta, res[2], swap(res[3], "sec")),
                name="fold_norm",
            )
            square = (square_keep, swap(square_send, "head"))
        keep, send = call(
            fold_kernel,
            (struct((rows, 2 * chunk), F32), struct((rows, 2 * chunk), BF16)),
            [SM, VM, VM],
            (meta, keep, swap(send, "sec")),
            name=f"fold{c}",
        )
        own = call(
            functools.partial(hidden_kernel, model),
            struct((rows, chunk), BF16),
            [VM] * 4,
            (keep, swap(send, "head")) + square,
            name=f"hidden{c}",
        )
        across = swap(own, "head")
        hidden.append((own, swap(own, "sec"), across, swap(across, "sec")))

    out_width = down_weight.shape[1]
    res = call(
        functools.partial(down_kernel, n_chunk, 512),
        (struct((rows, out_width), F32),) + (struct((rows, out_width), BF16),) * 3,
        [SM] + [VM] * (4 * n_chunk + 1),
        (meta,)
        + tuple(hidden[c][n] for n in range(4) for c in range(n_chunk))
        + (in_vmem(down_weight),),
        flops=2 * total * hidden_width * out_width,
        scratch=[pltpu.VMEM((total, hidden_width), BF16)],
        name="down",
    )
    parts = [turn(res[m], "ctx", n_context, m) for m in order]
    return call(
        final_kernel, struct((rows, out_width), BF16), [VM] * 5, (middle, res[0]) + tuple(parts), name="final"
    )


def local_attention(gathered, key_cache, value_cache, block_index, context_index, context_len):
    group_size = HQ // KVH
    kv_dev = key_cache.shape[1] // DH
    blocks_dev = key_cache.shape[0] // KB
    total_tokens = gathered.shape[0]
    key_blocks = key_cache.reshape(blocks_dev, KB, kv_dev, DH)
    value_blocks = value_cache.reshape(blocks_dev, KB, kv_dev, DH)
    local_ids = context_index * blocks_dev + jnp.arange(blocks_dev, dtype=jnp.int32)
    member = jnp.any(block_index[:, :, None] == local_ids[None, None, :], axis=1)
    member_rank = jnp.cumsum(member.astype(jnp.int32), axis=1) - 1
    slot_hit = member[:, None, :] & (
        member_rank[:, None, :] == jnp.arange(MOST, dtype=jnp.int32)[None, :, None]
    )
    slot_block = jnp.sum(
        jnp.where(slot_hit, jnp.arange(blocks_dev, dtype=jnp.int32)[None, None, :], 0), axis=2
    )
    slot_valid = jnp.any(slot_hit, axis=2)
    picked_keys = jnp.take(key_blocks, slot_block[0], axis=0).reshape(MOST * KB, kv_dev, DH)
    picked_values = jnp.take(value_blocks, slot_block[0], axis=0).reshape(MOST * KB, kv_dev, DH)
    key_pos = (
        (local_ids[0] + slot_block[0])[:, None] * KB + jnp.arange(KB, dtype=jnp.int32)[None, :]
    ).reshape(-1)
    live_keys = jnp.broadcast_to(slot_valid[0][:, None], (MOST, KB)).reshape(-1)
    query_pos = context_len - total_tokens + jnp.arange(KB, dtype=jnp.int32)
    allowed = live_keys[None, :] & (key_pos[None, :] <= query_pos[:, None])
    query_block = gathered.reshape(KB, kv_dev, group_size, DH)
    scores = jnp.einsum(
        "qhgd,phd->hgqp", query_block, picked_keys, preferred_element_type=jnp.float32
    ) / math.sqrt(DH)
    scores = jnp.where(allowed[None, None], scores, -jnp.inf)
    peak_score = jnp.max(scores, axis=-1, keepdims=True)
    unnormed = jnp.exp(scores - peak_score)
    row_total = jnp.sum(unnormed, axis=-1)
    mixture = jnp.einsum(
        "hgqp,phd->qhgd",
        unnormed.astype(jnp.bfloat16),
        picked_values,
        preferred_element_type=jnp.float32,
    )
    result = mixture / jnp.transpose(row_total, (2, 0, 1))[..., None]
    log_total = jnp.transpose(peak_score[..., 0] + jnp.log(row_total), (2, 0, 1))
    out_list = result.reshape(KB, -1)
    lse_list = log_total.reshape(KB, -1)
    return (out_list, lse_list)


def general_body(
    queries,
    key_cache,
    value_cache,
    block_index,
    stream,
    out_weight,
    norm_gain,
    gate_weight,
    up_weight,
    down_weight,
):
    n_context = lax.axis_size("ctx")
    context_index = lax.axis_index("ctx")
    context_len = key_cache.shape[0] * n_context
    gathered = lax.all_gather(queries, "ctx", axis=0, tiled=True)
    part_out, part_lse = local_attention(
        gathered, key_cache, value_cache, block_index, context_index, context_len
    )
    spread_out, spread_lse = (
        lax.all_to_all(part_out[:, None, :], "ctx", split_axis=0, concat_axis=1, tiled=True),
        lax.all_to_all(part_lse[:, None, :], "ctx", split_axis=0, concat_axis=1, tiled=True),
    )
    share_rows = spread_out.shape[0]
    head_count = spread_lse.shape[2]
    peak_value = jnp.max(spread_lse, axis=1, keepdims=True)
    share_weight = jnp.exp(spread_lse - peak_value)
    blended = jnp.sum(
        spread_out.reshape(share_rows, n_context, head_count, -1) * share_weight[..., None], axis=1
    )
    blended = blended / jnp.sum(share_weight, axis=1)[..., None]
    attention = lax.all_gather(
        blended.reshape(share_rows, -1).astype(jnp.bfloat16), "ctx", axis=0, tiled=True
    )
    row_piece = attention
    projected = lax.psum_scatter(
        jnp.dot(row_piece, out_weight, preferred_element_type=jnp.float32),
        ("head", "sec"),
        scatter_dimension=0,
        tiled=True,
    )
    middle = (stream.astype(jnp.float32) + projected).astype(jnp.bfloat16)
    full_middle = lax.all_gather(middle, "ctx", axis=1, tiled=True)
    middle_wide = full_middle.astype(jnp.float32)
    mean_square = jnp.mean(middle_wide * middle_wide, axis=-1, keepdims=True)
    normed = (middle_wide * lax.rsqrt(mean_square + 1e-05) * norm_gain).astype(jnp.bfloat16)
    normed_cols, middle_cols = (
        lax.all_to_all(normed, ("head", "sec"), split_axis=1, concat_axis=0, tiled=True),
        lax.all_to_all(full_middle, ("head", "sec"), split_axis=1, concat_axis=0, tiled=True),
    )
    row_piece = normed_cols
    gate_up = lax.psum_scatter(
        jnp.concatenate(
            [
                jnp.dot(row_piece, gate_weight, preferred_element_type=jnp.float32),
                jnp.dot(row_piece, up_weight, preferred_element_type=jnp.float32),
            ],
            axis=1,
        ),
        ("head", "sec"),
        scatter_dimension=0,
        tiled=True,
    )
    hidden_width = gate_weight.shape[1]
    hidden = (jax.nn.silu(gate_up[:, :hidden_width]) * gate_up[:, hidden_width:]).astype(
        jnp.bfloat16
    )
    all_hidden = lax.all_gather(hidden, ("head", "sec"), axis=0, tiled=True)
    row_piece = all_hidden
    down_part = lax.psum_scatter(
        jnp.dot(row_piece, down_weight, preferred_element_type=jnp.float32),
        "ctx",
        scatter_dimension=0,
        tiled=True,
    )
    own_middle = lax.dynamic_slice_in_dim(
        middle_cols, context_index * down_part.shape[0], down_part.shape[0], 0
    )
    return (own_middle.astype(jnp.float32) + down_part).astype(jnp.bfloat16)


def solution(mesh):
    size = dict(mesh.shape)
    direct = size["ctx"] == 4 and size["head"] == 2 and size["sec"] == 2
    return jax.shard_map(
        direct_body if direct else general_body,
        mesh=mesh,
        in_specs=(
            P(("groups", "ctx"), ("head", "sec")),
            P(("groups", "ctx"), ("head", "sec")),
            P(("groups", "ctx"), ("head", "sec")),
            P("groups", None),
            P(("groups", "head", "sec"), "ctx"),
            P(("head", "sec"), "ctx"),
            P(),
            P(("head", "sec"), "ctx"),
            P(("head", "sec"), "ctx"),
            P("ctx", ("head", "sec")),
        ),
        out_specs=P(("groups", "ctx"), ("head", "sec")),
        check_vma=False,
    )
```

```python
import functools
import math

import jax
import jax.numpy as jnp
from jax import lax
from jax.experimental import pallas as pl
from jax.experimental.pallas import tpu as pltpu
from jax.sharding import PartitionSpec as P

HQ = 64
KVH = 8
DH = 128
KB = 128
MOST = 4
LANES = 128
EPS = 1e-05
HS = ("head", "sec")
ALL = ("ctx", "head", "sec")


VM = pl.BlockSpec(memory_space=pltpu.VMEM)
SM = pl.BlockSpec(memory_space=pltpu.SMEM)
ANY = pl.BlockSpec(memory_space=pl.ANY)
F32 = jnp.float32
BF16 = jnp.bfloat16


def struct(shape, dtype):
    return jax.ShapeDtypeStruct(shape, dtype)


def call(kernel, out, in_specs, args, cost=3, scratch=(), vmem=8, name=None):
    outs = out if isinstance(out, (tuple, list)) else (out,)
    nbytes = sum(math.prod(a.shape) * a.dtype.itemsize for a in args)
    nbytes += sum(math.prod(o.shape) * o.dtype.itemsize for o in outs)
    return pl.pallas_call(
        kernel,
        out_shape=out,
        in_specs=in_specs,
        out_specs=jax.tree.map(lambda _: VM, out),
        scratch_shapes=scratch,
        compiler_params=pltpu.CompilerParams(vmem_limit_bytes=vmem << 20),
        cost_estimate=pl.CostEstimate(flops=cost * 10**9, bytes_accessed=nbytes, transcendentals=0),
        name=name,
    )(*args)


def in_vmem(x):
    return pltpu.with_memory_space_constraint(x, pltpu.VMEM)


def in_hbm(x):
    return pltpu.with_memory_space_constraint(x, pltpu.HBM)


def slots(index_ref, shard, blocks):
    first = jnp.int32(0)
    count = jnp.int32(0)
    for n in range(index_ref.shape[1]):
        block = index_ref[0, n]
        first += (block < shard * blocks).astype(jnp.int32)
        count += (block < (shard + 1) * blocks).astype(jnp.int32)
    return first, count - first


def slot_block(index_ref, first, count, slot, shard, blocks):
    entry = jnp.minimum(first + slot, index_ref.shape[1] - 1)
    local = jnp.clip(index_ref[0, entry] - shard * blocks, 0, blocks - 1)
    return local, slot < count


def pick_kernel(index_ref, meta_ref, key_ref, value_ref, key_out, value_out, sems):
    blocks = key_ref.shape[0] // KB
    shard = meta_ref[0]
    first, count = slots(index_ref, shard, blocks)
    copies = []
    for slot in range(MOST):
        local, _ = slot_block(index_ref, first, count, slot, shard, blocks)
        rows = pl.ds(pl.multiple_of(local * KB, KB), KB)
        for n, (src, dst) in enumerate(((key_ref, key_out), (value_ref, value_out))):
            copy = pltpu.make_async_copy(
                src.at[rows, :], dst.at[slot * KB : (slot + 1) * KB, :], sems.at[n, slot]
            )
            copy.start()
            copies.append(copy)
    for copy in copies:
        copy.wait()


def attend_kernel(offset, blocks, context_len, total, index_ref, meta_ref, q_ref, key_ref, value_ref, out_ref):
    rows = q_ref.shape[0]
    heads = q_ref.shape[1] // DH
    kv_dev = key_ref.shape[1] // DH
    group = heads // kv_dev
    shard = meta_ref[0]
    token0 = context_len - total + (shard ^ offset) * rows
    first, count = slots(index_ref, shard, blocks)
    limits = []
    for slot in range(MOST):
        local, valid = slot_block(index_ref, first, count, slot, shard, blocks)
        limit = token0 - (shard * blocks + local) * KB
        limits.append(jnp.where(valid, limit, jnp.int32(-(1 << 20))))
    row = lax.broadcasted_iota(jnp.int32, (group * rows, KB), 0) % rows
    lane = lax.broadcasted_iota(jnp.int32, (group * rows, KB), 1)
    ahead = lane - row
    head_lane = lax.broadcasted_iota(jnp.int32, (rows, LANES), 1)
    lse_tile = jnp.zeros((rows, LANES), F32)
    for kv in range(kv_dev):
        stacked = jnp.concatenate(
            [q_ref[:, (kv * group + h) * DH : (kv * group + h + 1) * DH] for h in range(group)], axis=0
        )
        scores = lax.dot_general(
            stacked,
            key_ref[:, kv * DH : (kv + 1) * DH],
            (((1,), (1,)), ((), ())),
            preferred_element_type=F32,
        ) * (1.0 / math.sqrt(DH))
        parts = [
            jnp.where(ahead <= limits[slot], scores[:, slot * KB : (slot + 1) * KB], -1e30)
            for slot in range(MOST)
        ]
        peak = functools.reduce(jnp.maximum, parts)
        peak = jnp.max(peak, axis=1, keepdims=True)
        parts = [jnp.exp(p - peak) for p in parts]
        row_total = jnp.sum(functools.reduce(jnp.add, parts), axis=1, keepdims=True)
        weights = jnp.concatenate([p.astype(BF16) for p in parts], axis=1)
        mixture = jnp.dot(
            weights, value_ref[:, kv * DH : (kv + 1) * DH], preferred_element_type=F32
        )
        mixture = (mixture / row_total).astype(BF16)
        lse = peak + jnp.log(row_total)
        for h in range(group):
            head = kv * group + h
            span = slice(h * rows, (h + 1) * rows)
            out_ref[:, head * DH : (head + 1) * DH] = mixture[span]
            lse_tile = jnp.where(head_lane == head, lse[span], lse_tile)
    high = lse_tile.astype(BF16).astype(F32)
    rest = lse_tile - high
    mid = rest.astype(BF16).astype(F32)
    low = rest - mid
    tile = high + pltpu.roll(mid, heads, 1) + pltpu.roll(low, 2 * heads, 1)
    out_ref[:, heads * DH :] = tile.astype(BF16)


def blend_kernel(*refs):
    out_ref = refs[-1]
    parts = refs[:-1]
    heads = out_ref.shape[1] // DH
    logs = []
    for part in parts:
        tile = part[:, heads * DH :].astype(F32)
        logs.append(
            tile + pltpu.roll(tile, LANES - heads, 1) + pltpu.roll(tile, LANES - 2 * heads, 1)
        )
    peak = functools.reduce(jnp.maximum, logs)
    shares = [jnp.exp(log - peak) for log in logs]
    total = functools.reduce(jnp.add, shares)
    shares = [share / total for share in shares]
    for head in range(heads):
        span = slice(head * DH, (head + 1) * DH)
        out_ref[:, span] = functools.reduce(
            jnp.add,
            [share[:, head : head + 1] * part[:, span].astype(F32) for share, part in zip(shares, parts)],
        ).astype(BF16)


def place_of(meta_ref, n_sec, n, rows, count):
    owner = meta_ref[0] ^ n
    other = ((owner % n_sec) != meta_ref[2]).astype(jnp.int32)
    return pl.multiple_of(other * (count // n_sec * rows) + owner // n_sec * rows, rows)


def product(rows_ref, weight_ref, source, keep_ref, send_ref, target, width, tile):
    half = rows_ref.shape[0] // 2
    for at in range(0, width, tile):
        part = jnp.dot(
            rows_ref[...],
            weight_ref[:, source + at : source + at + tile],
            preferred_element_type=F32,
        )
        keep_ref[:, target + at : target + at + tile] = part[:half]
        send_ref[:, target + at : target + at + tile] = part[half:].astype(BF16)


def project_kernel(n_sec, tile, meta_ref, *refs):
    pieces, (weight_ref, keep_ref, send_ref, rows_ref) = refs[:-4], refs[-4:]
    rows = pieces[0].shape[0]
    for n, piece in enumerate(pieces):
        rows_ref[pl.ds(place_of(meta_ref, n_sec, n, rows, len(pieces)), rows), :] = piece[...]
    product(rows_ref, weight_ref, 0, keep_ref, send_ref, 0, weight_ref.shape[1], tile)


def fold_kernel(meta_ref, keep_ref, got_ref, keep_out, send_out):
    rows = keep_out.shape[0]
    mine = pl.ds(pl.multiple_of(meta_ref[1] * rows, rows), rows)
    other = pl.ds(pl.multiple_of((1 - meta_ref[1]) * rows, rows), rows)
    keep_out[...] = keep_ref[mine, :] + got_ref[mine, :].astype(F32)
    send_out[...] = (keep_ref[other, :] + got_ref[other, :].astype(F32)).astype(BF16)


def middle_kernel(stream_ref, keep_ref, got_ref, out_ref):
    out_ref[...] = (
        stream_ref[...].astype(F32) + (keep_ref[...] + got_ref[...].astype(F32))
    ).astype(BF16)


def put_exact(ref, at, value):
    high = value.astype(BF16)
    ref[at, 0:LANES] = high
    ref[at, LANES : 2 * LANES] = (value - high.astype(F32)).astype(BF16)


def take_exact(tile):
    return tile[:, :LANES].astype(F32) + tile[:, LANES:].astype(F32)


def gate_kernel(n_sec, start, width, tile, with_norm, meta_ref, *refs):
    pieces = refs[:4]
    gain_ref, gate_ref, up_ref = refs[4:7]
    outs, rows_ref = refs[7:-1], refs[-1]
    rows = pieces[0].shape[0]
    half = rows_ref.shape[0] // 2
    model = rows_ref.shape[1]
    gain = gain_ref[:, pl.ds(pl.multiple_of(meta_ref[3] * model, model), model)]
    for n, piece in enumerate(pieces):
        wide = piece[...].astype(F32)
        at = place_of(meta_ref, n_sec, n, rows, len(pieces))
        rows_ref[pl.ds(at, rows), :] = (wide * gain).astype(BF16)
        if with_norm:
            square = jnp.broadcast_to(jnp.sum(wide * wide, axis=1, keepdims=True), (rows, LANES))

            @pl.when(at < half)
            def _():
                outs[2][pl.ds(at, rows), :] = square

            @pl.when(at >= half)
            def _():
                put_exact(outs[3], pl.ds(pl.multiple_of(at - half, rows), rows), square)

    product(rows_ref, gate_ref, start, outs[0], outs[1], 0, width, tile)
    product(rows_ref, up_ref, start, outs[0], outs[1], width, width, tile)


def fold_norm_kernel(meta_ref, keep_ref, got_ref, keep_out, send_out):
    rows = keep_out.shape[0]
    mine = pl.ds(pl.multiple_of(meta_ref[1] * rows, rows), rows)
    other = pl.ds(pl.multiple_of((1 - meta_ref[1]) * rows, rows), rows)
    keep_out[...] = keep_ref[mine, :] + take_exact(got_ref[mine, :])
    put_exact(send_out, slice(None), keep_ref[other, :] + take_exact(got_ref[other, :]))


def hidden_kernel(model, keep_ref, got_ref, square_ref, square_got_ref, out_ref):
    width = out_ref.shape[1]
    square = square_ref[...] + take_exact(square_got_ref[...])
    scale = lax.rsqrt(square / model + EPS)
    for at in range(0, width, LANES):
        gate = keep_ref[:, at : at + LANES] + got_ref[:, at : at + LANES].astype(F32)
        up = keep_ref[:, width + at : width + at + LANES] + got_ref[
            :, width + at : width + at + LANES
        ].astype(F32)
        gate = gate * scale
        out_ref[:, at : at + LANES] = (
            gate / (1.0 + jnp.exp(-gate)) * (up * scale)
        ).astype(BF16)


def down_kernel(n_chunk, tile, meta_ref, *refs):
    pieces = refs[: 4 * n_chunk]
    weight_ref, own_ref = refs[4 * n_chunk : 4 * n_chunk + 2]
    sends, rows_ref = refs[4 * n_chunk + 2 : -1], refs[-1]
    rows = pieces[0].shape[0]
    width = pieces[0].shape[1]
    shard, place = meta_ref[0], meta_ref[3]
    for n in range(4):
        at = pl.ds(pl.multiple_of((shard ^ place ^ n) * rows, rows), rows)
        for c in range(n_chunk):
            rows_ref[at, c * width : (c + 1) * width] = pieces[n * n_chunk + c][...]

    for at in range(0, weight_ref.shape[1], tile):
        columns = slice(at, at + tile)
        part = jnp.dot(rows_ref[...], weight_ref[:, columns], preferred_element_type=F32)
        own_ref[:, columns] = part[:rows]
        for n, send in enumerate(sends):
            send[:, columns] = part[(n + 1) * rows : (n + 2) * rows].astype(BF16)


def final_kernel(middle_ref, own_ref, *refs):
    parts, out_ref = refs[:-1], refs[-1]
    total = own_ref[...]
    for part in parts:
        total = total + part[...].astype(F32)
    out_ref[...] = (middle_ref[...].astype(F32) + total).astype(BF16)


def swap(x, axis):
    return lax.ppermute(x, axis, [(0, 1), (1, 0)])


def turn(x, axis, n, offset):
    return lax.ppermute(x, axis, [(i, i ^ offset) for i in range(n)])


def direct_body(
    queries,
    key_cache,
    value_cache,
    block_index,
    stream,
    out_weight,
    norm_gain,
    gate_weight,
    up_weight,
    down_weight,
):
    n_context, n_head, n_sec = (lax.axis_size(a) for a in ALL)
    shard, head, sec = (lax.axis_index(a) for a in ALL)
    place = head * n_sec + sec
    meta = jnp.stack([shard, head, sec, place]).astype(jnp.int32)
    rows, heads_width = queries.shape
    context_len = key_cache.shape[0] * n_context
    model = norm_gain.shape[0]
    total = rows * n_context
    blocks = key_cache.shape[0] // KB
    kv_width = key_cache.shape[1]
    order = (3, 1, 2)

    got_q = {m: turn(queries, "ctx", n_context, m) for m in order}
    got_q[0] = queries
    picked = struct((MOST * KB, kv_width), BF16)
    keys, values = call(
        pick_kernel,
        (picked, picked),
        [SM, SM, ANY, ANY],
        (block_index, meta, in_hbm(key_cache), in_hbm(value_cache)),
        scratch=[pltpu.SemaphoreType.DMA((2, MOST))],
        name="pick",
    )
    partial = {}
    for m in (0,) + order:
        partial[m] = call(
            functools.partial(attend_kernel, m, blocks, context_len, total),
            struct((rows, heads_width + LANES), BF16),
            [SM, SM, VM, VM, VM],
            (block_index, meta, got_q[m], keys, values),
            name=f"attend{m}",
        )
    back = {m: turn(partial[m], "ctx", n_context, m) for m in order}
    back[0] = partial[0]
    blended = call(
        blend_kernel,
        struct((rows, heads_width), BF16),
        [VM] * 4,
        tuple(back[m] for m in range(4)),
        name="blend",
    )

    attention = {m: turn(blended, "ctx", n_context, m) for m in order}
    attention[0] = blended
    width = out_weight.shape[1]
    keep, send = call(
        functools.partial(project_kernel, n_sec, 512),
        (struct((n_head * rows, width), F32), struct((n_head * rows, width), BF16)),
        [SM] + [VM] * 5,
        (meta,) + tuple(attention[m] for m in range(4)) + (in_vmem(out_weight),),
        scratch=[pltpu.VMEM((total, heads_width), BF16)],
        name="project",
    )
    got = swap(send, "sec")
    keep, send = call(
        fold_kernel,
        (struct((rows, width), F32), struct((rows, width), BF16)),
        [SM, VM, VM],
        (meta, keep, got),
        cost=6,
        name="fold",
    )
    got = swap(send, "head")
    middle = call(
        middle_kernel, struct((rows, width), BF16), [VM] * 3, (stream, keep, got), cost=6, name="middle"
    )

    middle = lax.ppermute(
        middle,
        ALL,
        [(a * n_context + b, b * n_context + a) for a in range(n_context) for b in range(n_context)],
    )
    all_middle = {m: turn(middle, "ctx", n_context, m) for m in order}
    all_middle[0] = middle
    hidden_width = gate_weight.shape[1]
    n_chunk = 2
    chunk = hidden_width // n_chunk
    hidden = []
    gate_vmem, up_vmem = in_vmem(gate_weight), in_vmem(up_weight)
    square = None
    for c in range(n_chunk):
        out = [struct((n_head * rows, 2 * chunk), F32), struct((n_head * rows, 2 * chunk), BF16)]
        if c == 0:
            out += [struct((n_head * rows, LANES), F32), struct((n_head * rows, 2 * LANES), BF16)]
        res = call(
            functools.partial(gate_kernel, n_sec, c * chunk, chunk, 256, c == 0),
            tuple(out),
            [SM] + [VM] * 7,
            (meta,) + tuple(all_middle[m] for m in range(4)) + (norm_gain[None], gate_vmem, up_vmem),
            scratch=[pltpu.VMEM((total, width), BF16)],
            name=f"gate{c}",
        )
        keep, send = res[:2]
        if c == 0:
            square_keep, square_send = call(
                fold_norm_kernel,
                (struct((rows, LANES), F32), struct((rows, 2 * LANES), BF16)),
                [SM, VM, VM],
                (meta, res[2], swap(res[3], "sec")),
                name="fold_norm",
            )
            square = (square_keep, swap(square_send, "head"))
        keep, send = call(
            fold_kernel,
            (struct((rows, 2 * chunk), F32), struct((rows, 2 * chunk), BF16)),
            [SM, VM, VM],
            (meta, keep, swap(send, "sec")),
            name=f"fold{c}",
        )
        own = call(
            functools.partial(hidden_kernel, model),
            struct((rows, chunk), BF16),
            [VM] * 4,
            (keep, swap(send, "head")) + square,
            name=f"hidden{c}",
        )
        across = swap(own, "head")
        hidden.append((own, swap(own, "sec"), across, swap(across, "sec")))

    out_width = down_weight.shape[1]
    res = call(
        functools.partial(down_kernel, n_chunk, 512),
        (struct((rows, out_width), F32),) + (struct((rows, out_width), BF16),) * 3,
        [SM] + [VM] * (4 * n_chunk + 1),
        (meta,)
        + tuple(hidden[c][n] for n in range(4) for c in range(n_chunk))
        + (in_vmem(down_weight),),
        scratch=[pltpu.VMEM((total, hidden_width), BF16)],
        name="down",
    )
    parts = [turn(res[m], "ctx", n_context, m) for m in order]
    return call(
        final_kernel, struct((rows, out_width), BF16), [VM] * 5, (middle, res[0]) + tuple(parts), name="final"
    )


def local_attention(gathered, key_cache, value_cache, block_index, context_index, context_len):
    group_size = HQ // KVH
    kv_dev = key_cache.shape[1] // DH
    blocks_dev = key_cache.shape[0] // KB
    total_tokens = gathered.shape[0]
    key_blocks = key_cache.reshape(blocks_dev, KB, kv_dev, DH)
    value_blocks = value_cache.reshape(blocks_dev, KB, kv_dev, DH)
    local_ids = context_index * blocks_dev + jnp.arange(blocks_dev, dtype=jnp.int32)
    member = jnp.any(block_index[:, :, None] == local_ids[None, None, :], axis=1)
    member_rank = jnp.cumsum(member.astype(jnp.int32), axis=1) - 1
    slot_hit = member[:, None, :] & (
        member_rank[:, None, :] == jnp.arange(MOST, dtype=jnp.int32)[None, :, None]
    )
    slot_block = jnp.sum(
        jnp.where(slot_hit, jnp.arange(blocks_dev, dtype=jnp.int32)[None, None, :], 0), axis=2
    )
    slot_valid = jnp.any(slot_hit, axis=2)
    picked_keys = jnp.take(key_blocks, slot_block[0], axis=0).reshape(MOST * KB, kv_dev, DH)
    picked_values = jnp.take(value_blocks, slot_block[0], axis=0).reshape(MOST * KB, kv_dev, DH)
    key_pos = (
        (local_ids[0] + slot_block[0])[:, None] * KB + jnp.arange(KB, dtype=jnp.int32)[None, :]
    ).reshape(-1)
    live_keys = jnp.broadcast_to(slot_valid[0][:, None], (MOST, KB)).reshape(-1)
    query_pos = context_len - total_tokens + jnp.arange(KB, dtype=jnp.int32)
    allowed = live_keys[None, :] & (key_pos[None, :] <= query_pos[:, None])
    query_block = gathered.reshape(KB, kv_dev, group_size, DH)
    scores = jnp.einsum(
        "qhgd,phd->hgqp", query_block, picked_keys, preferred_element_type=jnp.float32
    ) / math.sqrt(DH)
    scores = jnp.where(allowed[None, None], scores, -jnp.inf)
    peak_score = jnp.max(scores, axis=-1, keepdims=True)
    unnormed = jnp.exp(scores - peak_score)
    row_total = jnp.sum(unnormed, axis=-1)
    mixture = jnp.einsum(
        "hgqp,phd->qhgd",
        unnormed.astype(jnp.bfloat16),
        picked_values,
        preferred_element_type=jnp.float32,
    )
    result = mixture / jnp.transpose(row_total, (2, 0, 1))[..., None]
    log_total = jnp.transpose(peak_score[..., 0] + jnp.log(row_total), (2, 0, 1))
    out_list = result.reshape(KB, -1)
    lse_list = log_total.reshape(KB, -1)
    return (out_list, lse_list)


def general_body(
    queries,
    key_cache,
    value_cache,
    block_index,
    stream,
    out_weight,
    norm_gain,
    gate_weight,
    up_weight,
    down_weight,
):
    n_context = lax.axis_size("ctx")
    context_index = lax.axis_index("ctx")
    context_len = key_cache.shape[0] * n_context
    gathered = lax.all_gather(queries, "ctx", axis=0, tiled=True)
    part_out, part_lse = local_attention(
        gathered, key_cache, value_cache, block_index, context_index, context_len
    )
    spread_out, spread_lse = (
        lax.all_to_all(part_out[:, None, :], "ctx", split_axis=0, concat_axis=1, tiled=True),
        lax.all_to_all(part_lse[:, None, :], "ctx", split_axis=0, concat_axis=1, tiled=True),
    )
    share_rows = spread_out.shape[0]
    head_count = spread_lse.shape[2]
    peak_value = jnp.max(spread_lse, axis=1, keepdims=True)
    share_weight = jnp.exp(spread_lse - peak_value)
    blended = jnp.sum(
        spread_out.reshape(share_rows, n_context, head_count, -1) * share_weight[..., None], axis=1
    )
    blended = blended / jnp.sum(share_weight, axis=1)[..., None]
    attention = lax.all_gather(
        blended.reshape(share_rows, -1).astype(jnp.bfloat16), "ctx", axis=0, tiled=True
    )
    row_piece = attention
    projected = lax.psum_scatter(
        jnp.dot(row_piece, out_weight, preferred_element_type=jnp.float32),
        ("head", "sec"),
        scatter_dimension=0,
        tiled=True,
    )
    middle = (stream.astype(jnp.float32) + projected).astype(jnp.bfloat16)
    full_middle = lax.all_gather(middle, "ctx", axis=1, tiled=True)
    middle_wide = full_middle.astype(jnp.float32)
    mean_square = jnp.mean(middle_wide * middle_wide, axis=-1, keepdims=True)
    normed = (middle_wide * lax.rsqrt(mean_square + 1e-05) * norm_gain).astype(jnp.bfloat16)
    normed_cols, middle_cols = (
        lax.all_to_all(normed, ("head", "sec"), split_axis=1, concat_axis=0, tiled=True),
        lax.all_to_all(full_middle, ("head", "sec"), split_axis=1, concat_axis=0, tiled=True),
    )
    row_piece = normed_cols
    gate_up = lax.psum_scatter(
        jnp.concatenate(
            [
                jnp.dot(row_piece, gate_weight, preferred_element_type=jnp.float32),
                jnp.dot(row_piece, up_weight, preferred_element_type=jnp.float32),
            ],
            axis=1,
        ),
        ("head", "sec"),
        scatter_dimension=0,
        tiled=True,
    )
    hidden_width = gate_weight.shape[1]
    hidden = (jax.nn.silu(gate_up[:, :hidden_width]) * gate_up[:, hidden_width:]).astype(
        jnp.bfloat16
    )
    all_hidden = lax.all_gather(hidden, ("head", "sec"), axis=0, tiled=True)
    row_piece = all_hidden
    down_part = lax.psum_scatter(
        jnp.dot(row_piece, down_weight, preferred_element_type=jnp.float32),
        "ctx",
        scatter_dimension=0,
        tiled=True,
    )
    own_middle = lax.dynamic_slice_in_dim(
        middle_cols, context_index * down_part.shape[0], down_part.shape[0], 0
    )
    return (own_middle.astype(jnp.float32) + down_part).astype(jnp.bfloat16)


def solution(mesh):
    size = dict(mesh.shape)
    direct = size["ctx"] == 4 and size["head"] == 2 and size["sec"] == 2
    return jax.shard_map(
        direct_body if direct else general_body,
        mesh=mesh,
        in_specs=(
            P(("groups", "ctx"), ("head", "sec")),
            P(("groups", "ctx"), ("head", "sec")),
            P(("groups", "ctx"), ("head", "sec")),
            P("groups", None),
            P(("groups", "head", "sec"), "ctx"),
            P(("head", "sec"), "ctx"),
            P(),
            P(("head", "sec"), "ctx"),
            P(("head", "sec"), "ctx"),
            P("ctx", ("head", "sec")),
        ),
        out_specs=P(("groups", "ctx"), ("head", "sec")),
        check_vma=False,
    )
```

```python
import functools
import math

import jax
import jax.numpy as jnp
from jax import lax
from jax.experimental import pallas as pl
from jax.experimental.pallas import tpu as pltpu
from jax.sharding import PartitionSpec as P


HQ = 64
KVH = 8
DH = 128
KB = 128
MOST = 4
LANES = 128
EPS = 1e-05
ALL = ("ctx", "head", "sec")


VM = pl.BlockSpec(memory_space=pltpu.VMEM)
SM = pl.BlockSpec(memory_space=pltpu.SMEM)
ANY = pl.BlockSpec(memory_space=pl.ANY)
F32 = jnp.float32
BF16 = jnp.bfloat16


def struct(shape, dtype):
    return jax.ShapeDtypeStruct(shape, dtype)


def call(kernel, out, in_specs, args, cost=3, scratch=(), vmem=8):
    outs = out if isinstance(out, (tuple, list)) else (out,)
    nbytes = sum(math.prod(a.shape) * a.dtype.itemsize for a in args)
    nbytes += sum(math.prod(o.shape) * o.dtype.itemsize for o in outs)
    return pl.pallas_call(
        kernel,
        out_shape=out,
        in_specs=in_specs,
        out_specs=jax.tree.map(lambda _: VM, out),
        scratch_shapes=scratch,
        compiler_params=pltpu.CompilerParams(vmem_limit_bytes=vmem << 20),
        cost_estimate=pl.CostEstimate(flops=cost * 10**9, bytes_accessed=nbytes, transcendentals=0),
    )(*args)


def in_vmem(x):
    return pltpu.with_memory_space_constraint(x, pltpu.VMEM)


def in_hbm(x):
    return pltpu.with_memory_space_constraint(x, pltpu.HBM)


def slots(index_ref, shard, blocks):
    first = jnp.int32(0)
    count = jnp.int32(0)
    for n in range(index_ref.shape[1]):
        block = index_ref[0, n]
        first += (block < shard * blocks).astype(jnp.int32)
        count += (block < (shard + 1) * blocks).astype(jnp.int32)
    return first, count - first


def slot_block(index_ref, first, count, slot, shard, blocks):
    entry = jnp.minimum(first + slot, index_ref.shape[1] - 1)
    local = jnp.clip(index_ref[0, entry] - shard * blocks, 0, blocks - 1)
    return local, slot < count


def pick_kernel(index_ref, meta_ref, key_ref, value_ref, key_out, value_out, sems):
    blocks = key_ref.shape[0] // KB
    shard = meta_ref[0]
    first, count = slots(index_ref, shard, blocks)
    copies = []
    for slot in range(MOST):
        local, _ = slot_block(index_ref, first, count, slot, shard, blocks)
        rows = pl.ds(pl.multiple_of(local * KB, KB), KB)
        for n, (src, dst) in enumerate(((key_ref, key_out), (value_ref, value_out))):
            copy = pltpu.make_async_copy(
                src.at[rows, :], dst.at[slot * KB : (slot + 1) * KB, :], sems.at[n, slot]
            )
            copy.start()
            copies.append(copy)
    for copy in copies:
        copy.wait()


def attend_kernel(offset, blocks, context_len, total, index_ref, meta_ref, q_ref, key_ref, value_ref, out_ref):
    rows = q_ref.shape[0]
    heads = q_ref.shape[1] // DH
    kv_dev = key_ref.shape[1] // DH
    group = heads // kv_dev
    shard = meta_ref[0]
    token0 = context_len - total + (shard ^ offset) * rows
    first, count = slots(index_ref, shard, blocks)
    limits = []
    for slot in range(MOST):
        local, valid = slot_block(index_ref, first, count, slot, shard, blocks)
        limit = token0 - (shard * blocks + local) * KB
        limits.append(jnp.where(valid, limit, jnp.int32(-(1 << 20))))
    row = lax.broadcasted_iota(jnp.int32, (group * rows, KB), 0) % rows
    lane = lax.broadcasted_iota(jnp.int32, (group * rows, KB), 1)
    ahead = lane - row
    head_lane = lax.broadcasted_iota(jnp.int32, (rows, LANES), 1)
    lse_tile = jnp.zeros((rows, LANES), F32)
    for kv in range(kv_dev):
        stacked = jnp.concatenate(
            [q_ref[:, (kv * group + h) * DH : (kv * group + h + 1) * DH] for h in range(group)], axis=0
        )
        scores = lax.dot_general(
            stacked,
            key_ref[:, kv * DH : (kv + 1) * DH],
            (((1,), (1,)), ((), ())),
            preferred_element_type=F32,
        ) * (1.0 / math.sqrt(DH))
        parts = [
            jnp.where(ahead <= limits[slot], scores[:, slot * KB : (slot + 1) * KB], -1e30)
            for slot in range(MOST)
        ]
        peak = functools.reduce(jnp.maximum, parts)
        peak = jnp.max(peak, axis=1, keepdims=True)
        parts = [jnp.exp(p - peak) for p in parts]
        row_total = jnp.sum(functools.reduce(jnp.add, parts), axis=1, keepdims=True)
        weights = jnp.concatenate([p.astype(BF16) for p in parts], axis=1)
        mixture = jnp.dot(
            weights, value_ref[:, kv * DH : (kv + 1) * DH], preferred_element_type=F32
        )
        mixture = (mixture * (1.0 / row_total)).astype(BF16)
        lse = peak + jnp.log(row_total)
        for h in range(group):
            head = kv * group + h
            span = slice(h * rows, (h + 1) * rows)
            out_ref[:, head * DH : (head + 1) * DH] = mixture[span]
            lse_tile = jnp.where(head_lane == head, lse[span], lse_tile)
    high = lse_tile.astype(BF16).astype(F32)
    rest = lse_tile - high
    mid = rest.astype(BF16).astype(F32)
    low = rest - mid
    tile = high + pltpu.roll(mid, heads, 1) + pltpu.roll(low, 2 * heads, 1)
    out_ref[:, heads * DH :] = tile.astype(BF16)


def blend_kernel(*refs):
    out_ref = refs[-1]
    parts = refs[:-1]
    heads = out_ref.shape[1] // DH
    logs = []
    for part in parts:
        tile = part[:, heads * DH :].astype(F32)
        logs.append(
            tile + pltpu.roll(tile, LANES - heads, 1) + pltpu.roll(tile, LANES - 2 * heads, 1)
        )
    peak = functools.reduce(jnp.maximum, logs)
    shares = [jnp.exp(log - peak) for log in logs]
    total = functools.reduce(jnp.add, shares)
    shares = [share / total for share in shares]
    for head in range(heads):
        span = slice(head * DH, (head + 1) * DH)
        out_ref[:, span] = functools.reduce(
            jnp.add,
            [share[:, head : head + 1] * part[:, span].astype(F32) for share, part in zip(shares, parts)],
        ).astype(BF16)


def place_of(meta_ref, n_sec, n, rows, count):
    owner = meta_ref[0] ^ n
    other = ((owner % n_sec) != meta_ref[2]).astype(jnp.int32)
    return pl.multiple_of(other * (count // n_sec * rows) + owner // n_sec * rows, rows)


def product(rows_ref, weight_ref, source, keep_ref, send_ref, target, width, tile):
    half = rows_ref.shape[0] // 2
    for at in range(0, width, tile):
        size = min(tile, width - at)
        part = jnp.dot(
            rows_ref[...],
            weight_ref[:, source + at : source + at + size],
            preferred_element_type=F32,
        )
        keep_ref[:, target + at : target + at + size] = part[:half]
        send_ref[:, target + at : target + at + size] = part[half:].astype(BF16)


def project_kernel(n_sec, tile, meta_ref, *refs):
    pieces, (weight_ref, keep_ref, send_ref, rows_ref) = refs[:-4], refs[-4:]
    rows = pieces[0].shape[0]
    for n, piece in enumerate(pieces):
        rows_ref[pl.ds(place_of(meta_ref, n_sec, n, rows, len(pieces)), rows), :] = piece[...]
    product(rows_ref, weight_ref, 0, keep_ref, send_ref, 0, weight_ref.shape[1], tile)


def fold_kernel(width, meta_ref, keep_ref, got_ref, keep_out, send_out):
    rows = keep_out.shape[0]
    mine = pl.ds(pl.multiple_of(meta_ref[1] * rows, rows), rows)
    other = pl.ds(pl.multiple_of((1 - meta_ref[1]) * rows, rows), rows)
    keep_out[:, :width] = keep_ref[mine, :width] + got_ref[mine, :width].astype(F32)
    send_out[:, :width] = (keep_ref[other, :width] + got_ref[other, :width].astype(F32)).astype(BF16)
    if keep_ref.shape[1] > width:
        keep_out[:, width:] = keep_ref[mine, width:] + take_exact(got_ref[mine, width:])
        put_exact(send_out, slice(None), width, keep_ref[other, width:] + take_exact(got_ref[other, width:]))


def middle_kernel(stream_ref, keep_ref, got_ref, out_ref):
    out_ref[...] = (
        stream_ref[...].astype(F32) + (keep_ref[...] + got_ref[...].astype(F32))
    ).astype(BF16)


def put_exact(ref, rows, at, value):
    high = value.astype(BF16)
    ref[rows, at : at + LANES] = high
    ref[rows, at + LANES : at + 2 * LANES] = (value - high.astype(F32)).astype(BF16)


def take_exact(tile):
    return tile[:, :LANES].astype(F32) + tile[:, LANES:].astype(F32)


def gate_kernel(n_sec, start, width, tile, with_norm, meta_ref, *refs):
    pieces = refs[:4]
    gain_ref, gate_ref, up_ref, keep_ref, send_ref, rows_ref = refs[4:]
    rows = pieces[0].shape[0]
    half = rows_ref.shape[0] // 2
    model = rows_ref.shape[1]
    gain = gain_ref[:, pl.ds(pl.multiple_of(meta_ref[3] * model, model), model)]
    for n, piece in enumerate(pieces):
        wide = piece[...].astype(F32)
        at = place_of(meta_ref, n_sec, n, rows, len(pieces))
        rows_ref[pl.ds(at, rows), :] = (wide * gain).astype(BF16)
        if with_norm:
            square = jnp.broadcast_to(jnp.sum(wide * wide, axis=1, keepdims=True), (rows, LANES))

            @pl.when(at < half)
            def _():
                keep_ref[pl.ds(at, rows), 2 * width :] = square

            @pl.when(at >= half)
            def _():
                put_exact(send_ref, pl.ds(pl.multiple_of(at - half, rows), rows), 2 * width, square)

    product(rows_ref, gate_ref, start, keep_ref, send_ref, 0, width, tile)
    product(rows_ref, up_ref, start, keep_ref, send_ref, width, width, tile)


def scale_kernel(model, keep_ref, got_ref, out_ref):
    at = keep_ref.shape[1] - LANES
    square = keep_ref[:, at:] + take_exact(got_ref[:, at:])
    out_ref[...] = lax.rsqrt(square / model + EPS)


def hidden_kernel(scale_ref, keep_ref, got_ref, out_ref):
    width = out_ref.shape[1]
    scale = scale_ref[...]
    for at in range(0, width, LANES):
        gate = keep_ref[:, at : at + LANES] + got_ref[:, at : at + LANES].astype(F32)
        up = keep_ref[:, width + at : width + at + LANES] + got_ref[
            :, width + at : width + at + LANES
        ].astype(F32)
        gate = gate * scale
        out_ref[:, at : at + LANES] = (
            gate / (1.0 + jnp.exp(-gate)) * (up * scale)
        ).astype(BF16)


def first_hidden_kernel(model, keep_ref, got_ref, out_ref, scale_ref):
    scale_kernel(model, keep_ref, got_ref, scale_ref)
    hidden_kernel(scale_ref, keep_ref, got_ref, out_ref)


def down_kernel(n_chunk, tile, meta_ref, *refs):
    pieces = refs[: 4 * n_chunk]
    weight_ref, own_ref = refs[4 * n_chunk : 4 * n_chunk + 2]
    sends, rows_ref = refs[4 * n_chunk + 2 : -1], refs[-1]
    rows = pieces[0].shape[0]
    shard, place = meta_ref[0], meta_ref[3]
    for n in range(4):
        at = pl.ds(pl.multiple_of((shard ^ place ^ n) * rows, rows), rows)
        start = 0
        for c in range(n_chunk):
            piece = pieces[n * n_chunk + c]
            rows_ref[at, start : start + piece.shape[1]] = piece[...]
            start += piece.shape[1]

    for at in range(0, weight_ref.shape[1], tile):
        columns = slice(at, at + tile)
        part = jnp.dot(rows_ref[...], weight_ref[:, columns], preferred_element_type=F32)
        own_ref[:, columns] = part[:rows]
        for n, send in enumerate(sends):
            send[:, columns] = part[(n + 1) * rows : (n + 2) * rows].astype(BF16)


def final_kernel(middle_ref, own_ref, *refs):
    parts, out_ref = refs[:-1], refs[-1]
    total = own_ref[...]
    for part in parts:
        total = total + part[...].astype(F32)
    out_ref[...] = (middle_ref[...].astype(F32) + total).astype(BF16)


def swap(x, axis):
    return lax.ppermute(x, axis, [(0, 1), (1, 0)])


def turn(x, axis, n, offset):
    return lax.ppermute(x, axis, [(i, i ^ offset) for i in range(n)])


def direct_body(
    queries,
    key_cache,
    value_cache,
    block_index,
    stream,
    out_weight,
    norm_gain,
    gate_weight,
    up_weight,
    down_weight,
):
    n_context, n_head, n_sec = (lax.axis_size(a) for a in ALL)
    shard, head, sec = (lax.axis_index(a) for a in ALL)
    place = head * n_sec + sec
    meta = jnp.stack([shard, head, sec, place]).astype(jnp.int32)
    rows, heads_width = queries.shape
    context_len = key_cache.shape[0] * n_context
    model = norm_gain.shape[0]
    total = rows * n_context
    blocks = key_cache.shape[0] // KB
    kv_width = key_cache.shape[1]
    order = (3, 1, 2)

    got_q = {m: turn(queries, "ctx", n_context, m) for m in order}
    got_q[0] = queries
    picked = struct((MOST * KB, kv_width), BF16)
    keys, values = call(
        pick_kernel,
        (picked, picked),
        [SM, SM, ANY, ANY],
        (block_index, meta, in_hbm(key_cache), in_hbm(value_cache)),
        scratch=[pltpu.SemaphoreType.DMA((2, MOST))],
    )
    partial = {}
    for m in (0,) + order:
        partial[m] = call(
            functools.partial(attend_kernel, m, blocks, context_len, total),
            struct((rows, heads_width + LANES), BF16),
            [SM, SM, VM, VM, VM],
            (block_index, meta, got_q[m], keys, values),
        )
    back = {m: turn(partial[m], "ctx", n_context, m) for m in order}
    back[0] = partial[0]
    blended = call(
        blend_kernel, struct((rows, heads_width), BF16), [VM] * 4, tuple(back[m] for m in range(4))
    )

    attention = {m: turn(blended, "ctx", n_context, m) for m in order}
    attention[0] = blended
    width = out_weight.shape[1]
    keep, away = call(
        functools.partial(project_kernel, n_sec, 512),
        (struct((n_head * rows, width), F32), struct((n_head * rows, width), BF16)),
        [SM] + [VM] * 5,
        (meta,) + tuple(attention[m] for m in range(4)) + (in_vmem(out_weight),),
        scratch=[pltpu.VMEM((total, heads_width), BF16)],
    )
    got = swap(away, "sec")
    keep, away = call(
        functools.partial(fold_kernel, width),
        (struct((rows, width), F32), struct((rows, width), BF16)),
        [SM, VM, VM],
        (meta, keep, got),
        cost=6,
    )
    got = swap(away, "head")
    middle = call(middle_kernel, struct((rows, width), BF16), [VM] * 3, (stream, keep, got), cost=6)

    all_middle = {
        m: lax.ppermute(
            middle,
            ALL,
            [
                (a * n_context + b, (b ^ m) * n_context + a)
                for a in range(n_context)
                for b in range(n_context)
            ],
        )
        for m in (3, 0, 1, 2)
    }
    hidden_width = gate_weight.shape[1]
    units = hidden_width // LANES
    first = units * 2 // 5 * LANES
    chunks = ((0, first), (first, hidden_width - first))
    hidden = []
    gate_vmem, up_vmem = in_vmem(gate_weight), in_vmem(up_weight)
    scale = None
    for c, (start, chunk) in enumerate(chunks):
        extra = LANES if c == 0 else 0
        keep, away = call(
            functools.partial(gate_kernel, n_sec, start, chunk, 256, c == 0),
            (
                struct((n_head * rows, 2 * chunk + extra), F32),
                struct((n_head * rows, 2 * chunk + 2 * extra), BF16),
            ),
            [SM] + [VM] * 7,
            (meta,) + tuple(all_middle[m] for m in range(4)) + (norm_gain[None], gate_vmem, up_vmem),
            scratch=[pltpu.VMEM((total, width), BF16)],
        )
        keep, away = call(
            functools.partial(fold_kernel, 2 * chunk),
            (
                struct((rows, 2 * chunk + extra), F32),
                struct((rows, 2 * chunk + 2 * extra), BF16),
            ),
            [SM, VM, VM],
            (meta, keep, swap(away, "sec")),
        )
        got = swap(away, "head")
        if c == 0:
            own, scale = call(
                functools.partial(first_hidden_kernel, model),
                (struct((rows, chunk), BF16), struct((rows, LANES), F32)),
                [VM] * 2,
                (keep, got),
            )
        else:
            own = call(hidden_kernel, struct((rows, chunk), BF16), [VM] * 3, (scale, keep, got))
        across = swap(own, "head")
        beside = swap(own, "sec")
        hidden.append((own, beside, across, swap(across, "sec")))
    n_chunk = len(chunks)

    out_width = down_weight.shape[1]
    res = call(
        functools.partial(down_kernel, n_chunk, 512),
        (struct((rows, out_width), F32),) + (struct((rows, out_width), BF16),) * 3,
        [SM] + [VM] * (4 * n_chunk + 1),
        (meta,)
        + tuple(hidden[c][n] for n in range(4) for c in range(n_chunk))
        + (in_vmem(down_weight),),
        scratch=[pltpu.VMEM((total, hidden_width), BF16)],
    )
    parts = [turn(res[m], "ctx", n_context, m) for m in order]
    return call(
        final_kernel, struct((rows, out_width), BF16), [VM] * 5, (all_middle[0], res[0]) + tuple(parts)
    )


def local_attention(gathered, key_cache, value_cache, block_index, context_index, context_len):
    group_size = HQ // KVH
    kv_dev = key_cache.shape[1] // DH
    blocks_dev = key_cache.shape[0] // KB
    total_tokens = gathered.shape[0]
    key_blocks = key_cache.reshape(blocks_dev, KB, kv_dev, DH)
    value_blocks = value_cache.reshape(blocks_dev, KB, kv_dev, DH)
    local_ids = context_index * blocks_dev + jnp.arange(blocks_dev, dtype=jnp.int32)
    member = jnp.any(block_index[:, :, None] == local_ids[None, None, :], axis=1)
    member_rank = jnp.cumsum(member.astype(jnp.int32), axis=1) - 1
    slot_hit = member[:, None, :] & (
        member_rank[:, None, :] == jnp.arange(MOST, dtype=jnp.int32)[None, :, None]
    )
    slot_block = jnp.sum(
        jnp.where(slot_hit, jnp.arange(blocks_dev, dtype=jnp.int32)[None, None, :], 0), axis=2
    )
    slot_valid = jnp.any(slot_hit, axis=2)
    picked_keys = jnp.take(key_blocks, slot_block[0], axis=0).reshape(MOST * KB, kv_dev, DH)
    picked_values = jnp.take(value_blocks, slot_block[0], axis=0).reshape(MOST * KB, kv_dev, DH)
    key_pos = (
        (local_ids[0] + slot_block[0])[:, None] * KB + jnp.arange(KB, dtype=jnp.int32)[None, :]
    ).reshape(-1)
    live_keys = jnp.broadcast_to(slot_valid[0][:, None], (MOST, KB)).reshape(-1)
    query_pos = context_len - total_tokens + jnp.arange(KB, dtype=jnp.int32)
    allowed = live_keys[None, :] & (key_pos[None, :] <= query_pos[:, None])
    query_block = gathered.reshape(KB, kv_dev, group_size, DH)
    scores = jnp.einsum(
        "qhgd,phd->hgqp", query_block, picked_keys, preferred_element_type=jnp.float32
    ) / math.sqrt(DH)
    scores = jnp.where(allowed[None, None], scores, -jnp.inf)
    peak_score = jnp.max(scores, axis=-1, keepdims=True)
    unnormed = jnp.exp(scores - peak_score)
    row_total = jnp.sum(unnormed, axis=-1)
    mixture = jnp.einsum(
        "hgqp,phd->qhgd",
        unnormed.astype(jnp.bfloat16),
        picked_values,
        preferred_element_type=jnp.float32,
    )
    result = mixture / jnp.transpose(row_total, (2, 0, 1))[..., None]
    log_total = jnp.transpose(peak_score[..., 0] + jnp.log(row_total), (2, 0, 1))
    out_list = result.reshape(KB, -1)
    lse_list = log_total.reshape(KB, -1)
    return (out_list, lse_list)


def general_body(
    queries,
    key_cache,
    value_cache,
    block_index,
    stream,
    out_weight,
    norm_gain,
    gate_weight,
    up_weight,
    down_weight,
):
    n_context = lax.axis_size("ctx")
    context_index = lax.axis_index("ctx")
    context_len = key_cache.shape[0] * n_context
    gathered = lax.all_gather(queries, "ctx", axis=0, tiled=True)
    part_out, part_lse = local_attention(
        gathered, key_cache, value_cache, block_index, context_index, context_len
    )
    spread_out, spread_lse = (
        lax.all_to_all(part_out[:, None, :], "ctx", split_axis=0, concat_axis=1, tiled=True),
        lax.all_to_all(part_lse[:, None, :], "ctx", split_axis=0, concat_axis=1, tiled=True),
    )
    share_rows = spread_out.shape[0]
    head_count = spread_lse.shape[2]
    peak_value = jnp.max(spread_lse, axis=1, keepdims=True)
    share_weight = jnp.exp(spread_lse - peak_value)
    blended = jnp.sum(
        spread_out.reshape(share_rows, n_context, head_count, -1) * share_weight[..., None], axis=1
    )
    blended = blended / jnp.sum(share_weight, axis=1)[..., None]
    attention = lax.all_gather(
        blended.reshape(share_rows, -1).astype(jnp.bfloat16), "ctx", axis=0, tiled=True
    )
    row_piece = attention
    projected = lax.psum_scatter(
        jnp.dot(row_piece, out_weight, preferred_element_type=jnp.float32),
        ("head", "sec"),
        scatter_dimension=0,
        tiled=True,
    )
    middle = (stream.astype(jnp.float32) + projected).astype(jnp.bfloat16)
    full_middle = lax.all_gather(middle, "ctx", axis=1, tiled=True)
    middle_wide = full_middle.astype(jnp.float32)
    mean_square = jnp.mean(middle_wide * middle_wide, axis=-1, keepdims=True)
    normed = (middle_wide * lax.rsqrt(mean_square + 1e-05) * norm_gain).astype(jnp.bfloat16)
    normed_cols, middle_cols = (
        lax.all_to_all(normed, ("head", "sec"), split_axis=1, concat_axis=0, tiled=True),
        lax.all_to_all(full_middle, ("head", "sec"), split_axis=1, concat_axis=0, tiled=True),
    )
    row_piece = normed_cols
    gate_up = lax.psum_scatter(
        jnp.concatenate(
            [
                jnp.dot(row_piece, gate_weight, preferred_element_type=jnp.float32),
                jnp.dot(row_piece, up_weight, preferred_element_type=jnp.float32),
            ],
            axis=1,
        ),
        ("head", "sec"),
        scatter_dimension=0,
        tiled=True,
    )
    hidden_width = gate_weight.shape[1]
    hidden = (jax.nn.silu(gate_up[:, :hidden_width]) * gate_up[:, hidden_width:]).astype(
        jnp.bfloat16
    )
    all_hidden = lax.all_gather(hidden, ("head", "sec"), axis=0, tiled=True)
    row_piece = all_hidden
    down_part = lax.psum_scatter(
        jnp.dot(row_piece, down_weight, preferred_element_type=jnp.float32),
        "ctx",
        scatter_dimension=0,
        tiled=True,
    )
    own_middle = lax.dynamic_slice_in_dim(
        middle_cols, context_index * down_part.shape[0], down_part.shape[0], 0
    )
    return (own_middle.astype(jnp.float32) + down_part).astype(jnp.bfloat16)


def solution(mesh):
    size = dict(mesh.shape)
    direct = size["ctx"] == 4 and size["head"] == 2 and size["sec"] == 2
    return jax.shard_map(
        direct_body if direct else general_body,
        mesh=mesh,
        in_specs=(
            P(("groups", "ctx"), ("head", "sec")),
            P(("groups", "ctx"), ("head", "sec")),
            P(("groups", "ctx"), ("head", "sec")),
            P("groups", None),
            P(("groups", "head", "sec"), "ctx"),
            P(("head", "sec"), "ctx"),
            P(),
            P(("head", "sec"), "ctx"),
            P(("head", "sec"), "ctx"),
            P("ctx", ("head", "sec")),
        ),
        out_specs=P(("groups", "ctx"), ("head", "sec")),
        check_vma=False,
    )
```

```python
import functools
import math

import jax
import jax.numpy as jnp
from jax import lax
from jax.experimental import pallas as pl
from jax.experimental.pallas import tpu as pltpu
from jax.sharding import PartitionSpec as P


HQ = 64
KVH = 8
DH = 128
KB = 128
MOST = 4
LANES = 128
EPS = 1e-05
ALL = ("ctx", "head", "sec")


VM = pl.BlockSpec(memory_space=pltpu.VMEM)
SM = pl.BlockSpec(memory_space=pltpu.SMEM)
ANY = pl.BlockSpec(memory_space=pl.ANY)
F32 = jnp.float32
BF16 = jnp.bfloat16


def struct(shape, dtype):
    return jax.ShapeDtypeStruct(shape, dtype)


def call(kernel, out, in_specs, args, cost=3, scratch=(), vmem=8):
    outs = out if isinstance(out, (tuple, list)) else (out,)
    nbytes = sum(math.prod(a.shape) * a.dtype.itemsize for a in args)
    nbytes += sum(math.prod(o.shape) * o.dtype.itemsize for o in outs)
    return pl.pallas_call(
        kernel,
        out_shape=out,
        in_specs=in_specs,
        out_specs=jax.tree.map(lambda _: VM, out),
        scratch_shapes=scratch,
        compiler_params=pltpu.CompilerParams(vmem_limit_bytes=vmem << 20),
        cost_estimate=pl.CostEstimate(flops=cost * 10**9, bytes_accessed=nbytes, transcendentals=0),
    )(*args)


def in_vmem(x):
    return pltpu.with_memory_space_constraint(x, pltpu.VMEM)


def in_hbm(x):
    return pltpu.with_memory_space_constraint(x, pltpu.HBM)


N_META = 4


def slots(meta_ref, blocks):
    entries = meta_ref.shape[0] - N_META
    base = meta_ref[0] * blocks
    first = jnp.int32(0)
    end = jnp.int32(0)
    for n in range(entries):
        block = meta_ref[N_META + n]
        first += (block < base).astype(jnp.int32)
        end += (block < base + blocks).astype(jnp.int32)
    found = []
    for slot in range(MOST):
        entry = jnp.minimum(first + slot, entries - 1)
        local = jnp.clip(meta_ref[N_META + entry] - base, 0, blocks - 1)
        found.append((local, first + slot < end))
    return found


def attend(offset, blocks, context_len, total, meta_ref, q_ref, key_ref, value_ref, out_ref, score_ref, weight_ref):
    rows = q_ref.shape[0]
    heads = q_ref.shape[1] // DH
    kv_dev = key_ref.shape[1] // DH
    group = heads // kv_dev
    shard = meta_ref[0]
    scale = 1.0 / math.sqrt(DH)
    token0 = context_len - total + (shard ^ offset) * rows
    limits = [
        jnp.where(valid, token0 - (shard * blocks + local) * KB, jnp.int32(-(1 << 20)))
        for local, valid in slots(meta_ref, blocks)
    ]
    ahead = lax.broadcasted_iota(jnp.int32, (rows, KB), 1) - lax.broadcasted_iota(
        jnp.int32, (rows, KB), 0
    )
    allowed = [ahead <= limit for limit in limits]
    head_lane = lax.broadcasted_iota(jnp.int32, (rows, LANES), 1)
    lse_tile = jnp.zeros((rows, LANES), F32)
    for kv in range(kv_dev):
        stacked = jnp.concatenate(
            [q_ref[:, (kv * group + h) * DH : (kv * group + h + 1) * DH] for h in range(group)], axis=0
        )
        score_ref[kv] = lax.dot_general(
            stacked,
            key_ref[:, kv * DH : (kv + 1) * DH],
            (((1,), (1,)), ((), ())),
            preferred_element_type=F32,
        )
    for kv in range(kv_dev):
        totals = []
        for h in range(group):
            head = kv * group + h
            span = slice(h * rows, (h + 1) * rows)
            parts = [
                jnp.where(allowed[slot], score_ref[kv, span, slot * KB : (slot + 1) * KB], -1e30)
                for slot in range(MOST)
            ]
            peak = jnp.max(functools.reduce(jnp.maximum, parts), axis=1, keepdims=True)
            parts = [jnp.exp((p - peak) * scale) for p in parts]
            row_total = jnp.sum(functools.reduce(jnp.add, parts), axis=1, keepdims=True)
            for slot, p in enumerate(parts):
                weight_ref[kv, span, slot * KB : (slot + 1) * KB] = p.astype(BF16)
            totals.append(1.0 / row_total)
            lse_tile = jnp.where(head_lane == head, peak * scale + jnp.log(row_total), lse_tile)
        mixture = jnp.dot(
            weight_ref[kv], value_ref[:, kv * DH : (kv + 1) * DH], preferred_element_type=F32
        )
        for h in range(group):
            head = kv * group + h
            out_ref[:, head * DH : (head + 1) * DH] = (
                mixture[h * rows : (h + 1) * rows] * totals[h]
            ).astype(BF16)
    high = lse_tile.astype(BF16).astype(F32)
    rest = lse_tile - high
    mid = rest.astype(BF16).astype(F32)
    low = rest - mid
    tile = high + pltpu.roll(mid, heads, 1) + pltpu.roll(low, 2 * heads, 1)
    out_ref[:, heads * DH :] = tile.astype(BF16)


def first_attend_kernel(
    blocks, context_len, total, meta_ref, q_hbm, key_hbm, value_hbm,
    key_ref, value_ref, out_ref, q_ref, score_ref, weight_ref, sems, q_sem,
):
    copies = [pltpu.make_async_copy(q_hbm, q_ref, q_sem)]
    for slot, (local, _) in enumerate(slots(meta_ref, blocks)):
        rows = pl.ds(pl.multiple_of(local * KB, KB), KB)
        for n, (src, dst) in enumerate(((key_hbm, key_ref), (value_hbm, value_ref))):
            copies.append(
                pltpu.make_async_copy(
                    src.at[rows, :], dst.at[slot * KB : (slot + 1) * KB, :], sems.at[n, slot]
                )
            )
    for copy in copies:
        copy.start()
    for copy in copies:
        copy.wait()
    attend(
        0, blocks, context_len, total, meta_ref, q_ref, key_ref, value_ref, out_ref, score_ref, weight_ref
    )


def blend_kernel(*refs):
    out_ref = refs[-1]
    parts = refs[:-1]
    heads = out_ref.shape[1] // DH
    logs = []
    for part in parts:
        tile = part[:, heads * DH :].astype(F32)
        logs.append(
            tile + pltpu.roll(tile, LANES - heads, 1) + pltpu.roll(tile, LANES - 2 * heads, 1)
        )
    peak = functools.reduce(jnp.maximum, logs)
    shares = [jnp.exp(log - peak) for log in logs]
    total = functools.reduce(jnp.add, shares)
    shares = [share / total for share in shares]
    for head in range(heads):
        span = slice(head * DH, (head + 1) * DH)
        out_ref[:, span] = functools.reduce(
            jnp.add,
            [share[:, head : head + 1] * part[:, span].astype(F32) for share, part in zip(shares, parts)],
        ).astype(BF16)


def place_of(meta_ref, n_sec, n, rows, count):
    owner = meta_ref[0] ^ n
    other = ((owner % n_sec) != meta_ref[2]).astype(jnp.int32)
    return pl.multiple_of(other * (count // n_sec * rows) + owner // n_sec * rows, rows)


def product(rows_ref, weight_ref, source, keep_ref, send_ref, target, width, tile):
    half = rows_ref.shape[0] // 2
    for at in range(0, width, tile):
        size = min(tile, width - at)
        part = jnp.dot(
            rows_ref[...],
            weight_ref[:, source + at : source + at + size],
            preferred_element_type=F32,
        )
        keep_ref[:, target + at : target + at + size] = part[:half]
        send_ref[:, target + at : target + at + size] = part[half:].astype(BF16)


def project_kernel(n_sec, tile, meta_ref, *refs):
    pieces, (weight_ref, keep_ref, send_ref, rows_ref) = refs[:-4], refs[-4:]
    rows = pieces[0].shape[0]
    for n, piece in enumerate(pieces):
        rows_ref[pl.ds(place_of(meta_ref, n_sec, n, rows, len(pieces)), rows), :] = piece[...]
    product(rows_ref, weight_ref, 0, keep_ref, send_ref, 0, weight_ref.shape[1], tile)


def fold_kernel(width, meta_ref, keep_ref, got_ref, keep_out, send_out):
    rows = keep_out.shape[0]
    mine = pl.ds(pl.multiple_of(meta_ref[1] * rows, rows), rows)
    other = pl.ds(pl.multiple_of((1 - meta_ref[1]) * rows, rows), rows)
    keep_out[:, :width] = keep_ref[mine, :width] + got_ref[mine, :width].astype(F32)
    send_out[:, :width] = (keep_ref[other, :width] + got_ref[other, :width].astype(F32)).astype(BF16)
    if keep_ref.shape[1] > width:
        keep_out[:, width:] = keep_ref[mine, width:] + take_exact(got_ref[mine, width:])
        put_exact(send_out, slice(None), width, keep_ref[other, width:] + take_exact(got_ref[other, width:]))


def middle_kernel(stream_ref, keep_ref, got_ref, out_ref):
    out_ref[...] = (
        stream_ref[...].astype(F32) + (keep_ref[...] + got_ref[...].astype(F32))
    ).astype(BF16)


def put_exact(ref, rows, at, value):
    high = value.astype(BF16)
    ref[rows, at : at + LANES] = high
    ref[rows, at + LANES : at + 2 * LANES] = (value - high.astype(F32)).astype(BF16)


def take_exact(tile):
    return tile[:, :LANES].astype(F32) + tile[:, LANES:].astype(F32)


def prepare_kernel(meta_ref, piece_ref, gain_ref, row_ref, square_ref):
    model = piece_ref.shape[1]
    gain = gain_ref[:, pl.ds(pl.multiple_of(meta_ref[3] * model, model), model)]
    wide = piece_ref[...].astype(F32)
    row_ref[...] = (wide * gain).astype(BF16)
    square_ref[...] = jnp.broadcast_to(jnp.sum(wide * wide, axis=1, keepdims=True), square_ref.shape)


def first_gate_kernel(n_sec, width, tile, meta_ref, *refs):
    pieces, squares = refs[:4], refs[4:8]
    gate_ref, up_ref, keep_ref, send_ref, rows_ref = refs[8:]
    rows = pieces[0].shape[0]
    half = rows_ref.shape[0] // 2
    for n, (piece, square) in enumerate(zip(pieces, squares)):
        at = place_of(meta_ref, n_sec, n, rows, len(pieces))
        rows_ref[pl.ds(at, rows), :] = piece[...]

        @pl.when(at < half)
        def _():
            keep_ref[pl.ds(at, rows), 2 * width :] = square[...]

        @pl.when(at >= half)
        def _():
            put_exact(send_ref, pl.ds(pl.multiple_of(at - half, rows), rows), 2 * width, square[...])

    product(rows_ref, gate_ref, 0, keep_ref, send_ref, 0, width, tile)
    product(rows_ref, up_ref, 0, keep_ref, send_ref, width, width, tile)


def gate_kernel(start, width, tile, rows_ref, gate_ref, up_ref, keep_ref, send_ref):
    product(rows_ref, gate_ref, start, keep_ref, send_ref, 0, width, tile)
    product(rows_ref, up_ref, start, keep_ref, send_ref, width, width, tile)


def scale_kernel(model, keep_ref, got_ref, out_ref):
    at = keep_ref.shape[1] - LANES
    square = keep_ref[:, at:] + take_exact(got_ref[:, at:])
    out_ref[...] = lax.rsqrt(square / model + EPS)


def hidden_kernel(scale_ref, keep_ref, got_ref, out_ref):
    width = out_ref.shape[1]
    scale = scale_ref[...]
    for at in range(0, width, LANES):
        gate = keep_ref[:, at : at + LANES] + got_ref[:, at : at + LANES].astype(F32)
        up = keep_ref[:, width + at : width + at + LANES] + got_ref[
            :, width + at : width + at + LANES
        ].astype(F32)
        gate = gate * scale
        out_ref[:, at : at + LANES] = (
            gate / (1.0 + jnp.exp(-gate)) * (up * scale)
        ).astype(BF16)


def first_hidden_kernel(model, keep_ref, got_ref, out_ref, scale_ref):
    scale_kernel(model, keep_ref, got_ref, scale_ref)
    hidden_kernel(scale_ref, keep_ref, got_ref, out_ref)


def down_kernel(n_chunk, tile, meta_ref, *refs):
    pieces = refs[: 4 * n_chunk]
    weight_ref, own_ref = refs[4 * n_chunk : 4 * n_chunk + 2]
    sends, rows_ref = refs[4 * n_chunk + 2 : -1], refs[-1]
    rows = pieces[0].shape[0]
    shard, place = meta_ref[0], meta_ref[3]
    for n in range(4):
        at = pl.ds(pl.multiple_of((shard ^ place ^ n) * rows, rows), rows)
        start = 0
        for c in range(n_chunk):
            piece = pieces[n * n_chunk + c]
            rows_ref[at, start : start + piece.shape[1]] = piece[...]
            start += piece.shape[1]

    for at in range(0, weight_ref.shape[1], tile):
        columns = slice(at, at + tile)
        part = jnp.dot(rows_ref[...], weight_ref[:, columns], preferred_element_type=F32)
        own_ref[:, columns] = part[:rows]
        for n, send in enumerate(sends):
            send[:, columns] = part[(n + 1) * rows : (n + 2) * rows].astype(BF16)


def final_kernel(middle_ref, own_ref, *refs):
    parts, out_ref = refs[:-1], refs[-1]
    total = own_ref[...]
    for part in parts:
        total = total + part[...].astype(F32)
    out_ref[...] = (middle_ref[...].astype(F32) + total).astype(BF16)


def swap(x, axis):
    return lax.ppermute(x, axis, [(0, 1), (1, 0)])


def turn(x, axis, n, offset):
    return lax.ppermute(x, axis, [(i, i ^ offset) for i in range(n)])


def direct_body(
    queries,
    key_cache,
    value_cache,
    block_index,
    stream,
    out_weight,
    norm_gain,
    gate_weight,
    up_weight,
    down_weight,
):
    n_context, n_head, n_sec = (lax.axis_size(a) for a in ALL)
    shard, head, sec = (lax.axis_index(a) for a in ALL)
    place = head * n_sec + sec
    meta = jnp.concatenate(
        [jnp.stack([shard, head, sec, place]).astype(jnp.int32), block_index[0]]
    )
    rows, heads_width = queries.shape
    context_len = key_cache.shape[0] * n_context
    model = norm_gain.shape[0]
    total = rows * n_context
    blocks = key_cache.shape[0] // KB
    kv_width = key_cache.shape[1]
    order = (3, 1, 2)

    got_q = {m: turn(queries, "ctx", n_context, m) for m in order}
    picked = struct((MOST * KB, kv_width), BF16)
    partial_out = struct((rows, heads_width + LANES), BF16)
    kv_dev = kv_width // DH
    tall = heads_width // kv_width * rows
    scratch = [
        pltpu.VMEM((kv_dev, tall, MOST * KB), F32),
        pltpu.VMEM((kv_dev, tall, MOST * KB), BF16),
    ]
    keys, values, own_partial = call(
        functools.partial(first_attend_kernel, blocks, context_len, total),
        (picked, picked, partial_out),
        [SM, ANY, ANY, ANY],
        (meta, in_hbm(queries), in_hbm(key_cache), in_hbm(value_cache)),
        scratch=[pltpu.VMEM((rows, heads_width), BF16)]
        + scratch
        + [pltpu.SemaphoreType.DMA((2, MOST)), pltpu.SemaphoreType.DMA],
    )
    partial = {0: own_partial}
    for m in order:
        partial[m] = call(
            functools.partial(attend, m, blocks, context_len, total),
            partial_out,
            [SM, VM, VM, VM],
            (meta, got_q[m], keys, values),
            scratch=scratch,
        )
    back = {m: turn(partial[m], "ctx", n_context, m) for m in order}
    back[0] = partial[0]
    blended = call(
        blend_kernel, struct((rows, heads_width), BF16), [VM] * 4, tuple(back[m] for m in range(4))
    )

    attention = {m: turn(blended, "ctx", n_context, m) for m in order}
    attention[0] = blended
    width = out_weight.shape[1]
    keep, away = call(
        functools.partial(project_kernel, n_sec, 512),
        (struct((n_head * rows, width), F32), struct((n_head * rows, width), BF16)),
        [SM] + [VM] * 5,
        (meta,) + tuple(attention[m] for m in range(4)) + (in_vmem(out_weight),),
        scratch=[pltpu.VMEM((total, heads_width), BF16)],
    )
    got = swap(away, "sec")
    keep, away = call(
        functools.partial(fold_kernel, width),
        (struct((rows, width), F32), struct((rows, width), BF16)),
        [SM, VM, VM],
        (meta, keep, got),
        cost=6,
    )
    got = swap(away, "head")
    middle = call(middle_kernel, struct((rows, width), BF16), [VM] * 3, (stream, keep, got), cost=6)

    all_middle = {
        m: lax.ppermute(
            middle,
            ALL,
            [
                (a * n_context + b, (b ^ m) * n_context + a)
                for a in range(n_context)
                for b in range(n_context)
            ],
        )
        for m in (3, 0, 1, 2)
    }
    hidden_width = gate_weight.shape[1]
    first = hidden_width // 2 // LANES * LANES
    chunks = ((0, first), (first, hidden_width - first))
    hidden = []
    gate_vmem, up_vmem = in_vmem(gate_weight), in_vmem(up_weight)
    prepared = [
        call(
            prepare_kernel,
            (struct((rows, width), BF16), struct((rows, LANES), F32)),
            [SM, VM, VM],
            (meta, all_middle[m], norm_gain[None]),
        )
        for m in range(4)
    ]
    scale = None
    for c, (start, chunk) in enumerate(chunks):
        extra = LANES if c == 0 else 0
        out = (
            struct((n_head * rows, 2 * chunk + extra), F32),
            struct((n_head * rows, 2 * chunk + 2 * extra), BF16),
        )
        if c == 0:
            keep, away, all_rows = call(
                functools.partial(first_gate_kernel, n_sec, chunk, 512),
                out + (struct((total, width), BF16),),
                [SM] + [VM] * 10,
                (meta,)
                + tuple(p[0] for p in prepared)
                + tuple(p[1] for p in prepared)
                + (gate_vmem, up_vmem),
            )
        else:
            keep, away = call(
                functools.partial(gate_kernel, start, chunk, 512),
                out,
                [VM] * 3,
                (all_rows, gate_vmem, up_vmem),
            )
        keep, away = call(
            functools.partial(fold_kernel, 2 * chunk),
            (
                struct((rows, 2 * chunk + extra), F32),
                struct((rows, 2 * chunk + 2 * extra), BF16),
            ),
            [SM, VM, VM],
            (meta, keep, swap(away, "sec")),
        )
        got = swap(away, "head")
        if c == 0:
            own, scale = call(
                functools.partial(first_hidden_kernel, model),
                (struct((rows, chunk), BF16), struct((rows, LANES), F32)),
                [VM] * 2,
                (keep, got),
            )
        else:
            own = call(hidden_kernel, struct((rows, chunk), BF16), [VM] * 3, (scale, keep, got))
        across = swap(own, "head")
        beside = swap(own, "sec")
        hidden.append((own, beside, across, swap(across, "sec")))
    n_chunk = len(chunks)

    out_width = down_weight.shape[1]
    res = call(
        functools.partial(down_kernel, n_chunk, 512),
        (struct((rows, out_width), F32),) + (struct((rows, out_width), BF16),) * 3,
        [SM] + [VM] * (4 * n_chunk + 1),
        (meta,)
        + tuple(hidden[c][n] for n in range(4) for c in range(n_chunk))
        + (in_vmem(down_weight),),
        scratch=[pltpu.VMEM((total, hidden_width), BF16)],
    )
    parts = [turn(res[m], "ctx", n_context, m) for m in order]
    return call(
        final_kernel, struct((rows, out_width), BF16), [VM] * 5, (all_middle[0], res[0]) + tuple(parts)
    )


def local_attention(gathered, key_cache, value_cache, block_index, context_index, context_len):
    group_size = HQ // KVH
    kv_dev = key_cache.shape[1] // DH
    blocks_dev = key_cache.shape[0] // KB
    total_tokens = gathered.shape[0]
    key_blocks = key_cache.reshape(blocks_dev, KB, kv_dev, DH)
    value_blocks = value_cache.reshape(blocks_dev, KB, kv_dev, DH)
    local_ids = context_index * blocks_dev + jnp.arange(blocks_dev, dtype=jnp.int32)
    member = jnp.any(block_index[:, :, None] == local_ids[None, None, :], axis=1)
    member_rank = jnp.cumsum(member.astype(jnp.int32), axis=1) - 1
    slot_hit = member[:, None, :] & (
        member_rank[:, None, :] == jnp.arange(MOST, dtype=jnp.int32)[None, :, None]
    )
    slot_block = jnp.sum(
        jnp.where(slot_hit, jnp.arange(blocks_dev, dtype=jnp.int32)[None, None, :], 0), axis=2
    )
    slot_valid = jnp.any(slot_hit, axis=2)
    picked_keys = jnp.take(key_blocks, slot_block[0], axis=0).reshape(MOST * KB, kv_dev, DH)
    picked_values = jnp.take(value_blocks, slot_block[0], axis=0).reshape(MOST * KB, kv_dev, DH)
    key_pos = (
        (local_ids[0] + slot_block[0])[:, None] * KB + jnp.arange(KB, dtype=jnp.int32)[None, :]
    ).reshape(-1)
    live_keys = jnp.broadcast_to(slot_valid[0][:, None], (MOST, KB)).reshape(-1)
    query_pos = context_len - total_tokens + jnp.arange(KB, dtype=jnp.int32)
    allowed = live_keys[None, :] & (key_pos[None, :] <= query_pos[:, None])
    query_block = gathered.reshape(KB, kv_dev, group_size, DH)
    scores = jnp.einsum(
        "qhgd,phd->hgqp", query_block, picked_keys, preferred_element_type=jnp.float32
    ) / math.sqrt(DH)
    scores = jnp.where(allowed[None, None], scores, -jnp.inf)
    peak_score = jnp.max(scores, axis=-1, keepdims=True)
    unnormed = jnp.exp(scores - peak_score)
    row_total = jnp.sum(unnormed, axis=-1)
    mixture = jnp.einsum(
        "hgqp,phd->qhgd",
        unnormed.astype(jnp.bfloat16),
        picked_values,
        preferred_element_type=jnp.float32,
    )
    result = mixture / jnp.transpose(row_total, (2, 0, 1))[..., None]
    log_total = jnp.transpose(peak_score[..., 0] + jnp.log(row_total), (2, 0, 1))
    out_list = result.reshape(KB, -1)
    lse_list = log_total.reshape(KB, -1)
    return (out_list, lse_list)


def general_body(
    queries,
    key_cache,
    value_cache,
    block_index,
    stream,
    out_weight,
    norm_gain,
    gate_weight,
    up_weight,
    down_weight,
):
    n_context = lax.axis_size("ctx")
    context_index = lax.axis_index("ctx")
    context_len = key_cache.shape[0] * n_context
    gathered = lax.all_gather(queries, "ctx", axis=0, tiled=True)
    part_out, part_lse = local_attention(
        gathered, key_cache, value_cache, block_index, context_index, context_len
    )
    spread_out, spread_lse = (
        lax.all_to_all(part_out[:, None, :], "ctx", split_axis=0, concat_axis=1, tiled=True),
        lax.all_to_all(part_lse[:, None, :], "ctx", split_axis=0, concat_axis=1, tiled=True),
    )
    share_rows = spread_out.shape[0]
    head_count = spread_lse.shape[2]
    peak_value = jnp.max(spread_lse, axis=1, keepdims=True)
    share_weight = jnp.exp(spread_lse - peak_value)
    blended = jnp.sum(
        spread_out.reshape(share_rows, n_context, head_count, -1) * share_weight[..., None], axis=1
    )
    blended = blended / jnp.sum(share_weight, axis=1)[..., None]
    attention = lax.all_gather(
        blended.reshape(share_rows, -1).astype(jnp.bfloat16), "ctx", axis=0, tiled=True
    )
    row_piece = attention
    projected = lax.psum_scatter(
        jnp.dot(row_piece, out_weight, preferred_element_type=jnp.float32),
        ("head", "sec"),
        scatter_dimension=0,
        tiled=True,
    )
    middle = (stream.astype(jnp.float32) + projected).astype(jnp.bfloat16)
    full_middle = lax.all_gather(middle, "ctx", axis=1, tiled=True)
    middle_wide = full_middle.astype(jnp.float32)
    mean_square = jnp.mean(middle_wide * middle_wide, axis=-1, keepdims=True)
    normed = (middle_wide * lax.rsqrt(mean_square + 1e-05) * norm_gain).astype(jnp.bfloat16)
    normed_cols, middle_cols = (
        lax.all_to_all(normed, ("head", "sec"), split_axis=1, concat_axis=0, tiled=True),
        lax.all_to_all(full_middle, ("head", "sec"), split_axis=1, concat_axis=0, tiled=True),
    )
    row_piece = normed_cols
    gate_up = lax.psum_scatter(
        jnp.concatenate(
            [
                jnp.dot(row_piece, gate_weight, preferred_element_type=jnp.float32),
                jnp.dot(row_piece, up_weight, preferred_element_type=jnp.float32),
            ],
            axis=1,
        ),
        ("head", "sec"),
        scatter_dimension=0,
        tiled=True,
    )
    hidden_width = gate_weight.shape[1]
    hidden = (jax.nn.silu(gate_up[:, :hidden_width]) * gate_up[:, hidden_width:]).astype(
        jnp.bfloat16
    )
    all_hidden = lax.all_gather(hidden, ("head", "sec"), axis=0, tiled=True)
    row_piece = all_hidden
    down_part = lax.psum_scatter(
        jnp.dot(row_piece, down_weight, preferred_element_type=jnp.float32),
        "ctx",
        scatter_dimension=0,
        tiled=True,
    )
    own_middle = lax.dynamic_slice_in_dim(
        middle_cols, context_index * down_part.shape[0], down_part.shape[0], 0
    )
    return (own_middle.astype(jnp.float32) + down_part).astype(jnp.bfloat16)


def solution(mesh):
    size = dict(mesh.shape)
    direct = size["ctx"] == 4 and size["head"] == 2 and size["sec"] == 2
    return jax.shard_map(
        direct_body if direct else general_body,
        mesh=mesh,
        in_specs=(
            P(("groups", "ctx"), ("head", "sec")),
            P(("groups", "ctx"), ("head", "sec")),
            P(("groups", "ctx"), ("head", "sec")),
            P("groups", None),
            P(("groups", "head", "sec"), "ctx"),
            P(("head", "sec"), "ctx"),
            P(),
            P(("head", "sec"), "ctx"),
            P(("head", "sec"), "ctx"),
            P("ctx", ("head", "sec")),
        ),
        out_specs=P(("groups", "ctx"), ("head", "sec")),
        check_vma=False,
    )
```

```python
import functools
import math

import jax
import jax.numpy as jnp
from jax import lax
from jax.experimental import pallas as pl
from jax.experimental.pallas import tpu as pltpu
from jax.sharding import PartitionSpec as P


HQ = 64
KVH = 8
DH = 128
KB = 128
MOST = 4
LANES = 128
EPS = 1e-05
ALL = ("ctx", "head", "sec")


VM = pl.BlockSpec(memory_space=pltpu.VMEM)
SM = pl.BlockSpec(memory_space=pltpu.SMEM)
ANY = pl.BlockSpec(memory_space=pl.ANY)
F32 = jnp.float32
BF16 = jnp.bfloat16


def struct(shape, dtype):
    return jax.ShapeDtypeStruct(shape, dtype)


def call(kernel, out, in_specs, args, cost=3, scratch=(), vmem=8):
    outs = out if isinstance(out, (tuple, list)) else (out,)
    nbytes = sum(math.prod(a.shape) * a.dtype.itemsize for a in args)
    nbytes += sum(math.prod(o.shape) * o.dtype.itemsize for o in outs)
    return pl.pallas_call(
        kernel,
        out_shape=out,
        in_specs=in_specs,
        out_specs=jax.tree.map(lambda _: VM, out),
        scratch_shapes=scratch,
        compiler_params=pltpu.CompilerParams(vmem_limit_bytes=vmem << 20),
        cost_estimate=pl.CostEstimate(flops=cost * 10**9, bytes_accessed=nbytes, transcendentals=0),
    )(*args)


def in_vmem(x):
    return pltpu.with_memory_space_constraint(x, pltpu.VMEM)


def in_hbm(x):
    return pltpu.with_memory_space_constraint(x, pltpu.HBM)


N_META = 4


def slots(meta_ref, blocks):
    entries = meta_ref.shape[0] - N_META
    base = meta_ref[0] * blocks
    first = jnp.int32(0)
    end = jnp.int32(0)
    for n in range(entries):
        block = meta_ref[N_META + n]
        first += (block < base).astype(jnp.int32)
        end += (block < base + blocks).astype(jnp.int32)
    found = []
    for slot in range(MOST):
        entry = jnp.minimum(first + slot, entries - 1)
        local = jnp.clip(meta_ref[N_META + entry] - base, 0, blocks - 1)
        found.append((local, first + slot < end))
    return found


def attend(offset, blocks, context_len, total, meta_ref, q_ref, key_ref, value_ref, out_ref, score_ref, weight_ref):
    rows = q_ref.shape[0]
    heads = q_ref.shape[1] // DH
    kv_dev = key_ref.shape[1] // DH
    group = heads // kv_dev
    shard = meta_ref[0]
    scale = 1.0 / math.sqrt(DH)
    token0 = context_len - total + (shard ^ offset) * rows
    limits = [
        jnp.where(valid, token0 - (shard * blocks + local) * KB, jnp.int32(-(1 << 20)))
        for local, valid in slots(meta_ref, blocks)
    ]
    ahead = lax.broadcasted_iota(jnp.int32, (rows, KB), 1) - lax.broadcasted_iota(
        jnp.int32, (rows, KB), 0
    )
    allowed = [ahead <= limit for limit in limits]
    head_lane = lax.broadcasted_iota(jnp.int32, (rows, LANES), 1)
    peak_tile = jnp.zeros((rows, LANES), F32)
    total_tile = jnp.ones((rows, LANES), F32)
    for kv in range(kv_dev):
        stacked = jnp.concatenate(
            [q_ref[:, (kv * group + h) * DH : (kv * group + h + 1) * DH] for h in range(group)], axis=0
        )
        score_ref[kv] = lax.dot_general(
            stacked,
            key_ref[:, kv * DH : (kv + 1) * DH],
            (((1,), (1,)), ((), ())),
            preferred_element_type=F32,
        )
    for kv in range(kv_dev):
        for h in range(group):
            head = kv * group + h
            span = slice(h * rows, (h + 1) * rows)
            parts = [
                jnp.where(allowed[slot], score_ref[kv, span, slot * KB : (slot + 1) * KB], -1e30)
                for slot in range(MOST)
            ]
            peak = jnp.max(functools.reduce(jnp.maximum, parts), axis=1, keepdims=True)
            parts = [jnp.exp((p - peak) * scale) for p in parts]
            row_total = jnp.sum(functools.reduce(jnp.add, parts), axis=1, keepdims=True)
            for slot, p in enumerate(parts):
                weight_ref[kv, span, slot * KB : (slot + 1) * KB] = p.astype(BF16)
            peak_tile = jnp.where(head_lane == head, peak, peak_tile)
            total_tile = jnp.where(head_lane == head, row_total, total_tile)
    inverse = 1.0 / total_tile
    for kv in range(kv_dev):
        mixture = jnp.dot(
            weight_ref[kv], value_ref[:, kv * DH : (kv + 1) * DH], preferred_element_type=F32
        )
        for h in range(group):
            head = kv * group + h
            out_ref[:, head * DH : (head + 1) * DH] = (
                mixture[h * rows : (h + 1) * rows] * inverse[:, head : head + 1]
            ).astype(BF16)
    lse_tile = peak_tile * scale + jnp.log(total_tile)
    high = lse_tile.astype(BF16).astype(F32)
    rest = lse_tile - high
    mid = rest.astype(BF16).astype(F32)
    low = rest - mid
    tile = high + pltpu.roll(mid, heads, 1) + pltpu.roll(low, 2 * heads, 1)
    out_ref[:, heads * DH :] = tile.astype(BF16)


def first_attend_kernel(
    blocks, context_len, total, meta_ref, q_hbm, key_hbm, value_hbm,
    key_ref, value_ref, out_ref, q_ref, score_ref, weight_ref, sems, q_sem,
):
    copies = [pltpu.make_async_copy(q_hbm, q_ref, q_sem)]
    for slot, (local, _) in enumerate(slots(meta_ref, blocks)):
        rows = pl.ds(pl.multiple_of(local * KB, KB), KB)
        for n, (src, dst) in enumerate(((key_hbm, key_ref), (value_hbm, value_ref))):
            copies.append(
                pltpu.make_async_copy(
                    src.at[rows, :], dst.at[slot * KB : (slot + 1) * KB, :], sems.at[n, slot]
                )
            )
    for copy in copies:
        copy.start()
    for copy in copies:
        copy.wait()
    attend(
        0, blocks, context_len, total, meta_ref, q_ref, key_ref, value_ref, out_ref, score_ref, weight_ref
    )


def blend_kernel(*refs):
    out_ref = refs[-1]
    parts = refs[:-1]
    heads = out_ref.shape[1] // DH
    logs = []
    for part in parts:
        tile = part[:, heads * DH :].astype(F32)
        logs.append(
            tile + pltpu.roll(tile, LANES - heads, 1) + pltpu.roll(tile, LANES - 2 * heads, 1)
        )
    peak = functools.reduce(jnp.maximum, logs)
    shares = [jnp.exp(log - peak) for log in logs]
    total = functools.reduce(jnp.add, shares)
    shares = [share / total for share in shares]
    for head in range(heads):
        span = slice(head * DH, (head + 1) * DH)
        out_ref[:, span] = functools.reduce(
            jnp.add,
            [share[:, head : head + 1] * part[:, span].astype(F32) for share, part in zip(shares, parts)],
        ).astype(BF16)


def place_of(meta_ref, n_sec, n, rows, count):
    owner = meta_ref[0] ^ n
    other = ((owner % n_sec) != meta_ref[2]).astype(jnp.int32)
    return pl.multiple_of(other * (count // n_sec * rows) + owner // n_sec * rows, rows)


def product(rows_ref, weight_ref, source, keep_ref, send_ref, target, width, tile):
    half = rows_ref.shape[0] // 2
    for at in range(0, width, tile):
        size = min(tile, width - at)
        part = jnp.dot(
            rows_ref[...],
            weight_ref[:, source + at : source + at + size],
            preferred_element_type=F32,
        )
        keep_ref[:, target + at : target + at + size] = part[:half]
        send_ref[:, target + at : target + at + size] = part[half:].astype(BF16)


def project_kernel(n_sec, tile, meta_ref, *refs):
    pieces, (weight_ref, keep_ref, send_ref, rows_ref) = refs[:-4], refs[-4:]
    rows = pieces[0].shape[0]
    for n, piece in enumerate(pieces):
        rows_ref[pl.ds(place_of(meta_ref, n_sec, n, rows, len(pieces)), rows), :] = piece[...]
    product(rows_ref, weight_ref, 0, keep_ref, send_ref, 0, weight_ref.shape[1], tile)


def fold_kernel(width, meta_ref, keep_ref, got_ref, keep_out, send_out):
    rows = keep_out.shape[0]
    mine = pl.ds(pl.multiple_of(meta_ref[1] * rows, rows), rows)
    other = pl.ds(pl.multiple_of((1 - meta_ref[1]) * rows, rows), rows)
    keep_out[:, :width] = keep_ref[mine, :width] + got_ref[mine, :width].astype(F32)
    send_out[:, :width] = (keep_ref[other, :width] + got_ref[other, :width].astype(F32)).astype(BF16)
    if keep_ref.shape[1] > width:
        keep_out[:, width:] = keep_ref[mine, width:] + take_exact(got_ref[mine, width:])
        put_exact(send_out, slice(None), width, keep_ref[other, width:] + take_exact(got_ref[other, width:]))


def middle_kernel(stream_ref, keep_ref, got_ref, out_ref):
    out_ref[...] = (
        stream_ref[...].astype(F32) + (keep_ref[...] + got_ref[...].astype(F32))
    ).astype(BF16)


def put_exact(ref, rows, at, value):
    high = value.astype(BF16)
    ref[rows, at : at + LANES] = high
    ref[rows, at + LANES : at + 2 * LANES] = (value - high.astype(F32)).astype(BF16)


def take_exact(tile):
    return tile[:, :LANES].astype(F32) + tile[:, LANES:].astype(F32)


def prepare_kernel(meta_ref, piece_ref, gain_ref, row_ref, square_ref):
    model = piece_ref.shape[1]
    gain = gain_ref[:, pl.ds(pl.multiple_of(meta_ref[3] * model, model), model)]
    wide = piece_ref[...].astype(F32)
    row_ref[...] = (wide * gain).astype(BF16)
    square_ref[...] = jnp.broadcast_to(jnp.sum(wide * wide, axis=1, keepdims=True), square_ref.shape)


def first_gate_kernel(n_sec, width, tile, meta_ref, *refs):
    pieces, squares = refs[:4], refs[4:8]
    gate_ref, up_ref, keep_ref, send_ref, rows_ref = refs[8:]
    rows = pieces[0].shape[0]
    half = rows_ref.shape[0] // 2
    for n, (piece, square) in enumerate(zip(pieces, squares)):
        at = place_of(meta_ref, n_sec, n, rows, len(pieces))
        rows_ref[pl.ds(at, rows), :] = piece[...]

        @pl.when(at < half)
        def _():
            keep_ref[pl.ds(at, rows), 2 * width :] = square[...]

        @pl.when(at >= half)
        def _():
            put_exact(send_ref, pl.ds(pl.multiple_of(at - half, rows), rows), 2 * width, square[...])

    product(rows_ref, gate_ref, 0, keep_ref, send_ref, 0, width, tile)
    product(rows_ref, up_ref, 0, keep_ref, send_ref, width, width, tile)


def gate_kernel(start, width, tile, rows_ref, gate_ref, up_ref, keep_ref, send_ref):
    product(rows_ref, gate_ref, start, keep_ref, send_ref, 0, width, tile)
    product(rows_ref, up_ref, start, keep_ref, send_ref, width, width, tile)


def scale_kernel(model, keep_ref, got_ref, out_ref):
    at = keep_ref.shape[1] - LANES
    square = keep_ref[:, at:] + take_exact(got_ref[:, at:])
    out_ref[...] = lax.rsqrt(square / model + EPS)


def hidden_kernel(scale_ref, keep_ref, got_ref, out_ref):
    width = out_ref.shape[1]
    scale = scale_ref[...]
    for at in range(0, width, LANES):
        gate = keep_ref[:, at : at + LANES] + got_ref[:, at : at + LANES].astype(F32)
        up = keep_ref[:, width + at : width + at + LANES] + got_ref[
            :, width + at : width + at + LANES
        ].astype(F32)
        gate = gate * scale
        out_ref[:, at : at + LANES] = (
            gate / (1.0 + jnp.exp(-gate)) * (up * scale)
        ).astype(BF16)


def first_hidden_kernel(model, keep_ref, got_ref, out_ref, scale_ref):
    scale_kernel(model, keep_ref, got_ref, scale_ref)
    hidden_kernel(scale_ref, keep_ref, got_ref, out_ref)


def gather_rows(meta_ref, pieces, rows_ref):
    rows = pieces[0].shape[0]
    for n, piece in enumerate(pieces):
        at = pl.ds(pl.multiple_of((meta_ref[0] ^ meta_ref[3] ^ n) * rows, rows), rows)
        rows_ref[at, :] = piece[...]


def first_down_kernel(tile, meta_ref, *refs):
    pieces, (weight_ref, out_ref, rows_ref) = refs[:4], refs[4:]
    gather_rows(meta_ref, pieces, rows_ref)
    depth = rows_ref.shape[1]
    for at in range(0, weight_ref.shape[1], tile):
        out_ref[:, at : at + tile] = jnp.dot(
            rows_ref[...], weight_ref[:depth, at : at + tile], preferred_element_type=F32
        )


def down_kernel(tile, meta_ref, *refs):
    pieces, (weight_ref, so_far_ref, own_ref) = refs[:4], refs[4:7]
    sends, rows_ref = refs[7:-1], refs[-1]
    gather_rows(meta_ref, pieces, rows_ref)
    rows = pieces[0].shape[0]
    depth = rows_ref.shape[1]
    start = weight_ref.shape[0] - depth
    for at in range(0, weight_ref.shape[1], tile):
        columns = slice(at, at + tile)
        part = so_far_ref[:, columns] + jnp.dot(
            rows_ref[...], weight_ref[start:, columns], preferred_element_type=F32
        )
        own_ref[:, columns] = part[:rows]
        for n, send in enumerate(sends):
            send[:, columns] = part[(n + 1) * rows : (n + 2) * rows].astype(BF16)


def final_kernel(middle_ref, own_ref, *refs):
    parts, out_ref = refs[:-1], refs[-1]
    total = own_ref[...]
    for part in parts:
        total = total + part[...].astype(F32)
    out_ref[...] = (middle_ref[...].astype(F32) + total).astype(BF16)


def swap(x, axis):
    return lax.ppermute(x, axis, [(0, 1), (1, 0)])


def turn(x, axis, n, offset):
    return lax.ppermute(x, axis, [(i, i ^ offset) for i in range(n)])


def direct_body(
    queries,
    key_cache,
    value_cache,
    block_index,
    stream,
    out_weight,
    norm_gain,
    gate_weight,
    up_weight,
    down_weight,
):
    n_context, n_head, n_sec = (lax.axis_size(a) for a in ALL)
    shard, head, sec = (lax.axis_index(a) for a in ALL)
    place = head * n_sec + sec
    meta = jnp.concatenate(
        [jnp.stack([shard, head, sec, place]).astype(jnp.int32), block_index[0]]
    )
    rows, heads_width = queries.shape
    context_len = key_cache.shape[0] * n_context
    model = norm_gain.shape[0]
    total = rows * n_context
    blocks = key_cache.shape[0] // KB
    kv_width = key_cache.shape[1]
    order = (3, 2, 1)

    got_q = {m: turn(queries, "ctx", n_context, m) for m in order}
    picked = struct((MOST * KB, kv_width), BF16)
    partial_out = struct((rows, heads_width + LANES), BF16)
    kv_dev = kv_width // DH
    tall = heads_width // kv_width * rows
    scratch = [
        pltpu.VMEM((kv_dev, tall, MOST * KB), F32),
        pltpu.VMEM((kv_dev, tall, MOST * KB), BF16),
    ]
    keys, values, own_partial = call(
        functools.partial(first_attend_kernel, blocks, context_len, total),
        (picked, picked, partial_out),
        [SM, ANY, ANY, ANY],
        (meta, in_hbm(queries), in_hbm(key_cache), in_hbm(value_cache)),
        scratch=[pltpu.VMEM((rows, heads_width), BF16)]
        + scratch
        + [pltpu.SemaphoreType.DMA((2, MOST)), pltpu.SemaphoreType.DMA],
    )
    partial = {0: own_partial}
    for m in order:
        partial[m] = call(
            functools.partial(attend, m, blocks, context_len, total),
            partial_out,
            [SM, VM, VM, VM],
            (meta, got_q[m], keys, values),
            scratch=scratch,
        )
    back = {m: turn(partial[m], "ctx", n_context, m) for m in order}
    back[0] = partial[0]
    blended = call(
        blend_kernel, struct((rows, heads_width), BF16), [VM] * 4, tuple(back[m] for m in range(4))
    )

    attention = {m: turn(blended, "ctx", n_context, m) for m in order}
    attention[0] = blended
    width = out_weight.shape[1]
    keep, away = call(
        functools.partial(project_kernel, n_sec, 512),
        (struct((n_head * rows, width), F32), struct((n_head * rows, width), BF16)),
        [SM] + [VM] * 5,
        (meta,) + tuple(attention[m] for m in range(4)) + (in_vmem(out_weight),),
        scratch=[pltpu.VMEM((total, heads_width), BF16)],
        cost=6,
    )
    got = swap(away, "sec")
    keep, away = call(
        functools.partial(fold_kernel, width),
        (struct((rows, width), F32), struct((rows, width), BF16)),
        [SM, VM, VM],
        (meta, keep, got),
        cost=6,
    )
    got = swap(away, "head")
    middle = call(middle_kernel, struct((rows, width), BF16), [VM] * 3, (stream, keep, got), cost=6)

    all_middle = {
        m: lax.ppermute(
            middle,
            ALL,
            [
                (a * n_context + b, (b ^ m) * n_context + a)
                for a in range(n_context)
                for b in range(n_context)
            ],
        )
        for m in (3, 0, 1, 2)
    }
    hidden_width = gate_weight.shape[1]
    first = hidden_width // 2 // LANES * LANES
    chunks = ((0, first), (first, hidden_width - first))
    hidden = []
    gate_vmem, up_vmem = in_vmem(gate_weight), in_vmem(up_weight)
    prepared = [
        call(
            prepare_kernel,
            (struct((rows, width), BF16), struct((rows, LANES), F32)),
            [SM, VM, VM],
            (meta, all_middle[m], norm_gain[None]),
            cost=0,
        )
        for m in range(4)
    ]
    scale = None
    for c, (start, chunk) in enumerate(chunks):
        extra = LANES if c == 0 else 0
        out = (
            struct((n_head * rows, 2 * chunk + extra), F32),
            struct((n_head * rows, 2 * chunk + 2 * extra), BF16),
        )
        if c == 0:
            keep, away, all_rows = call(
                functools.partial(first_gate_kernel, n_sec, chunk, 512),
                out + (struct((total, width), BF16),),
                [SM] + [VM] * 10,
                (meta,)
                + tuple(p[0] for p in prepared)
                + tuple(p[1] for p in prepared)
                + (gate_vmem, up_vmem),
            )
        else:
            keep, away = call(
                functools.partial(gate_kernel, start, chunk, 512),
                out,
                [VM] * 3,
                (all_rows, gate_vmem, up_vmem),
            )
        keep, away = call(
            functools.partial(fold_kernel, 2 * chunk),
            (
                struct((rows, 2 * chunk + extra), F32),
                struct((rows, 2 * chunk + 2 * extra), BF16),
            ),
            [SM, VM, VM],
            (meta, keep, swap(away, "sec")),
        )
        got = swap(away, "head")
        if c == 0:
            own, scale = call(
                functools.partial(first_hidden_kernel, model),
                (struct((rows, chunk), BF16), struct((rows, LANES), F32)),
                [VM] * 2,
                (keep, got),
            )
        else:
            own = call(hidden_kernel, struct((rows, chunk), BF16), [VM] * 3, (scale, keep, got))
        across = swap(own, "head")
        beside = swap(own, "sec")
        hidden.append((own, beside, across, swap(across, "sec")))
    out_width = down_weight.shape[1]
    down_vmem = in_vmem(down_weight)
    so_far = call(
        functools.partial(first_down_kernel, 512),
        struct((total, out_width), F32),
        [SM] + [VM] * 5,
        (meta,) + hidden[0] + (down_vmem,),
        scratch=[pltpu.VMEM((total, chunks[0][1]), BF16)],
    )
    res = call(
        functools.partial(down_kernel, 512),
        (struct((rows, out_width), F32),) + (struct((rows, out_width), BF16),) * 3,
        [SM] + [VM] * 6,
        (meta,) + hidden[1] + (down_vmem, so_far),
        scratch=[pltpu.VMEM((total, chunks[1][1]), BF16)],
    )
    parts = [turn(res[m], "ctx", n_context, m) for m in order]
    return call(
        final_kernel, struct((rows, out_width), BF16), [VM] * 5, (all_middle[0], res[0]) + tuple(parts)
    )


def local_attention(gathered, key_cache, value_cache, block_index, context_index, context_len):
    group_size = HQ // KVH
    kv_dev = key_cache.shape[1] // DH
    blocks_dev = key_cache.shape[0] // KB
    total_tokens = gathered.shape[0]
    key_blocks = key_cache.reshape(blocks_dev, KB, kv_dev, DH)
    value_blocks = value_cache.reshape(blocks_dev, KB, kv_dev, DH)
    local_ids = context_index * blocks_dev + jnp.arange(blocks_dev, dtype=jnp.int32)
    member = jnp.any(block_index[:, :, None] == local_ids[None, None, :], axis=1)
    member_rank = jnp.cumsum(member.astype(jnp.int32), axis=1) - 1
    slot_hit = member[:, None, :] & (
        member_rank[:, None, :] == jnp.arange(MOST, dtype=jnp.int32)[None, :, None]
    )
    slot_block = jnp.sum(
        jnp.where(slot_hit, jnp.arange(blocks_dev, dtype=jnp.int32)[None, None, :], 0), axis=2
    )
    slot_valid = jnp.any(slot_hit, axis=2)
    picked_keys = jnp.take(key_blocks, slot_block[0], axis=0).reshape(MOST * KB, kv_dev, DH)
    picked_values = jnp.take(value_blocks, slot_block[0], axis=0).reshape(MOST * KB, kv_dev, DH)
    key_pos = (
        (local_ids[0] + slot_block[0])[:, None] * KB + jnp.arange(KB, dtype=jnp.int32)[None, :]
    ).reshape(-1)
    live_keys = jnp.broadcast_to(slot_valid[0][:, None], (MOST, KB)).reshape(-1)
    query_pos = context_len - total_tokens + jnp.arange(KB, dtype=jnp.int32)
    allowed = live_keys[None, :] & (key_pos[None, :] <= query_pos[:, None])
    query_block = gathered.reshape(KB, kv_dev, group_size, DH)
    scores = jnp.einsum(
        "qhgd,phd->hgqp", query_block, picked_keys, preferred_element_type=jnp.float32
    ) / math.sqrt(DH)
    scores = jnp.where(allowed[None, None], scores, -jnp.inf)
    peak_score = jnp.max(scores, axis=-1, keepdims=True)
    unnormed = jnp.exp(scores - peak_score)
    row_total = jnp.sum(unnormed, axis=-1)
    mixture = jnp.einsum(
        "hgqp,phd->qhgd",
        unnormed.astype(jnp.bfloat16),
        picked_values,
        preferred_element_type=jnp.float32,
    )
    result = mixture / jnp.transpose(row_total, (2, 0, 1))[..., None]
    log_total = jnp.transpose(peak_score[..., 0] + jnp.log(row_total), (2, 0, 1))
    out_list = result.reshape(KB, -1)
    lse_list = log_total.reshape(KB, -1)
    return (out_list, lse_list)


def general_body(
    queries,
    key_cache,
    value_cache,
    block_index,
    stream,
    out_weight,
    norm_gain,
    gate_weight,
    up_weight,
    down_weight,
):
    n_context = lax.axis_size("ctx")
    context_index = lax.axis_index("ctx")
    context_len = key_cache.shape[0] * n_context
    gathered = lax.all_gather(queries, "ctx", axis=0, tiled=True)
    part_out, part_lse = local_attention(
        gathered, key_cache, value_cache, block_index, context_index, context_len
    )
    spread_out, spread_lse = (
        lax.all_to_all(part_out[:, None, :], "ctx", split_axis=0, concat_axis=1, tiled=True),
        lax.all_to_all(part_lse[:, None, :], "ctx", split_axis=0, concat_axis=1, tiled=True),
    )
    share_rows = spread_out.shape[0]
    head_count = spread_lse.shape[2]
    peak_value = jnp.max(spread_lse, axis=1, keepdims=True)
    share_weight = jnp.exp(spread_lse - peak_value)
    blended = jnp.sum(
        spread_out.reshape(share_rows, n_context, head_count, -1) * share_weight[..., None], axis=1
    )
    blended = blended / jnp.sum(share_weight, axis=1)[..., None]
    attention = lax.all_gather(
        blended.reshape(share_rows, -1).astype(jnp.bfloat16), "ctx", axis=0, tiled=True
    )
    row_piece = attention
    projected = lax.psum_scatter(
        jnp.dot(row_piece, out_weight, preferred_element_type=jnp.float32),
        ("head", "sec"),
        scatter_dimension=0,
        tiled=True,
    )
    middle = (stream.astype(jnp.float32) + projected).astype(jnp.bfloat16)
    full_middle = lax.all_gather(middle, "ctx", axis=1, tiled=True)
    middle_wide = full_middle.astype(jnp.float32)
    mean_square = jnp.mean(middle_wide * middle_wide, axis=-1, keepdims=True)
    normed = (middle_wide * lax.rsqrt(mean_square + 1e-05) * norm_gain).astype(jnp.bfloat16)
    normed_cols, middle_cols = (
        lax.all_to_all(normed, ("head", "sec"), split_axis=1, concat_axis=0, tiled=True),
        lax.all_to_all(full_middle, ("head", "sec"), split_axis=1, concat_axis=0, tiled=True),
    )
    row_piece = normed_cols
    gate_up = lax.psum_scatter(
        jnp.concatenate(
            [
                jnp.dot(row_piece, gate_weight, preferred_element_type=jnp.float32),
                jnp.dot(row_piece, up_weight, preferred_element_type=jnp.float32),
            ],
            axis=1,
        ),
        ("head", "sec"),
        scatter_dimension=0,
        tiled=True,
    )
    hidden_width = gate_weight.shape[1]
    hidden = (jax.nn.silu(gate_up[:, :hidden_width]) * gate_up[:, hidden_width:]).astype(
        jnp.bfloat16
    )
    all_hidden = lax.all_gather(hidden, ("head", "sec"), axis=0, tiled=True)
    row_piece = all_hidden
    down_part = lax.psum_scatter(
        jnp.dot(row_piece, down_weight, preferred_element_type=jnp.float32),
        "ctx",
        scatter_dimension=0,
        tiled=True,
    )
    own_middle = lax.dynamic_slice_in_dim(
        middle_cols, context_index * down_part.shape[0], down_part.shape[0], 0
    )
    return (own_middle.astype(jnp.float32) + down_part).astype(jnp.bfloat16)


def solution(mesh):
    size = dict(mesh.shape)
    direct = size["ctx"] == 4 and size["head"] == 2 and size["sec"] == 2
    return jax.shard_map(
        direct_body if direct else general_body,
        mesh=mesh,
        in_specs=(
            P(("groups", "ctx"), ("head", "sec")),
            P(("groups", "ctx"), ("head", "sec")),
            P(("groups", "ctx"), ("head", "sec")),
            P("groups", None),
            P(("groups", "head", "sec"), "ctx"),
            P(("head", "sec"), "ctx"),
            P(),
            P(("head", "sec"), "ctx"),
            P(("head", "sec"), "ctx"),
            P("ctx", ("head", "sec")),
        ),
        out_specs=P(("groups", "ctx"), ("head", "sec")),
        check_vma=False,
    )
```

```python
import functools
import math

import jax
import jax.numpy as jnp
from jax import lax
from jax.experimental import pallas as pl
from jax.experimental.pallas import tpu as pltpu
from jax.sharding import PartitionSpec as P


HQ = 64
KVH = 8
DH = 128
KB = 128
MOST = 4
LANES = 128
EPS = 1e-05
ALL = ("ctx", "head", "sec")


VM = pl.BlockSpec(memory_space=pltpu.VMEM)
SM = pl.BlockSpec(memory_space=pltpu.SMEM)
ANY = pl.BlockSpec(memory_space=pl.ANY)
F32 = jnp.float32
BF16 = jnp.bfloat16


def struct(shape, dtype):
    return jax.ShapeDtypeStruct(shape, dtype)


def call(kernel, out, in_specs, args, cost=3, scratch=(), vmem=8):
    outs = out if isinstance(out, (tuple, list)) else (out,)
    nbytes = sum(math.prod(a.shape) * a.dtype.itemsize for a in args)
    nbytes += sum(math.prod(o.shape) * o.dtype.itemsize for o in outs)
    return pl.pallas_call(
        kernel,
        out_shape=out,
        in_specs=in_specs,
        out_specs=jax.tree.map(lambda _: VM, out),
        scratch_shapes=scratch,
        compiler_params=pltpu.CompilerParams(vmem_limit_bytes=vmem << 20),
        cost_estimate=pl.CostEstimate(flops=cost * 10**9, bytes_accessed=nbytes, transcendentals=0),
    )(*args)


def in_vmem(x):
    return pltpu.with_memory_space_constraint(x, pltpu.VMEM)


def in_hbm(x):
    return pltpu.with_memory_space_constraint(x, pltpu.HBM)


def slots(index_ref, blocks):
    entries = index_ref.shape[1]
    base = lax.axis_index("ctx") * blocks
    first = jnp.int32(0)
    end = jnp.int32(0)
    for n in range(entries):
        block = index_ref[0, n]
        first += (block < base).astype(jnp.int32)
        end += (block < base + blocks).astype(jnp.int32)
    found = []
    for slot in range(MOST):
        entry = jnp.minimum(first + slot, entries - 1)
        local = jnp.clip(index_ref[0, entry] - base, 0, blocks - 1)
        found.append((local, first + slot < end))
    return found


def attend(offset, first_token, start_ref, q_ref, key_ref, value_ref, out_ref, score_ref, weight_ref):
    rows = q_ref.shape[0]
    heads = q_ref.shape[1] // DH
    kv_dev = key_ref.shape[1] // DH
    group = heads // kv_dev
    scale = 1.0 / math.sqrt(DH)
    token0 = first_token + (lax.axis_index("ctx") ^ offset) * rows
    ahead = (
        lax.broadcasted_iota(jnp.int32, (rows, KB), 1)
        - lax.broadcasted_iota(jnp.int32, (rows, KB), 0)
        - token0
    )
    allowed = [ahead + start_ref[slot : slot + 1, :] <= 0 for slot in range(MOST)]
    head_lane = lax.broadcasted_iota(jnp.int32, (rows, LANES), 1)
    peak_tile = jnp.zeros((rows, LANES), F32)
    total_tile = jnp.ones((rows, LANES), F32)
    for kv in range(kv_dev):
        stacked = jnp.concatenate(
            [q_ref[:, (kv * group + h) * DH : (kv * group + h + 1) * DH] for h in range(group)], axis=0
        )
        score_ref[kv] = lax.dot_general(
            stacked,
            key_ref[:, kv * DH : (kv + 1) * DH],
            (((1,), (1,)), ((), ())),
            preferred_element_type=F32,
        )
    for kv in range(kv_dev):
        for h in range(group):
            head = kv * group + h
            span = slice(h * rows, (h + 1) * rows)
            parts = [
                jnp.where(allowed[slot], score_ref[kv, span, slot * KB : (slot + 1) * KB], -1e30)
                for slot in range(MOST)
            ]
            peak = jnp.max(functools.reduce(jnp.maximum, parts), axis=1, keepdims=True)
            parts = [jnp.exp((p - peak) * scale) for p in parts]
            row_total = jnp.sum(functools.reduce(jnp.add, parts), axis=1, keepdims=True)
            for slot, p in enumerate(parts):
                weight_ref[kv, span, slot * KB : (slot + 1) * KB] = p.astype(BF16)
            peak_tile = jnp.where(head_lane == head, peak, peak_tile)
            total_tile = jnp.where(head_lane == head, row_total, total_tile)
    inverse = 1.0 / total_tile
    for kv in range(kv_dev):
        mixture = jnp.dot(
            weight_ref[kv], value_ref[:, kv * DH : (kv + 1) * DH], preferred_element_type=F32
        )
        for h in range(group):
            head = kv * group + h
            out_ref[:, head * DH : (head + 1) * DH] = (
                mixture[h * rows : (h + 1) * rows] * inverse[:, head : head + 1]
            ).astype(BF16)
    lse_tile = peak_tile * scale + jnp.log(total_tile)
    high = lse_tile.astype(BF16).astype(F32)
    rest = lse_tile - high
    mid = rest.astype(BF16).astype(F32)
    low = rest - mid
    tile = high + pltpu.roll(mid, heads, 1) + pltpu.roll(low, 2 * heads, 1)
    out_ref[:, heads * DH :] = tile.astype(BF16)


def first_attend_kernel(
    blocks, first_token, index_ref, q_hbm, key_hbm, value_hbm,
    key_ref, value_ref, start_ref, out_ref, q_ref, score_ref, weight_ref, sems, q_sem,
):
    copies = [pltpu.make_async_copy(q_hbm, q_ref, q_sem)]
    found = slots(index_ref, blocks)
    for slot, (local, _) in enumerate(found):
        rows = pl.ds(pl.multiple_of(local * KB, KB), KB)
        for n, (src, dst) in enumerate(((key_hbm, key_ref), (value_hbm, value_ref))):
            copies.append(
                pltpu.make_async_copy(
                    src.at[rows, :], dst.at[slot * KB : (slot + 1) * KB, :], sems.at[n, slot]
                )
            )
    for copy in copies:
        copy.start()
    row = lax.broadcasted_iota(jnp.int32, start_ref.shape, 0)
    starts = jnp.zeros(start_ref.shape, jnp.int32)
    base = lax.axis_index("ctx") * blocks
    for slot, (local, valid) in enumerate(found):
        starts = jnp.where(row == slot, jnp.where(valid, (base + local) * KB, jnp.int32(1 << 29)), starts)
    start_ref[...] = starts
    for copy in copies:
        copy.wait()
    attend(0, first_token, start_ref, q_ref, key_ref, value_ref, out_ref, score_ref, weight_ref)


def blend_kernel(*refs):
    out_ref = refs[-1]
    parts = refs[:-1]
    heads = out_ref.shape[1] // DH
    logs = []
    for part in parts:
        tile = part[:, heads * DH :].astype(F32)
        logs.append(
            tile + pltpu.roll(tile, LANES - heads, 1) + pltpu.roll(tile, LANES - 2 * heads, 1)
        )
    peak = functools.reduce(jnp.maximum, logs)
    shares = [jnp.exp(log - peak) for log in logs]
    total = functools.reduce(jnp.add, shares)
    shares = [share / total for share in shares]
    for head in range(heads):
        span = slice(head * DH, (head + 1) * DH)
        out_ref[:, span] = functools.reduce(
            jnp.add,
            [share[:, head : head + 1] * part[:, span].astype(F32) for share, part in zip(shares, parts)],
        ).astype(BF16)


def place():
    return lax.axis_index("head") * lax.axis_size("sec") + lax.axis_index("sec")


def place_of(n, rows, count):
    n_sec = lax.axis_size("sec")
    owner = lax.axis_index("ctx") ^ n
    other = ((owner % n_sec) != lax.axis_index("sec")).astype(jnp.int32)
    return pl.multiple_of(other * (count // n_sec * rows) + owner // n_sec * rows, rows)


def product(rows_ref, weight_ref, source, keep_ref, send_ref, target, width, tile):
    half = rows_ref.shape[0] // 2
    for at in range(0, width, tile):
        size = min(tile, width - at)
        part = jnp.dot(
            rows_ref[...],
            weight_ref[:, source + at : source + at + size],
            preferred_element_type=F32,
        )
        keep_ref[:, target + at : target + at + size] = part[:half]
        send_ref[:, target + at : target + at + size] = part[half:].astype(BF16)


def project_kernel(tile, *refs):
    pieces, (weight_ref, keep_ref, send_ref, rows_ref) = refs[:-4], refs[-4:]
    rows = pieces[0].shape[0]
    for n, piece in enumerate(pieces):
        rows_ref[pl.ds(place_of(n, rows, len(pieces)), rows), :] = piece[...]
    product(rows_ref, weight_ref, 0, keep_ref, send_ref, 0, weight_ref.shape[1], tile)


def fold_kernel(width, keep_ref, got_ref, keep_out, send_out):
    rows = keep_out.shape[0]
    head = lax.axis_index("head")
    mine = pl.ds(pl.multiple_of(head * rows, rows), rows)
    other = pl.ds(pl.multiple_of((1 - head) * rows, rows), rows)
    keep_out[:, :width] = keep_ref[mine, :width] + got_ref[mine, :width].astype(F32)
    send_out[:, :width] = (keep_ref[other, :width] + got_ref[other, :width].astype(F32)).astype(BF16)
    if keep_ref.shape[1] > width:
        keep_out[:, width:] = keep_ref[mine, width:] + take_exact(got_ref[mine, width:])
        put_exact(send_out, slice(None), width, keep_ref[other, width:] + take_exact(got_ref[other, width:]))


def middle_kernel(stream_ref, keep_ref, got_ref, out_ref):
    out_ref[...] = (
        stream_ref[...].astype(F32) + (keep_ref[...] + got_ref[...].astype(F32))
    ).astype(BF16)


def put_exact(ref, rows, at, value):
    high = value.astype(BF16)
    ref[rows, at : at + LANES] = high
    ref[rows, at + LANES : at + 2 * LANES] = (value - high.astype(F32)).astype(BF16)


def take_exact(tile):
    return tile[:, :LANES].astype(F32) + tile[:, LANES:].astype(F32)


def prepare_kernel(piece_ref, gain_ref, row_ref, square_ref):
    model = piece_ref.shape[1]
    gain = gain_ref[:, pl.ds(pl.multiple_of(place() * model, model), model)]
    wide = piece_ref[...].astype(F32)
    row_ref[...] = (wide * gain).astype(BF16)
    square_ref[...] = jnp.broadcast_to(jnp.sum(wide * wide, axis=1, keepdims=True), square_ref.shape)


def first_gate_kernel(width, tile, *refs):
    pieces, squares = refs[:4], refs[4:8]
    gate_ref, up_ref, keep_ref, send_ref, rows_ref = refs[8:]
    rows = pieces[0].shape[0]
    half = rows_ref.shape[0] // 2
    for n, (piece, square) in enumerate(zip(pieces, squares)):
        at = place_of(n, rows, len(pieces))
        rows_ref[pl.ds(at, rows), :] = piece[...]

        @pl.when(at < half)
        def _():
            keep_ref[pl.ds(at, rows), 2 * width :] = square[...]

        @pl.when(at >= half)
        def _():
            put_exact(send_ref, pl.ds(pl.multiple_of(at - half, rows), rows), 2 * width, square[...])

    product(rows_ref, gate_ref, 0, keep_ref, send_ref, 0, width, tile)
    product(rows_ref, up_ref, 0, keep_ref, send_ref, width, width, tile)


def gate_kernel(start, width, tile, rows_ref, gate_ref, up_ref, keep_ref, send_ref):
    product(rows_ref, gate_ref, start, keep_ref, send_ref, 0, width, tile)
    product(rows_ref, up_ref, start, keep_ref, send_ref, width, width, tile)


def scale_kernel(model, keep_ref, got_ref, out_ref):
    at = keep_ref.shape[1] - LANES
    square = keep_ref[:, at:] + take_exact(got_ref[:, at:])
    out_ref[...] = lax.rsqrt(square / model + EPS)


def hidden_kernel(scale_ref, keep_ref, got_ref, out_ref):
    width = out_ref.shape[1]
    scale = scale_ref[...]
    for at in range(0, width, LANES):
        gate = keep_ref[:, at : at + LANES] + got_ref[:, at : at + LANES].astype(F32)
        up = keep_ref[:, width + at : width + at + LANES] + got_ref[
            :, width + at : width + at + LANES
        ].astype(F32)
        gate = gate * scale
        out_ref[:, at : at + LANES] = (
            gate / (1.0 + jnp.exp(-gate)) * (up * scale)
        ).astype(BF16)


def first_hidden_kernel(model, keep_ref, got_ref, out_ref, scale_ref):
    scale_kernel(model, keep_ref, got_ref, scale_ref)
    hidden_kernel(scale_ref, keep_ref, got_ref, out_ref)


def gather_rows(pieces, rows_ref):
    rows = pieces[0].shape[0]
    for n, piece in enumerate(pieces):
        at = pl.ds(pl.multiple_of((lax.axis_index("ctx") ^ place() ^ n) * rows, rows), rows)
        rows_ref[at, :] = piece[...]


def first_down_kernel(tile, *refs):
    pieces, (weight_ref, out_ref, rows_ref) = refs[:4], refs[4:]
    gather_rows(pieces, rows_ref)
    depth = rows_ref.shape[1]
    for at in range(0, weight_ref.shape[1], tile):
        out_ref[:, at : at + tile] = jnp.dot(
            rows_ref[...], weight_ref[:depth, at : at + tile], preferred_element_type=F32
        )


def down_kernel(tile, *refs):
    pieces, (weight_ref, so_far_ref, own_ref) = refs[:4], refs[4:7]
    sends, rows_ref = refs[7:-1], refs[-1]
    gather_rows(pieces, rows_ref)
    rows = pieces[0].shape[0]
    depth = rows_ref.shape[1]
    start = weight_ref.shape[0] - depth
    for at in range(0, weight_ref.shape[1], tile):
        columns = slice(at, at + tile)
        part = so_far_ref[:, columns] + jnp.dot(
            rows_ref[...], weight_ref[start:, columns], preferred_element_type=F32
        )
        own_ref[:, columns] = part[:rows]
        for n, send in enumerate(sends):
            send[:, columns] = part[(n + 1) * rows : (n + 2) * rows].astype(BF16)


def final_kernel(middle_ref, own_ref, *refs):
    parts, out_ref = refs[:-1], refs[-1]
    total = own_ref[...]
    for part in parts:
        total = total + part[...].astype(F32)
    out_ref[...] = (middle_ref[...].astype(F32) + total).astype(BF16)


def swap(x, axis):
    return lax.ppermute(x, axis, [(0, 1), (1, 0)])


def turn(x, axis, n, offset):
    return lax.ppermute(x, axis, [(i, i ^ offset) for i in range(n)])


def direct_body(
    queries,
    key_cache,
    value_cache,
    block_index,
    stream,
    out_weight,
    norm_gain,
    gate_weight,
    up_weight,
    down_weight,
):
    n_context, n_head, _ = (lax.axis_size(a) for a in ALL)
    rows, heads_width = queries.shape
    context_len = key_cache.shape[0] * n_context
    model = norm_gain.shape[0]
    total = rows * n_context
    blocks = key_cache.shape[0] // KB
    kv_width = key_cache.shape[1]
    order = (3, 2, 1)

    got_q = {m: turn(queries, "ctx", n_context, m) for m in (2, 1)}
    got_q[3] = turn(got_q[2], "ctx", n_context, 1)
    picked = struct((MOST * KB, kv_width), BF16)
    partial_out = struct((rows, heads_width + LANES), BF16)
    kv_dev = kv_width // DH
    tall = heads_width // kv_width * rows
    scratch = [
        pltpu.VMEM((kv_dev, tall, MOST * KB), F32),
        pltpu.VMEM((kv_dev, tall, MOST * KB), BF16),
    ]
    keys, values, starts, own_partial = call(
        functools.partial(first_attend_kernel, blocks, context_len - total),
        (picked, picked, struct((8, LANES), jnp.int32), partial_out),
        [SM, ANY, ANY, ANY],
        (block_index, in_hbm(queries), in_hbm(key_cache), in_hbm(value_cache)),
        scratch=[pltpu.VMEM((rows, heads_width), BF16)]
        + scratch
        + [pltpu.SemaphoreType.DMA((2, MOST)), pltpu.SemaphoreType.DMA],
    )
    partial = {0: own_partial}
    for m in order:
        partial[m] = call(
            functools.partial(attend, m, context_len - total),
            partial_out,
            [VM] * 4,
            (starts, got_q[m], keys, values),
            scratch=scratch,
        )
    back = {m: turn(partial[m], "ctx", n_context, m) for m in order}
    back[0] = partial[0]
    blended = call(
        blend_kernel, struct((rows, heads_width), BF16), [VM] * 4, tuple(back[m] for m in range(4))
    )

    attention = {m: turn(blended, "ctx", n_context, m) for m in order}
    attention[0] = blended
    width = out_weight.shape[1]
    keep, away = call(
        functools.partial(project_kernel, 512),
        (struct((n_head * rows, width), F32), struct((n_head * rows, width), BF16)),
        [VM] * 5,
        tuple(attention[m] for m in range(4)) + (in_vmem(out_weight),),
        scratch=[pltpu.VMEM((total, heads_width), BF16)],
        cost=6,
    )
    got = swap(away, "sec")
    keep, away = call(
        functools.partial(fold_kernel, width),
        (struct((rows, width), F32), struct((rows, width), BF16)),
        [VM, VM],
        (keep, got),
        cost=6,
    )
    got = swap(away, "head")
    middle = call(middle_kernel, struct((rows, width), BF16), [VM] * 3, (stream, keep, got), cost=6)

    all_middle = {
        m: lax.ppermute(
            middle,
            ALL,
            [
                (a * n_context + b, (b ^ m) * n_context + a)
                for a in range(n_context)
                for b in range(n_context)
            ],
        )
        for m in (3, 0, 1, 2)
    }
    hidden_width = gate_weight.shape[1]
    first = hidden_width // 2 // LANES * LANES
    chunks = ((0, first), (first, hidden_width - first))
    hidden = []
    gate_vmem, up_vmem = in_vmem(gate_weight), in_vmem(up_weight)
    prepared = [
        call(
            prepare_kernel,
            (struct((rows, width), BF16), struct((rows, LANES), F32)),
            [VM, VM],
            (all_middle[m], norm_gain[None]),
            cost=0,
        )
        for m in range(4)
    ]
    scale = None
    for c, (start, chunk) in enumerate(chunks):
        extra = LANES if c == 0 else 0
        out = (
            struct((n_head * rows, 2 * chunk + extra), F32),
            struct((n_head * rows, 2 * chunk + 2 * extra), BF16),
        )
        if c == 0:
            keep, away, all_rows = call(
                functools.partial(first_gate_kernel, chunk, 512),
                out + (struct((total, width), BF16),),
                [VM] * 10,
                tuple(p[0] for p in prepared)
                + tuple(p[1] for p in prepared)
                + (gate_vmem, up_vmem),
            )
        else:
            keep, away = call(
                functools.partial(gate_kernel, start, chunk, 512),
                out,
                [VM] * 3,
                (all_rows, gate_vmem, up_vmem),
            )
        keep, away = call(
            functools.partial(fold_kernel, 2 * chunk),
            (
                struct((rows, 2 * chunk + extra), F32),
                struct((rows, 2 * chunk + 2 * extra), BF16),
            ),
            [VM, VM],
            (keep, swap(away, "sec")),
        )
        got = swap(away, "head")
        if c == 0:
            own, scale = call(
                functools.partial(first_hidden_kernel, model),
                (struct((rows, chunk), BF16), struct((rows, LANES), F32)),
                [VM] * 2,
                (keep, got),
            )
        else:
            own = call(hidden_kernel, struct((rows, chunk), BF16), [VM] * 3, (scale, keep, got))
        across = swap(own, "head")
        beside = swap(own, "sec")
        hidden.append((own, beside, across, swap(across, "sec")))
    out_width = down_weight.shape[1]
    down_vmem = in_vmem(down_weight)
    so_far = call(
        functools.partial(first_down_kernel, 512),
        struct((total, out_width), F32),
        [VM] * 5,
        hidden[0] + (down_vmem,),
        scratch=[pltpu.VMEM((total, chunks[0][1]), BF16)],
    )
    res = call(
        functools.partial(down_kernel, 512),
        (struct((rows, out_width), F32),) + (struct((rows, out_width), BF16),) * 3,
        [VM] * 6,
        hidden[1] + (down_vmem, so_far),
        scratch=[pltpu.VMEM((total, chunks[1][1]), BF16)],
    )
    parts = [turn(res[m], "ctx", n_context, m) for m in order]
    return call(
        final_kernel, struct((rows, out_width), BF16), [VM] * 5, (all_middle[0], res[0]) + tuple(parts)
    )


def local_attention(gathered, key_cache, value_cache, block_index, context_index, context_len):
    group_size = HQ // KVH
    kv_dev = key_cache.shape[1] // DH
    blocks_dev = key_cache.shape[0] // KB
    total_tokens = gathered.shape[0]
    key_blocks = key_cache.reshape(blocks_dev, KB, kv_dev, DH)
    value_blocks = value_cache.reshape(blocks_dev, KB, kv_dev, DH)
    local_ids = context_index * blocks_dev + jnp.arange(blocks_dev, dtype=jnp.int32)
    member = jnp.any(block_index[:, :, None] == local_ids[None, None, :], axis=1)
    member_rank = jnp.cumsum(member.astype(jnp.int32), axis=1) - 1
    slot_hit = member[:, None, :] & (
        member_rank[:, None, :] == jnp.arange(MOST, dtype=jnp.int32)[None, :, None]
    )
    slot_block = jnp.sum(
        jnp.where(slot_hit, jnp.arange(blocks_dev, dtype=jnp.int32)[None, None, :], 0), axis=2
    )
    slot_valid = jnp.any(slot_hit, axis=2)
    picked_keys = jnp.take(key_blocks, slot_block[0], axis=0).reshape(MOST * KB, kv_dev, DH)
    picked_values = jnp.take(value_blocks, slot_block[0], axis=0).reshape(MOST * KB, kv_dev, DH)
    key_pos = (
        (local_ids[0] + slot_block[0])[:, None] * KB + jnp.arange(KB, dtype=jnp.int32)[None, :]
    ).reshape(-1)
    live_keys = jnp.broadcast_to(slot_valid[0][:, None], (MOST, KB)).reshape(-1)
    query_pos = context_len - total_tokens + jnp.arange(KB, dtype=jnp.int32)
    allowed = live_keys[None, :] & (key_pos[None, :] <= query_pos[:, None])
    query_block = gathered.reshape(KB, kv_dev, group_size, DH)
    scores = jnp.einsum(
        "qhgd,phd->hgqp", query_block, picked_keys, preferred_element_type=jnp.float32
    ) / math.sqrt(DH)
    scores = jnp.where(allowed[None, None], scores, -jnp.inf)
    peak_score = jnp.max(scores, axis=-1, keepdims=True)
    unnormed = jnp.exp(scores - peak_score)
    row_total = jnp.sum(unnormed, axis=-1)
    mixture = jnp.einsum(
        "hgqp,phd->qhgd",
        unnormed.astype(jnp.bfloat16),
        picked_values,
        preferred_element_type=jnp.float32,
    )
    result = mixture / jnp.transpose(row_total, (2, 0, 1))[..., None]
    log_total = jnp.transpose(peak_score[..., 0] + jnp.log(row_total), (2, 0, 1))
    out_list = result.reshape(KB, -1)
    lse_list = log_total.reshape(KB, -1)
    return (out_list, lse_list)


def general_body(
    queries,
    key_cache,
    value_cache,
    block_index,
    stream,
    out_weight,
    norm_gain,
    gate_weight,
    up_weight,
    down_weight,
):
    n_context = lax.axis_size("ctx")
    context_index = lax.axis_index("ctx")
    context_len = key_cache.shape[0] * n_context
    gathered = lax.all_gather(queries, "ctx", axis=0, tiled=True)
    part_out, part_lse = local_attention(
        gathered, key_cache, value_cache, block_index, context_index, context_len
    )
    spread_out, spread_lse = (
        lax.all_to_all(part_out[:, None, :], "ctx", split_axis=0, concat_axis=1, tiled=True),
        lax.all_to_all(part_lse[:, None, :], "ctx", split_axis=0, concat_axis=1, tiled=True),
    )
    share_rows = spread_out.shape[0]
    head_count = spread_lse.shape[2]
    peak_value = jnp.max(spread_lse, axis=1, keepdims=True)
    share_weight = jnp.exp(spread_lse - peak_value)
    blended = jnp.sum(
        spread_out.reshape(share_rows, n_context, head_count, -1) * share_weight[..., None], axis=1
    )
    blended = blended / jnp.sum(share_weight, axis=1)[..., None]
    attention = lax.all_gather(
        blended.reshape(share_rows, -1).astype(jnp.bfloat16), "ctx", axis=0, tiled=True
    )
    row_piece = attention
    projected = lax.psum_scatter(
        jnp.dot(row_piece, out_weight, preferred_element_type=jnp.float32),
        ("head", "sec"),
        scatter_dimension=0,
        tiled=True,
    )
    middle = (stream.astype(jnp.float32) + projected).astype(jnp.bfloat16)
    full_middle = lax.all_gather(middle, "ctx", axis=1, tiled=True)
    middle_wide = full_middle.astype(jnp.float32)
    mean_square = jnp.mean(middle_wide * middle_wide, axis=-1, keepdims=True)
    normed = (middle_wide * lax.rsqrt(mean_square + 1e-05) * norm_gain).astype(jnp.bfloat16)
    normed_cols, middle_cols = (
        lax.all_to_all(normed, ("head", "sec"), split_axis=1, concat_axis=0, tiled=True),
        lax.all_to_all(full_middle, ("head", "sec"), split_axis=1, concat_axis=0, tiled=True),
    )
    row_piece = normed_cols
    gate_up = lax.psum_scatter(
        jnp.concatenate(
            [
                jnp.dot(row_piece, gate_weight, preferred_element_type=jnp.float32),
                jnp.dot(row_piece, up_weight, preferred_element_type=jnp.float32),
            ],
            axis=1,
        ),
        ("head", "sec"),
        scatter_dimension=0,
        tiled=True,
    )
    hidden_width = gate_weight.shape[1]
    hidden = (jax.nn.silu(gate_up[:, :hidden_width]) * gate_up[:, hidden_width:]).astype(
        jnp.bfloat16
    )
    all_hidden = lax.all_gather(hidden, ("head", "sec"), axis=0, tiled=True)
    row_piece = all_hidden
    down_part = lax.psum_scatter(
        jnp.dot(row_piece, down_weight, preferred_element_type=jnp.float32),
        "ctx",
        scatter_dimension=0,
        tiled=True,
    )
    own_middle = lax.dynamic_slice_in_dim(
        middle_cols, context_index * down_part.shape[0], down_part.shape[0], 0
    )
    return (own_middle.astype(jnp.float32) + down_part).astype(jnp.bfloat16)


def solution(mesh):
    size = dict(mesh.shape)
    direct = size["ctx"] == 4 and size["head"] == 2 and size["sec"] == 2
    return jax.shard_map(
        direct_body if direct else general_body,
        mesh=mesh,
        in_specs=(
            P(("groups", "ctx"), ("head", "sec")),
            P(("groups", "ctx"), ("head", "sec")),
            P(("groups", "ctx"), ("head", "sec")),
            P("groups", None),
            P(("groups", "head", "sec"), "ctx"),
            P(("head", "sec"), "ctx"),
            P(),
            P(("head", "sec"), "ctx"),
            P(("head", "sec"), "ctx"),
            P("ctx", ("head", "sec")),
        ),
        out_specs=P(("groups", "ctx"), ("head", "sec")),
        check_vma=False,
    )
```

```python
import functools
import math

import jax
import jax.numpy as jnp
from jax import lax
from jax.experimental import pallas as pl
from jax.experimental.pallas import tpu as pltpu
from jax.sharding import PartitionSpec as P


HQ = 64
KVH = 8
DH = 128
KB = 128
MOST = 4
LANES = 128
EPS = 1e-05
ALL = ("ctx", "head", "sec")


VM = pl.BlockSpec(memory_space=pltpu.VMEM)
SM = pl.BlockSpec(memory_space=pltpu.SMEM)
ANY = pl.BlockSpec(memory_space=pl.ANY)
F32 = jnp.float32
BF16 = jnp.bfloat16


def struct(shape, dtype):
    return jax.ShapeDtypeStruct(shape, dtype)


def call(kernel, out, in_specs, args, cost=3, scratch=(), vmem=8):
    outs = out if isinstance(out, (tuple, list)) else (out,)
    nbytes = sum(math.prod(a.shape) * a.dtype.itemsize for a in args)
    nbytes += sum(math.prod(o.shape) * o.dtype.itemsize for o in outs)
    return pl.pallas_call(
        kernel,
        out_shape=out,
        in_specs=in_specs,
        out_specs=jax.tree.map(lambda _: VM, out),
        scratch_shapes=scratch,
        compiler_params=pltpu.CompilerParams(vmem_limit_bytes=vmem << 20),
        cost_estimate=pl.CostEstimate(flops=cost * 10**9, bytes_accessed=nbytes, transcendentals=0),
    )(*args)


def in_vmem(x):
    return pltpu.with_memory_space_constraint(x, pltpu.VMEM)


def in_hbm(x):
    return pltpu.with_memory_space_constraint(x, pltpu.HBM)


def slots(index_ref, blocks):
    entries = index_ref.shape[1]
    base = lax.axis_index("ctx") * blocks
    first = jnp.int32(0)
    end = jnp.int32(0)
    for n in range(entries):
        block = index_ref[0, n]
        first += (block < base).astype(jnp.int32)
        end += (block < base + blocks).astype(jnp.int32)
    found = []
    for slot in range(MOST):
        entry = jnp.minimum(first + slot, entries - 1)
        local = jnp.clip(index_ref[0, entry] - base, 0, blocks - 1)
        found.append((local, first + slot < end))
    return found


def attend(offset, first_token, start_ref, q_ref, key_ref, value_ref, out_ref, score_ref, weight_ref):
    rows = q_ref.shape[0]
    heads = q_ref.shape[1] // DH
    kv_dev = key_ref.shape[1] // DH
    group = heads // kv_dev
    scale = 1.0 / math.sqrt(DH)
    token0 = first_token + (lax.axis_index("ctx") ^ offset) * rows
    ahead = (
        lax.broadcasted_iota(jnp.int32, (rows, KB), 1)
        - lax.broadcasted_iota(jnp.int32, (rows, KB), 0)
        - token0
    )
    allowed = [ahead + start_ref[slot : slot + 1, :] <= 0 for slot in range(MOST)]
    head_lane = lax.broadcasted_iota(jnp.int32, (rows, LANES), 1)
    peak_tile = jnp.zeros((rows, LANES), F32)
    total_tile = jnp.ones((rows, LANES), F32)
    for kv in range(kv_dev):
        stacked = jnp.concatenate(
            [q_ref[:, (kv * group + h) * DH : (kv * group + h + 1) * DH] for h in range(group)], axis=0
        )
        score_ref[kv] = lax.dot_general(
            stacked,
            key_ref[:, kv * DH : (kv + 1) * DH],
            (((1,), (1,)), ((), ())),
            preferred_element_type=F32,
        )
    for kv in range(kv_dev):
        for h in range(group):
            head = kv * group + h
            span = slice(h * rows, (h + 1) * rows)
            parts = [
                jnp.where(allowed[slot], score_ref[kv, span, slot * KB : (slot + 1) * KB], -1e30)
                for slot in range(MOST)
            ]
            peak = jnp.max(functools.reduce(jnp.maximum, parts), axis=1, keepdims=True)
            parts = [jnp.exp((p - peak) * scale) for p in parts]
            row_total = jnp.sum(functools.reduce(jnp.add, parts), axis=1, keepdims=True)
            for slot, p in enumerate(parts):
                weight_ref[kv, span, slot * KB : (slot + 1) * KB] = p.astype(BF16)
            peak_tile = jnp.where(head_lane == head, peak, peak_tile)
            total_tile = jnp.where(head_lane == head, row_total, total_tile)
    inverse = 1.0 / total_tile
    for kv in range(kv_dev):
        mixture = jnp.dot(
            weight_ref[kv], value_ref[:, kv * DH : (kv + 1) * DH], preferred_element_type=F32
        )
        for h in range(group):
            head = kv * group + h
            out_ref[:, head * DH : (head + 1) * DH] = (
                mixture[h * rows : (h + 1) * rows] * inverse[:, head : head + 1]
            ).astype(BF16)
    lse_tile = peak_tile * scale + jnp.log(total_tile)
    high = lse_tile.astype(BF16).astype(F32)
    rest = lse_tile - high
    mid = rest.astype(BF16).astype(F32)
    low = rest - mid
    tile = high + pltpu.roll(mid, heads, 1) + pltpu.roll(low, 2 * heads, 1)
    out_ref[:, heads * DH :] = tile.astype(BF16)


def first_attend_kernel(
    blocks, first_token, index_ref, q_hbm, key_hbm, value_hbm,
    key_ref, value_ref, start_ref, out_ref, q_ref, score_ref, weight_ref, sems, q_sem,
):
    copies = [pltpu.make_async_copy(q_hbm, q_ref, q_sem)]
    found = slots(index_ref, blocks)
    for slot, (local, _) in enumerate(found):
        rows = pl.ds(pl.multiple_of(local * KB, KB), KB)
        for n, (src, dst) in enumerate(((key_hbm, key_ref), (value_hbm, value_ref))):
            copies.append(
                pltpu.make_async_copy(
                    src.at[rows, :], dst.at[slot * KB : (slot + 1) * KB, :], sems.at[n, slot]
                )
            )
    for copy in copies:
        copy.start()
    row = lax.broadcasted_iota(jnp.int32, start_ref.shape, 0)
    starts = jnp.zeros(start_ref.shape, jnp.int32)
    base = lax.axis_index("ctx") * blocks
    for slot, (local, valid) in enumerate(found):
        starts = jnp.where(row == slot, jnp.where(valid, (base + local) * KB, jnp.int32(1 << 29)), starts)
    start_ref[...] = starts
    for copy in copies:
        copy.wait()
    attend(0, first_token, start_ref, q_ref, key_ref, value_ref, out_ref, score_ref, weight_ref)


def blend_kernel(*refs):
    out_ref = refs[-1]
    parts = refs[:-1]
    heads = out_ref.shape[1] // DH
    logs = []
    for part in parts:
        tile = part[:, heads * DH :].astype(F32)
        logs.append(
            tile + pltpu.roll(tile, LANES - heads, 1) + pltpu.roll(tile, LANES - 2 * heads, 1)
        )
    peak = functools.reduce(jnp.maximum, logs)
    shares = [jnp.exp(log - peak) for log in logs]
    total = functools.reduce(jnp.add, shares)
    shares = [share / total for share in shares]
    for head in range(heads):
        span = slice(head * DH, (head + 1) * DH)
        out_ref[:, span] = functools.reduce(
            jnp.add,
            [share[:, head : head + 1] * part[:, span].astype(F32) for share, part in zip(shares, parts)],
        ).astype(BF16)


def place():
    return lax.axis_index("head") * lax.axis_size("sec") + lax.axis_index("sec")


def place_of(n, rows, count):
    n_sec = lax.axis_size("sec")
    owner = lax.axis_index("ctx") ^ n
    other = ((owner % n_sec) != lax.axis_index("sec")).astype(jnp.int32)
    return pl.multiple_of(other * (count // n_sec * rows) + owner // n_sec * rows, rows)


def product(rows_ref, weight_ref, source, keep_ref, send_ref, target, width, tile):
    half = rows_ref.shape[0] // 2
    for at in range(0, width, tile):
        size = min(tile, width - at)
        part = jnp.dot(
            rows_ref[...],
            weight_ref[:, source + at : source + at + size],
            preferred_element_type=F32,
        )
        keep_ref[:, target + at : target + at + size] = part[:half]
        send_ref[:, target + at : target + at + size] = part[half:].astype(BF16)


def project_kernel(tile, *refs):
    pieces, (weight_ref, keep_ref, send_ref, rows_ref) = refs[:-4], refs[-4:]
    rows = pieces[0].shape[0]
    for n, piece in enumerate(pieces):
        rows_ref[pl.ds(place_of(n, rows, len(pieces)), rows), :] = piece[...]
    product(rows_ref, weight_ref, 0, keep_ref, send_ref, 0, weight_ref.shape[1], tile)


def fold_kernel(width, keep_ref, got_ref, keep_out, send_out):
    rows = keep_out.shape[0]
    head = lax.axis_index("head")
    mine = pl.ds(pl.multiple_of(head * rows, rows), rows)
    other = pl.ds(pl.multiple_of((1 - head) * rows, rows), rows)
    keep_out[:, :width] = keep_ref[mine, :width] + got_ref[mine, :width].astype(F32)
    send_out[:, :width] = (keep_ref[other, :width] + got_ref[other, :width].astype(F32)).astype(BF16)
    if keep_ref.shape[1] > width:
        keep_out[:, width:] = keep_ref[mine, width:] + take_exact(got_ref[mine, width:])
        put_exact(send_out, slice(None), width, keep_ref[other, width:] + take_exact(got_ref[other, width:]))


def middle_kernel(stream_ref, keep_ref, got_ref, out_ref):
    out_ref[...] = (
        stream_ref[...].astype(F32) + (keep_ref[...] + got_ref[...].astype(F32))
    ).astype(BF16)


def put_exact(ref, rows, at, value):
    high = value.astype(BF16)
    ref[rows, at : at + LANES] = high
    ref[rows, at + LANES : at + 2 * LANES] = (value - high.astype(F32)).astype(BF16)


def take_exact(tile):
    return tile[:, :LANES].astype(F32) + tile[:, LANES:].astype(F32)


def prepare_kernel(piece_ref, gain_ref, row_ref, square_ref):
    model = piece_ref.shape[1]
    gain = gain_ref[:, pl.ds(pl.multiple_of(place() * model, model), model)]
    wide = piece_ref[...].astype(F32)
    row_ref[...] = (wide * gain).astype(BF16)
    square_ref[...] = jnp.broadcast_to(jnp.sum(wide * wide, axis=1, keepdims=True), square_ref.shape)


def first_gate_kernel(width, tile, *refs):
    pieces, squares = refs[:4], refs[4:8]
    gate_ref, up_ref, keep_ref, send_ref, rows_ref = refs[8:]
    rows = pieces[0].shape[0]
    half = rows_ref.shape[0] // 2
    for n, (piece, square) in enumerate(zip(pieces, squares)):
        at = place_of(n, rows, len(pieces))
        rows_ref[pl.ds(at, rows), :] = piece[...]

        @pl.when(at < half)
        def _():
            keep_ref[pl.ds(at, rows), 2 * width :] = square[...]

        @pl.when(at >= half)
        def _():
            put_exact(send_ref, pl.ds(pl.multiple_of(at - half, rows), rows), 2 * width, square[...])

    product(rows_ref, gate_ref, 0, keep_ref, send_ref, 0, width, tile)
    product(rows_ref, up_ref, 0, keep_ref, send_ref, width, width, tile)


def gate_kernel(start, width, tile, rows_ref, gate_ref, up_ref, keep_ref, send_ref):
    product(rows_ref, gate_ref, start, keep_ref, send_ref, 0, width, tile)
    product(rows_ref, up_ref, start, keep_ref, send_ref, width, width, tile)


def scale_kernel(model, keep_ref, got_ref, out_ref):
    at = keep_ref.shape[1] - LANES
    square = keep_ref[:, at:] + take_exact(got_ref[:, at:])
    out_ref[...] = lax.rsqrt(square / model + EPS)


def hidden_kernel(scale_ref, keep_ref, got_ref, out_ref):
    width = out_ref.shape[1]
    scale = scale_ref[...]
    for at in range(0, width, LANES):
        gate = keep_ref[:, at : at + LANES] + got_ref[:, at : at + LANES].astype(F32)
        up = keep_ref[:, width + at : width + at + LANES] + got_ref[
            :, width + at : width + at + LANES
        ].astype(F32)
        gate = gate * scale
        out_ref[:, at : at + LANES] = (
            gate / (1.0 + jnp.exp(-gate)) * (up * scale)
        ).astype(BF16)


def first_hidden_kernel(model, keep_ref, got_ref, out_ref, scale_ref):
    scale_kernel(model, keep_ref, got_ref, scale_ref)
    hidden_kernel(scale_ref, keep_ref, got_ref, out_ref)


def gather_rows(pieces, rows_ref):
    rows = pieces[0].shape[0]
    for n, piece in enumerate(pieces):
        at = pl.ds(pl.multiple_of((lax.axis_index("ctx") ^ place() ^ n) * rows, rows), rows)
        rows_ref[at, :] = piece[...]


def part_down_kernel(tile, start, *refs):
    pieces, weight_ref, so_far = refs[:4], refs[4], refs[5:-2]
    out_ref, rows_ref = refs[-2:]
    gather_rows(pieces, rows_ref)
    depth = rows_ref.shape[1]
    for at in range(0, weight_ref.shape[1], tile):
        columns = slice(at, at + tile)
        part = jnp.dot(
            rows_ref[...], weight_ref[start : start + depth, columns], preferred_element_type=F32
        )
        for ref in so_far:
            part = part + ref[:, columns]
        out_ref[:, columns] = part


def down_kernel(tile, *refs):
    pieces, (weight_ref, so_far_ref, own_ref) = refs[:4], refs[4:7]
    sends, rows_ref = refs[7:-1], refs[-1]
    gather_rows(pieces, rows_ref)
    rows = pieces[0].shape[0]
    depth = rows_ref.shape[1]
    start = weight_ref.shape[0] - depth
    for at in range(0, weight_ref.shape[1], tile):
        columns = slice(at, at + tile)
        part = so_far_ref[:, columns] + jnp.dot(
            rows_ref[...], weight_ref[start:, columns], preferred_element_type=F32
        )
        own_ref[:, columns] = part[:rows]
        for n, send in enumerate(sends):
            send[:, columns] = part[(n + 1) * rows : (n + 2) * rows].astype(BF16)


def final_kernel(middle_ref, own_ref, *refs):
    parts, out_ref = refs[:-1], refs[-1]
    total = own_ref[...]
    for part in parts:
        total = total + part[...].astype(F32)
    out_ref[...] = (middle_ref[...].astype(F32) + total).astype(BF16)


def swap(x, axis):
    return lax.ppermute(x, axis, [(0, 1), (1, 0)])


def turn(x, axis, n, offset):
    return lax.ppermute(x, axis, [(i, i ^ offset) for i in range(n)])


def direct_body(
    queries,
    key_cache,
    value_cache,
    block_index,
    stream,
    out_weight,
    norm_gain,
    gate_weight,
    up_weight,
    down_weight,
):
    n_context, n_head, _ = (lax.axis_size(a) for a in ALL)
    rows, heads_width = queries.shape
    context_len = key_cache.shape[0] * n_context
    model = norm_gain.shape[0]
    total = rows * n_context
    blocks = key_cache.shape[0] // KB
    kv_width = key_cache.shape[1]
    order = (3, 2, 1)

    got_q = {m: turn(queries, "ctx", n_context, m) for m in (2, 1)}
    got_q[3] = turn(got_q[2], "ctx", n_context, 1)
    picked = struct((MOST * KB, kv_width), BF16)
    partial_out = struct((rows, heads_width + LANES), BF16)
    kv_dev = kv_width // DH
    tall = heads_width // kv_width * rows
    scratch = [
        pltpu.VMEM((kv_dev, tall, MOST * KB), F32),
        pltpu.VMEM((kv_dev, tall, MOST * KB), BF16),
    ]
    keys, values, starts, own_partial = call(
        functools.partial(first_attend_kernel, blocks, context_len - total),
        (picked, picked, struct((8, LANES), jnp.int32), partial_out),
        [SM, ANY, ANY, ANY],
        (block_index, in_hbm(queries), in_hbm(key_cache), in_hbm(value_cache)),
        scratch=[pltpu.VMEM((rows, heads_width), BF16)]
        + scratch
        + [pltpu.SemaphoreType.DMA((2, MOST)), pltpu.SemaphoreType.DMA],
    )
    partial = {0: own_partial}
    for m in order:
        partial[m] = call(
            functools.partial(attend, m, context_len - total),
            partial_out,
            [VM] * 4,
            (starts, got_q[m], keys, values),
            scratch=scratch,
        )
    back = {m: turn(partial[m], "ctx", n_context, m) for m in order}
    back[0] = partial[0]
    blended = call(
        blend_kernel, struct((rows, heads_width), BF16), [VM] * 4, tuple(back[m] for m in range(4))
    )

    attention = {m: turn(blended, "ctx", n_context, m) for m in order}
    attention[0] = blended
    width = out_weight.shape[1]
    keep, away = call(
        functools.partial(project_kernel, 512),
        (struct((n_head * rows, width), F32), struct((n_head * rows, width), BF16)),
        [VM] * 5,
        tuple(attention[m] for m in range(4)) + (in_vmem(out_weight),),
        scratch=[pltpu.VMEM((total, heads_width), BF16)],
        cost=6,
    )
    got = swap(away, "sec")
    keep, away = call(
        functools.partial(fold_kernel, width),
        (struct((rows, width), F32), struct((rows, width), BF16)),
        [VM, VM],
        (keep, got),
        cost=6,
    )
    got = swap(away, "head")
    middle = call(middle_kernel, struct((rows, width), BF16), [VM] * 3, (stream, keep, got), cost=6)

    all_middle = {
        m: lax.ppermute(
            middle,
            ALL,
            [
                (a * n_context + b, (b ^ m) * n_context + a)
                for a in range(n_context)
                for b in range(n_context)
            ],
        )
        for m in (3, 0, 1, 2)
    }
    hidden_width = gate_weight.shape[1]
    first = hidden_width * 2 // 7 // (2 * LANES) * 2 * LANES
    second = (hidden_width - first) // 2 // LANES * LANES
    widths = (first, second, hidden_width - first - second)
    chunks = tuple((sum(widths[:c]), widths[c]) for c in range(len(widths)))
    hidden = []
    gate_vmem, up_vmem = in_vmem(gate_weight), in_vmem(up_weight)
    prepared = [
        call(
            prepare_kernel,
            (struct((rows, width), BF16), struct((rows, LANES), F32)),
            [VM, VM],
            (all_middle[m], norm_gain[None]),
            cost=0,
        )
        for m in range(4)
    ]
    scale = None
    for c, (start, chunk) in enumerate(chunks):
        extra = LANES if c == 0 else 0
        out = (
            struct((n_head * rows, 2 * chunk + extra), F32),
            struct((n_head * rows, 2 * chunk + 2 * extra), BF16),
        )
        if c == 0:
            keep, away, all_rows = call(
                functools.partial(first_gate_kernel, chunk, 512),
                out + (struct((total, width), BF16),),
                [VM] * 10,
                tuple(p[0] for p in prepared)
                + tuple(p[1] for p in prepared)
                + (gate_vmem, up_vmem),
            )
        else:
            keep, away = call(
                functools.partial(gate_kernel, start, chunk, 512),
                out,
                [VM] * 3,
                (all_rows, gate_vmem, up_vmem),
            )
        keep, away = call(
            functools.partial(fold_kernel, 2 * chunk),
            (
                struct((rows, 2 * chunk + extra), F32),
                struct((rows, 2 * chunk + 2 * extra), BF16),
            ),
            [VM, VM],
            (keep, swap(away, "sec")),
        )
        got = swap(away, "head")
        if c == 0:
            own, scale = call(
                functools.partial(first_hidden_kernel, model),
                (struct((rows, chunk), BF16), struct((rows, LANES), F32)),
                [VM] * 2,
                (keep, got),
            )
        else:
            own = call(hidden_kernel, struct((rows, chunk), BF16), [VM] * 3, (scale, keep, got))
        across = swap(own, "head")
        beside = swap(own, "sec")
        hidden.append((own, beside, across, swap(across, "sec")))
    out_width = down_weight.shape[1]
    down_vmem = in_vmem(down_weight)
    so_far = ()
    for c, (start, chunk) in enumerate(chunks[:-1]):
        so_far = (
            call(
                functools.partial(part_down_kernel, 512, start),
                struct((total, out_width), F32),
                [VM] * (5 + len(so_far)),
                hidden[c] + (down_vmem,) + so_far,
                scratch=[pltpu.VMEM((total, chunk), BF16)],
            ),
        )
    res = call(
        functools.partial(down_kernel, 512),
        (struct((rows, out_width), F32),) + (struct((rows, out_width), BF16),) * 3,
        [VM] * 6,
        hidden[-1] + (down_vmem,) + so_far,
        scratch=[pltpu.VMEM((total, chunks[-1][1]), BF16)],
    )
    parts = [turn(res[m], "ctx", n_context, m) for m in order]
    return call(
        final_kernel, struct((rows, out_width), BF16), [VM] * 5, (all_middle[0], res[0]) + tuple(parts)
    )


def local_attention(gathered, key_cache, value_cache, block_index, context_index, context_len):
    group_size = HQ // KVH
    kv_dev = key_cache.shape[1] // DH
    blocks_dev = key_cache.shape[0] // KB
    total_tokens = gathered.shape[0]
    key_blocks = key_cache.reshape(blocks_dev, KB, kv_dev, DH)
    value_blocks = value_cache.reshape(blocks_dev, KB, kv_dev, DH)
    local_ids = context_index * blocks_dev + jnp.arange(blocks_dev, dtype=jnp.int32)
    member = jnp.any(block_index[:, :, None] == local_ids[None, None, :], axis=1)
    member_rank = jnp.cumsum(member.astype(jnp.int32), axis=1) - 1
    slot_hit = member[:, None, :] & (
        member_rank[:, None, :] == jnp.arange(MOST, dtype=jnp.int32)[None, :, None]
    )
    slot_block = jnp.sum(
        jnp.where(slot_hit, jnp.arange(blocks_dev, dtype=jnp.int32)[None, None, :], 0), axis=2
    )
    slot_valid = jnp.any(slot_hit, axis=2)
    picked_keys = jnp.take(key_blocks, slot_block[0], axis=0).reshape(MOST * KB, kv_dev, DH)
    picked_values = jnp.take(value_blocks, slot_block[0], axis=0).reshape(MOST * KB, kv_dev, DH)
    key_pos = (
        (local_ids[0] + slot_block[0])[:, None] * KB + jnp.arange(KB, dtype=jnp.int32)[None, :]
    ).reshape(-1)
    live_keys = jnp.broadcast_to(slot_valid[0][:, None], (MOST, KB)).reshape(-1)
    query_pos = context_len - total_tokens + jnp.arange(KB, dtype=jnp.int32)
    allowed = live_keys[None, :] & (key_pos[None, :] <= query_pos[:, None])
    query_block = gathered.reshape(KB, kv_dev, group_size, DH)
    scores = jnp.einsum(
        "qhgd,phd->hgqp", query_block, picked_keys, preferred_element_type=jnp.float32
    ) / math.sqrt(DH)
    scores = jnp.where(allowed[None, None], scores, -jnp.inf)
    peak_score = jnp.max(scores, axis=-1, keepdims=True)
    unnormed = jnp.exp(scores - peak_score)
    row_total = jnp.sum(unnormed, axis=-1)
    mixture = jnp.einsum(
        "hgqp,phd->qhgd",
        unnormed.astype(jnp.bfloat16),
        picked_values,
        preferred_element_type=jnp.float32,
    )
    result = mixture / jnp.transpose(row_total, (2, 0, 1))[..., None]
    log_total = jnp.transpose(peak_score[..., 0] + jnp.log(row_total), (2, 0, 1))
    out_list = result.reshape(KB, -1)
    lse_list = log_total.reshape(KB, -1)
    return (out_list, lse_list)


def general_body(
    queries,
    key_cache,
    value_cache,
    block_index,
    stream,
    out_weight,
    norm_gain,
    gate_weight,
    up_weight,
    down_weight,
):
    n_context = lax.axis_size("ctx")
    context_index = lax.axis_index("ctx")
    context_len = key_cache.shape[0] * n_context
    gathered = lax.all_gather(queries, "ctx", axis=0, tiled=True)
    part_out, part_lse = local_attention(
        gathered, key_cache, value_cache, block_index, context_index, context_len
    )
    spread_out, spread_lse = (
        lax.all_to_all(part_out[:, None, :], "ctx", split_axis=0, concat_axis=1, tiled=True),
        lax.all_to_all(part_lse[:, None, :], "ctx", split_axis=0, concat_axis=1, tiled=True),
    )
    share_rows = spread_out.shape[0]
    head_count = spread_lse.shape[2]
    peak_value = jnp.max(spread_lse, axis=1, keepdims=True)
    share_weight = jnp.exp(spread_lse - peak_value)
    blended = jnp.sum(
        spread_out.reshape(share_rows, n_context, head_count, -1) * share_weight[..., None], axis=1
    )
    blended = blended / jnp.sum(share_weight, axis=1)[..., None]
    attention = lax.all_gather(
        blended.reshape(share_rows, -1).astype(jnp.bfloat16), "ctx", axis=0, tiled=True
    )
    row_piece = attention
    projected = lax.psum_scatter(
        jnp.dot(row_piece, out_weight, preferred_element_type=jnp.float32),
        ("head", "sec"),
        scatter_dimension=0,
        tiled=True,
    )
    middle = (stream.astype(jnp.float32) + projected).astype(jnp.bfloat16)
    full_middle = lax.all_gather(middle, "ctx", axis=1, tiled=True)
    middle_wide = full_middle.astype(jnp.float32)
    mean_square = jnp.mean(middle_wide * middle_wide, axis=-1, keepdims=True)
    normed = (middle_wide * lax.rsqrt(mean_square + 1e-05) * norm_gain).astype(jnp.bfloat16)
    normed_cols, middle_cols = (
        lax.all_to_all(normed, ("head", "sec"), split_axis=1, concat_axis=0, tiled=True),
        lax.all_to_all(full_middle, ("head", "sec"), split_axis=1, concat_axis=0, tiled=True),
    )
    row_piece = normed_cols
    gate_up = lax.psum_scatter(
        jnp.concatenate(
            [
                jnp.dot(row_piece, gate_weight, preferred_element_type=jnp.float32),
                jnp.dot(row_piece, up_weight, preferred_element_type=jnp.float32),
            ],
            axis=1,
        ),
        ("head", "sec"),
        scatter_dimension=0,
        tiled=True,
    )
    hidden_width = gate_weight.shape[1]
    hidden = (jax.nn.silu(gate_up[:, :hidden_width]) * gate_up[:, hidden_width:]).astype(
        jnp.bfloat16
    )
    all_hidden = lax.all_gather(hidden, ("head", "sec"), axis=0, tiled=True)
    row_piece = all_hidden
    down_part = lax.psum_scatter(
        jnp.dot(row_piece, down_weight, preferred_element_type=jnp.float32),
        "ctx",
        scatter_dimension=0,
        tiled=True,
    )
    own_middle = lax.dynamic_slice_in_dim(
        middle_cols, context_index * down_part.shape[0], down_part.shape[0], 0
    )
    return (own_middle.astype(jnp.float32) + down_part).astype(jnp.bfloat16)


def solution(mesh):
    size = dict(mesh.shape)
    direct = size["ctx"] == 4 and size["head"] == 2 and size["sec"] == 2
    return jax.shard_map(
        direct_body if direct else general_body,
        mesh=mesh,
        in_specs=(
            P(("groups", "ctx"), ("head", "sec")),
            P(("groups", "ctx"), ("head", "sec")),
            P(("groups", "ctx"), ("head", "sec")),
            P("groups", None),
            P(("groups", "head", "sec"), "ctx"),
            P(("head", "sec"), "ctx"),
            P(),
            P(("head", "sec"), "ctx"),
            P(("head", "sec"), "ctx"),
            P("ctx", ("head", "sec")),
        ),
        out_specs=P(("groups", "ctx"), ("head", "sec")),
        check_vma=False,
    )
```

```python
import functools
import math

import jax
import jax.numpy as jnp
from jax import lax
from jax.experimental import pallas as pl
from jax.experimental.pallas import tpu as pltpu
from jax.sharding import PartitionSpec as P


HQ = 64
KVH = 8
DH = 128
KB = 128
MOST = 4
LANES = 128
EPS = 1e-05
CTX, HEAD, SEC = "ctx", "head", "sec"
ALL = (CTX, HEAD, SEC)
HS = (HEAD, SEC)
ROWS = ("groups", CTX)


VM = pl.BlockSpec(memory_space=pltpu.VMEM)
SM = pl.BlockSpec(memory_space=pltpu.SMEM)
ANY = pl.BlockSpec(memory_space=pl.ANY)
F32 = jnp.float32
BF16 = jnp.bfloat16


def struct(shape, dtype):
    return jax.ShapeDtypeStruct(shape, dtype)


def call(kernel, out, in_specs, args, cost=3, scratch=(), vmem=8):
    outs = out if isinstance(out, (tuple, list)) else (out,)
    nbytes = sum(math.prod(a.shape) * a.dtype.itemsize for a in args)
    nbytes += sum(math.prod(o.shape) * o.dtype.itemsize for o in outs)
    return pl.pallas_call(
        kernel,
        out_shape=out,
        in_specs=in_specs,
        out_specs=jax.tree.map(lambda _: VM, out),
        scratch_shapes=scratch,
        compiler_params=pltpu.CompilerParams(vmem_limit_bytes=vmem << 20),
        cost_estimate=pl.CostEstimate(flops=cost * 10**9, bytes_accessed=nbytes, transcendentals=0),
    )(*args)


def in_vmem(x):
    return pltpu.with_memory_space_constraint(x, pltpu.VMEM)


def in_hbm(x):
    return pltpu.with_memory_space_constraint(x, pltpu.HBM)


def slots(index_ref, blocks):
    entries = index_ref.shape[1]
    base = lax.axis_index(CTX) * blocks
    first = jnp.int32(0)
    end = jnp.int32(0)
    for n in range(entries):
        block = index_ref[0, n]
        first += (block < base).astype(jnp.int32)
        end += (block < base + blocks).astype(jnp.int32)
    found = []
    for slot in range(MOST):
        entry = jnp.minimum(first + slot, entries - 1)
        local = jnp.clip(index_ref[0, entry] - base, 0, blocks - 1)
        found.append((local, first + slot < end))
    return found


def attend(offset, first_token, start_ref, q_ref, key_ref, value_ref, out_ref, score_ref, weight_ref):
    rows = q_ref.shape[0]
    heads = q_ref.shape[1] // DH
    kv_dev = key_ref.shape[1] // DH
    group = heads // kv_dev
    scale = 1.0 / math.sqrt(DH)
    token0 = first_token + (lax.axis_index(CTX) ^ offset) * rows
    ahead = (
        lax.broadcasted_iota(jnp.int32, (rows, KB), 1)
        - lax.broadcasted_iota(jnp.int32, (rows, KB), 0)
        - token0
    )
    allowed = [ahead + start_ref[slot : slot + 1, :] <= 0 for slot in range(MOST)]
    head_lane = lax.broadcasted_iota(jnp.int32, (rows, LANES), 1)
    peak_tile = jnp.zeros((rows, LANES), F32)
    total_tile = jnp.ones((rows, LANES), F32)
    for kv in range(kv_dev):
        stacked = jnp.concatenate(
            [q_ref[:, (kv * group + h) * DH : (kv * group + h + 1) * DH] for h in range(group)], axis=0
        )
        score_ref[kv] = lax.dot_general(
            stacked,
            key_ref[:, kv * DH : (kv + 1) * DH],
            (((1,), (1,)), ((), ())),
            preferred_element_type=F32,
        )
    for kv in range(kv_dev):
        for h in range(group):
            head = kv * group + h
            span = slice(h * rows, (h + 1) * rows)
            parts = [
                jnp.where(allowed[slot], score_ref[kv, span, slot * KB : (slot + 1) * KB], -1e30)
                for slot in range(MOST)
            ]
            peak = jnp.max(functools.reduce(jnp.maximum, parts), axis=1, keepdims=True)
            parts = [jnp.exp((p - peak) * scale) for p in parts]
            row_total = jnp.sum(functools.reduce(jnp.add, parts), axis=1, keepdims=True)
            for slot, p in enumerate(parts):
                weight_ref[kv, span, slot * KB : (slot + 1) * KB] = p.astype(BF16)
            peak_tile = jnp.where(head_lane == head, peak, peak_tile)
            total_tile = jnp.where(head_lane == head, row_total, total_tile)
    inverse = 1.0 / total_tile
    for kv in range(kv_dev):
        mixture = jnp.dot(
            weight_ref[kv], value_ref[:, kv * DH : (kv + 1) * DH], preferred_element_type=F32
        )
        for h in range(group):
            head = kv * group + h
            out_ref[:, head * DH : (head + 1) * DH] = (
                mixture[h * rows : (h + 1) * rows] * inverse[:, head : head + 1]
            ).astype(BF16)
    lse_tile = peak_tile * scale + jnp.log(total_tile)
    high = lse_tile.astype(BF16).astype(F32)
    rest = lse_tile - high
    mid = rest.astype(BF16).astype(F32)
    low = rest - mid
    tile = high + pltpu.roll(mid, heads, 1) + pltpu.roll(low, 2 * heads, 1)
    out_ref[:, heads * DH :] = tile.astype(BF16)


def first_attend_kernel(
    blocks, first_token, index_ref, q_hbm, key_hbm, value_hbm,
    key_ref, value_ref, start_ref, out_ref, q_ref, score_ref, weight_ref, sems, q_sem,
):
    copies = [pltpu.make_async_copy(q_hbm, q_ref, q_sem)]
    found = slots(index_ref, blocks)
    for slot, (local, _) in enumerate(found):
        rows = pl.ds(pl.multiple_of(local * KB, KB), KB)
        for n, (src, dst) in enumerate(((key_hbm, key_ref), (value_hbm, value_ref))):
            copies.append(
                pltpu.make_async_copy(
                    src.at[rows, :], dst.at[slot * KB : (slot + 1) * KB, :], sems.at[n, slot]
                )
            )
    for copy in copies:
        copy.start()
    row = lax.broadcasted_iota(jnp.int32, start_ref.shape, 0)
    starts = jnp.zeros(start_ref.shape, jnp.int32)
    base = lax.axis_index(CTX) * blocks
    for slot, (local, valid) in enumerate(found):
        starts = jnp.where(row == slot, jnp.where(valid, (base + local) * KB, jnp.int32(1 << 29)), starts)
    start_ref[...] = starts
    for copy in copies:
        copy.wait()
    attend(0, first_token, start_ref, q_ref, key_ref, value_ref, out_ref, score_ref, weight_ref)


def blend_kernel(*refs):
    out_ref = refs[-1]
    parts = refs[:-1]
    heads = out_ref.shape[1] // DH
    logs = []
    for part in parts:
        tile = part[:, heads * DH :].astype(F32)
        logs.append(
            tile + pltpu.roll(tile, LANES - heads, 1) + pltpu.roll(tile, LANES - 2 * heads, 1)
        )
    peak = functools.reduce(jnp.maximum, logs)
    shares = [jnp.exp(log - peak) for log in logs]
    total = functools.reduce(jnp.add, shares)
    shares = [share / total for share in shares]
    for head in range(heads):
        span = slice(head * DH, (head + 1) * DH)
        out_ref[:, span] = functools.reduce(
            jnp.add,
            [share[:, head : head + 1] * part[:, span].astype(F32) for share, part in zip(shares, parts)],
        ).astype(BF16)


def place():
    return lax.axis_index(HEAD) * lax.axis_size(SEC) + lax.axis_index(SEC)


def place_of(n, rows, count):
    n_sec = lax.axis_size(SEC)
    owner = lax.axis_index(CTX) ^ n
    other = ((owner % n_sec) != lax.axis_index(SEC)).astype(jnp.int32)
    return pl.multiple_of(other * (count // n_sec * rows) + owner // n_sec * rows, rows)


def product(rows_ref, weight_ref, source, keep_ref, send_ref, target, width, tile):
    half = rows_ref.shape[0] // 2
    for at in range(0, width, tile):
        size = min(tile, width - at)
        part = jnp.dot(
            rows_ref[...],
            weight_ref[:, source + at : source + at + size],
            preferred_element_type=F32,
        )
        keep_ref[:, target + at : target + at + size] = part[:half]
        send_ref[:, target + at : target + at + size] = part[half:].astype(BF16)


def project_kernel(tile, *refs):
    pieces, (weight_ref, keep_ref, send_ref, rows_ref) = refs[:-4], refs[-4:]
    rows = pieces[0].shape[0]
    for n, piece in enumerate(pieces):
        rows_ref[pl.ds(place_of(n, rows, len(pieces)), rows), :] = piece[...]
    product(rows_ref, weight_ref, 0, keep_ref, send_ref, 0, weight_ref.shape[1], tile)


def fold_kernel(width, keep_ref, got_ref, keep_out, send_out):
    rows = keep_out.shape[0]
    head = lax.axis_index(HEAD)
    mine = pl.ds(pl.multiple_of(head * rows, rows), rows)
    other = pl.ds(pl.multiple_of((1 - head) * rows, rows), rows)
    keep_out[:, :width] = keep_ref[mine, :width] + got_ref[mine, :width].astype(F32)
    send_out[:, :width] = (keep_ref[other, :width] + got_ref[other, :width].astype(F32)).astype(BF16)
    if keep_ref.shape[1] > width:
        keep_out[:, width:] = keep_ref[mine, width:] + take_exact(got_ref[mine, width:])
        put_exact(send_out, slice(None), width, keep_ref[other, width:] + take_exact(got_ref[other, width:]))


def middle_kernel(stream_ref, keep_ref, got_ref, out_ref):
    out_ref[...] = (
        stream_ref[...].astype(F32) + (keep_ref[...] + got_ref[...].astype(F32))
    ).astype(BF16)


def put_exact(ref, rows, at, value):
    high = value.astype(BF16)
    ref[rows, at : at + LANES] = high
    ref[rows, at + LANES : at + 2 * LANES] = (value - high.astype(F32)).astype(BF16)


def take_exact(tile):
    return tile[:, :LANES].astype(F32) + tile[:, LANES:].astype(F32)


def prepare_kernel(piece_ref, gain_ref, row_ref, square_ref):
    model = piece_ref.shape[1]
    gain = gain_ref[:, pl.ds(pl.multiple_of(place() * model, model), model)]
    wide = piece_ref[...].astype(F32)
    row_ref[...] = (wide * gain).astype(BF16)
    square_ref[...] = jnp.broadcast_to(jnp.sum(wide * wide, axis=1, keepdims=True), square_ref.shape)


def first_gate_kernel(width, tile, *refs):
    pieces, squares = refs[:4], refs[4:8]
    gate_ref, up_ref, keep_ref, send_ref, rows_ref = refs[8:]
    rows = pieces[0].shape[0]
    half = rows_ref.shape[0] // 2
    for n, (piece, square) in enumerate(zip(pieces, squares)):
        at = place_of(n, rows, len(pieces))
        rows_ref[pl.ds(at, rows), :] = piece[...]

        @pl.when(at < half)
        def _():
            keep_ref[pl.ds(at, rows), 2 * width :] = square[...]

        @pl.when(at >= half)
        def _():
            put_exact(send_ref, pl.ds(pl.multiple_of(at - half, rows), rows), 2 * width, square[...])

    product(rows_ref, gate_ref, 0, keep_ref, send_ref, 0, width, tile)
    product(rows_ref, up_ref, 0, keep_ref, send_ref, width, width, tile)


def gate_kernel(start, width, tile, rows_ref, gate_ref, up_ref, keep_ref, send_ref):
    product(rows_ref, gate_ref, start, keep_ref, send_ref, 0, width, tile)
    product(rows_ref, up_ref, start, keep_ref, send_ref, width, width, tile)


def scale_kernel(model, keep_ref, got_ref, out_ref):
    at = keep_ref.shape[1] - LANES
    square = keep_ref[:, at:] + take_exact(got_ref[:, at:])
    out_ref[...] = lax.rsqrt(square / model + EPS)


def hidden_kernel(scale_ref, keep_ref, got_ref, out_ref):
    width = out_ref.shape[1]
    scale = scale_ref[...]
    for at in range(0, width, LANES):
        gate = keep_ref[:, at : at + LANES] + got_ref[:, at : at + LANES].astype(F32)
        up = keep_ref[:, width + at : width + at + LANES] + got_ref[
            :, width + at : width + at + LANES
        ].astype(F32)
        gate = gate * scale
        out_ref[:, at : at + LANES] = (
            gate / (1.0 + jnp.exp(-gate)) * (up * scale)
        ).astype(BF16)


def first_hidden_kernel(model, keep_ref, got_ref, out_ref, scale_ref):
    scale_kernel(model, keep_ref, got_ref, scale_ref)
    hidden_kernel(scale_ref, keep_ref, got_ref, out_ref)


def gather_rows(pieces, rows_ref):
    rows = pieces[0].shape[0]
    for n, piece in enumerate(pieces):
        at = pl.ds(pl.multiple_of((lax.axis_index(CTX) ^ place() ^ n) * rows, rows), rows)
        rows_ref[at, :] = piece[...]


def part_down_kernel(tile, start, *refs):
    pieces, weight_ref, so_far = refs[:4], refs[4], refs[5:-2]
    out_ref, rows_ref = refs[-2:]
    gather_rows(pieces, rows_ref)
    depth = rows_ref.shape[1]
    for at in range(0, weight_ref.shape[1], tile):
        columns = slice(at, at + tile)
        part = jnp.dot(
            rows_ref[...], weight_ref[start : start + depth, columns], preferred_element_type=F32
        )
        for ref in so_far:
            part = part + ref[:, columns]
        out_ref[:, columns] = part


def down_kernel(tile, *refs):
    pieces, (weight_ref, so_far_ref, own_ref) = refs[:4], refs[4:7]
    sends, rows_ref = refs[7:-1], refs[-1]
    gather_rows(pieces, rows_ref)
    rows = pieces[0].shape[0]
    depth = rows_ref.shape[1]
    start = weight_ref.shape[0] - depth
    for at in range(0, weight_ref.shape[1], tile):
        columns = slice(at, at + tile)
        part = so_far_ref[:, columns] + jnp.dot(
            rows_ref[...], weight_ref[start:, columns], preferred_element_type=F32
        )
        own_ref[:, columns] = part[:rows]
        for n, send in enumerate(sends):
            send[:, columns] = part[(n + 1) * rows : (n + 2) * rows].astype(BF16)


def final_kernel(middle_ref, own_ref, *refs):
    parts, out_ref = refs[:-1], refs[-1]
    total = own_ref[...]
    for part in parts:
        total = total + part[...].astype(F32)
    out_ref[...] = (middle_ref[...].astype(F32) + total).astype(BF16)


def swap(x, axis):
    return lax.ppermute(x, axis, [(0, 1), (1, 0)])


def turn(x, axis, n, offset):
    return lax.ppermute(x, axis, [(i, i ^ offset) for i in range(n)])


def direct_body(
    queries,
    key_cache,
    value_cache,
    block_index,
    stream,
    out_weight,
    norm_gain,
    gate_weight,
    up_weight,
    down_weight,
):
    n_context, n_head, _ = (lax.axis_size(a) for a in ALL)
    rows, heads_width = queries.shape
    context_len = key_cache.shape[0] * n_context
    model = norm_gain.shape[0]
    total = rows * n_context
    blocks = key_cache.shape[0] // KB
    kv_width = key_cache.shape[1]
    order = (3, 2, 1)

    got_q = {m: turn(queries, CTX, n_context, m) for m in (2, 1)}
    got_q[3] = turn(got_q[2], CTX, n_context, 1)
    picked = struct((MOST * KB, kv_width), BF16)
    partial_out = struct((rows, heads_width + LANES), BF16)
    kv_dev = kv_width // DH
    tall = heads_width // kv_width * rows
    scratch = [
        pltpu.VMEM((kv_dev, tall, MOST * KB), F32),
        pltpu.VMEM((kv_dev, tall, MOST * KB), BF16),
    ]
    keys, values, starts, own_partial = call(
        functools.partial(first_attend_kernel, blocks, context_len - total),
        (picked, picked, struct((8, LANES), jnp.int32), partial_out),
        [SM, ANY, ANY, ANY],
        (block_index, in_hbm(queries), in_hbm(key_cache), in_hbm(value_cache)),
        scratch=[pltpu.VMEM((rows, heads_width), BF16)]
        + scratch
        + [pltpu.SemaphoreType.DMA((2, MOST)), pltpu.SemaphoreType.DMA],
    )
    partial = {0: own_partial}
    for m in order:
        partial[m] = call(
            functools.partial(attend, m, context_len - total),
            partial_out,
            [VM] * 4,
            (starts, got_q[m], keys, values),
            scratch=scratch,
        )
    back = {m: turn(partial[m], CTX, n_context, m) for m in order}
    back[0] = partial[0]
    blended = call(
        blend_kernel, struct((rows, heads_width), BF16), [VM] * 4, tuple(back[m] for m in range(4))
    )

    attention = {m: turn(blended, CTX, n_context, m) for m in (2, 1)}
    attention[3] = turn(attention[2], CTX, n_context, 1)
    attention[0] = blended
    width = out_weight.shape[1]
    keep, away = call(
        functools.partial(project_kernel, 512),
        (struct((n_head * rows, width), F32), struct((n_head * rows, width), BF16)),
        [VM] * 5,
        tuple(attention[m] for m in range(4)) + (in_vmem(out_weight),),
        scratch=[pltpu.VMEM((total, heads_width), BF16)],
        cost=6,
    )
    got = swap(away, SEC)
    keep, away = call(
        functools.partial(fold_kernel, width),
        (struct((rows, width), F32), struct((rows, width), BF16)),
        [VM, VM],
        (keep, got),
        cost=6,
    )
    got = swap(away, HEAD)
    middle = call(middle_kernel, struct((rows, width), BF16), [VM] * 3, (stream, keep, got), cost=6)

    all_middle = {
        m: lax.ppermute(
            middle,
            ALL,
            [
                (a * n_context + b, (b ^ m) * n_context + a)
                for a in range(n_context)
                for b in range(n_context)
            ],
        )
        for m in (3, 0, 1, 2)
    }
    hidden_width = gate_weight.shape[1]
    first = hidden_width * 2 // 7 // (2 * LANES) * 2 * LANES
    second = (hidden_width - first) // 2 // LANES * LANES
    widths = (first, second, hidden_width - first - second)
    chunks = tuple((sum(widths[:c]), widths[c]) for c in range(len(widths)))
    hidden = []
    gate_vmem, up_vmem = in_vmem(gate_weight), in_vmem(up_weight)
    prepared = [
        call(
            prepare_kernel,
            (struct((rows, width), BF16), struct((rows, LANES), F32)),
            [VM, VM],
            (all_middle[m], norm_gain[None]),
            cost=0,
        )
        for m in range(4)
    ]
    scale = None
    for c, (start, chunk) in enumerate(chunks):
        extra = LANES if c == 0 else 0
        out = (
            struct((n_head * rows, 2 * chunk + extra), F32),
            struct((n_head * rows, 2 * chunk + 2 * extra), BF16),
        )
        if c == 0:
            keep, away, all_rows = call(
                functools.partial(first_gate_kernel, chunk, 512),
                out + (struct((total, width), BF16),),
                [VM] * 10,
                tuple(p[0] for p in prepared)
                + tuple(p[1] for p in prepared)
                + (gate_vmem, up_vmem),
            )
        else:
            keep, away = call(
                functools.partial(gate_kernel, start, chunk, 512),
                out,
                [VM] * 3,
                (all_rows, gate_vmem, up_vmem),
            )
        keep, away = call(
            functools.partial(fold_kernel, 2 * chunk),
            (
                struct((rows, 2 * chunk + extra), F32),
                struct((rows, 2 * chunk + 2 * extra), BF16),
            ),
            [VM, VM],
            (keep, swap(away, SEC)),
        )
        got = swap(away, HEAD)
        if c == 0:
            own, scale = call(
                functools.partial(first_hidden_kernel, model),
                (struct((rows, chunk), BF16), struct((rows, LANES), F32)),
                [VM] * 2,
                (keep, got),
            )
        else:
            own = call(hidden_kernel, struct((rows, chunk), BF16), [VM] * 3, (scale, keep, got))
        across = swap(own, HEAD)
        beside = swap(own, SEC)
        hidden.append((own, beside, across, swap(across, SEC)))
    out_width = down_weight.shape[1]
    down_vmem = in_vmem(down_weight)
    so_far = ()
    for c, (start, chunk) in enumerate(chunks[:-1]):
        so_far = (
            call(
                functools.partial(part_down_kernel, 512, start),
                struct((total, out_width), F32),
                [VM] * (5 + len(so_far)),
                hidden[c] + (down_vmem,) + so_far,
                scratch=[pltpu.VMEM((total, chunk), BF16)],
            ),
        )
    res = call(
        functools.partial(down_kernel, 512),
        (struct((rows, out_width), F32),) + (struct((rows, out_width), BF16),) * 3,
        [VM] * 6,
        hidden[-1] + (down_vmem,) + so_far,
        scratch=[pltpu.VMEM((total, chunks[-1][1]), BF16)],
    )
    parts = [turn(res[m], CTX, n_context, m) for m in order]
    return call(
        final_kernel, struct((rows, out_width), BF16), [VM] * 5, (all_middle[0], res[0]) + tuple(parts)
    )


def local_attention(gathered, key_cache, value_cache, block_index, context_index, context_len):
    group_size = HQ // KVH
    kv_dev = key_cache.shape[1] // DH
    blocks_dev = key_cache.shape[0] // KB
    total_tokens = gathered.shape[0]
    key_blocks = key_cache.reshape(blocks_dev, KB, kv_dev, DH)
    value_blocks = value_cache.reshape(blocks_dev, KB, kv_dev, DH)
    local_ids = context_index * blocks_dev + jnp.arange(blocks_dev, dtype=jnp.int32)
    member = jnp.any(block_index[:, :, None] == local_ids[None, None, :], axis=1)
    member_rank = jnp.cumsum(member.astype(jnp.int32), axis=1) - 1
    slot_hit = member[:, None, :] & (
        member_rank[:, None, :] == jnp.arange(MOST, dtype=jnp.int32)[None, :, None]
    )
    slot_block = jnp.sum(
        jnp.where(slot_hit, jnp.arange(blocks_dev, dtype=jnp.int32)[None, None, :], 0), axis=2
    )
    slot_valid = jnp.any(slot_hit, axis=2)
    picked_keys = jnp.take(key_blocks, slot_block[0], axis=0).reshape(MOST * KB, kv_dev, DH)
    picked_values = jnp.take(value_blocks, slot_block[0], axis=0).reshape(MOST * KB, kv_dev, DH)
    key_pos = (
        (local_ids[0] + slot_block[0])[:, None] * KB + jnp.arange(KB, dtype=jnp.int32)[None, :]
    ).reshape(-1)
    live_keys = jnp.broadcast_to(slot_valid[0][:, None], (MOST, KB)).reshape(-1)
    query_pos = context_len - total_tokens + jnp.arange(KB, dtype=jnp.int32)
    allowed = live_keys[None, :] & (key_pos[None, :] <= query_pos[:, None])
    query_block = gathered.reshape(KB, kv_dev, group_size, DH)
    scores = jnp.einsum(
        "qhgd,phd->hgqp", query_block, picked_keys, preferred_element_type=jnp.float32
    ) / math.sqrt(DH)
    scores = jnp.where(allowed[None, None], scores, -jnp.inf)
    peak_score = jnp.max(scores, axis=-1, keepdims=True)
    unnormed = jnp.exp(scores - peak_score)
    row_total = jnp.sum(unnormed, axis=-1)
    mixture = jnp.einsum(
        "hgqp,phd->qhgd",
        unnormed.astype(jnp.bfloat16),
        picked_values,
        preferred_element_type=jnp.float32,
    )
    result = mixture / jnp.transpose(row_total, (2, 0, 1))[..., None]
    log_total = jnp.transpose(peak_score[..., 0] + jnp.log(row_total), (2, 0, 1))
    out_list = result.reshape(KB, -1)
    lse_list = log_total.reshape(KB, -1)
    return (out_list, lse_list)


def general_body(
    queries,
    key_cache,
    value_cache,
    block_index,
    stream,
    out_weight,
    norm_gain,
    gate_weight,
    up_weight,
    down_weight,
):
    n_context = lax.axis_size(CTX)
    context_index = lax.axis_index(CTX)
    context_len = key_cache.shape[0] * n_context
    gathered = lax.all_gather(queries, CTX, axis=0, tiled=True)
    part_out, part_lse = local_attention(
        gathered, key_cache, value_cache, block_index, context_index, context_len
    )
    spread_out, spread_lse = (
        lax.all_to_all(part_out[:, None, :], CTX, split_axis=0, concat_axis=1, tiled=True),
        lax.all_to_all(part_lse[:, None, :], CTX, split_axis=0, concat_axis=1, tiled=True),
    )
    share_rows = spread_out.shape[0]
    head_count = spread_lse.shape[2]
    peak_value = jnp.max(spread_lse, axis=1, keepdims=True)
    share_weight = jnp.exp(spread_lse - peak_value)
    blended = jnp.sum(
        spread_out.reshape(share_rows, n_context, head_count, -1) * share_weight[..., None], axis=1
    )
    blended = blended / jnp.sum(share_weight, axis=1)[..., None]
    attention = lax.all_gather(
        blended.reshape(share_rows, -1).astype(jnp.bfloat16), CTX, axis=0, tiled=True
    )
    row_piece = attention
    projected = lax.psum_scatter(
        jnp.dot(row_piece, out_weight, preferred_element_type=jnp.float32),
        HS,
        scatter_dimension=0,
        tiled=True,
    )
    middle = (stream.astype(jnp.float32) + projected).astype(jnp.bfloat16)
    full_middle = lax.all_gather(middle, CTX, axis=1, tiled=True)
    middle_wide = full_middle.astype(jnp.float32)
    mean_square = jnp.mean(middle_wide * middle_wide, axis=-1, keepdims=True)
    normed = (middle_wide * lax.rsqrt(mean_square + 1e-05) * norm_gain).astype(jnp.bfloat16)
    normed_cols, middle_cols = (
        lax.all_to_all(normed, HS, split_axis=1, concat_axis=0, tiled=True),
        lax.all_to_all(full_middle, HS, split_axis=1, concat_axis=0, tiled=True),
    )
    row_piece = normed_cols
    gate_up = lax.psum_scatter(
        jnp.concatenate(
            [
                jnp.dot(row_piece, gate_weight, preferred_element_type=jnp.float32),
                jnp.dot(row_piece, up_weight, preferred_element_type=jnp.float32),
            ],
            axis=1,
        ),
        HS,
        scatter_dimension=0,
        tiled=True,
    )
    hidden_width = gate_weight.shape[1]
    hidden = (jax.nn.silu(gate_up[:, :hidden_width]) * gate_up[:, hidden_width:]).astype(
        jnp.bfloat16
    )
    all_hidden = lax.all_gather(hidden, HS, axis=0, tiled=True)
    row_piece = all_hidden
    down_part = lax.psum_scatter(
        jnp.dot(row_piece, down_weight, preferred_element_type=jnp.float32),
        CTX,
        scatter_dimension=0,
        tiled=True,
    )
    own_middle = lax.dynamic_slice_in_dim(
        middle_cols, context_index * down_part.shape[0], down_part.shape[0], 0
    )
    return (own_middle.astype(jnp.float32) + down_part).astype(jnp.bfloat16)


def solution(mesh):
    size = dict(mesh.shape)
    direct = size[CTX] == 4 and size[HEAD] == 2 and size[SEC] == 2
    return jax.shard_map(
        direct_body if direct else general_body,
        mesh=mesh,
        in_specs=(
            P(ROWS, HS),
            P(ROWS, HS),
            P(ROWS, HS),
            P("groups", None),
            P(("groups",) + HS, CTX),
            P(HS, CTX),
            P(),
            P(HS, CTX),
            P(HS, CTX),
            P(CTX, HS),
        ),
        out_specs=P(ROWS, HS),
        check_vma=False,
    )
```

```python
import functools
import math

import jax
import jax.numpy as jnp
from jax import lax
from jax.experimental import pallas as pl
from jax.experimental.pallas import tpu as pltpu
from jax.sharding import PartitionSpec as P


HQ = 64
KVH = 8
DH = 128
KB = 128
MOST = 4
LANES = 128
EPS = 1e-05
CTX, HEAD, SEC = "ctx", "head", "sec"
ALL = (CTX, HEAD, SEC)
HS = (HEAD, SEC)
ROWS = ("groups", CTX)


VM = pl.BlockSpec(memory_space=pltpu.VMEM)
SM = pl.BlockSpec(memory_space=pltpu.SMEM)
ANY = pl.BlockSpec(memory_space=pl.ANY)
F32 = jnp.float32
BF16 = jnp.bfloat16


def struct(shape, dtype):
    return jax.ShapeDtypeStruct(shape, dtype)


def call(kernel, out, in_specs, args, cost=3, scratch=(), vmem=8):
    outs = out if isinstance(out, (tuple, list)) else (out,)
    nbytes = sum(math.prod(a.shape) * a.dtype.itemsize for a in args)
    nbytes += sum(math.prod(o.shape) * o.dtype.itemsize for o in outs)
    return pl.pallas_call(
        kernel,
        out_shape=out,
        in_specs=in_specs,
        out_specs=jax.tree.map(lambda _: VM, out),
        scratch_shapes=scratch,
        compiler_params=pltpu.CompilerParams(vmem_limit_bytes=vmem << 20),
        cost_estimate=pl.CostEstimate(flops=cost * 10**9, bytes_accessed=nbytes, transcendentals=0),
    )(*args)


def in_vmem(x):
    return pltpu.with_memory_space_constraint(x, pltpu.VMEM)


def in_hbm(x):
    return pltpu.with_memory_space_constraint(x, pltpu.HBM)


def slots(index_ref, blocks):
    entries = index_ref.shape[1]
    base = lax.axis_index(CTX) * blocks
    first = jnp.int32(0)
    end = jnp.int32(0)
    for n in range(entries):
        block = index_ref[0, n]
        first += (block < base).astype(jnp.int32)
        end += (block < base + blocks).astype(jnp.int32)
    found = []
    for slot in range(MOST):
        entry = jnp.minimum(first + slot, entries - 1)
        local = jnp.clip(index_ref[0, entry] - base, 0, blocks - 1)
        found.append((local, first + slot < end))
    return found


def attend(offset, first_token, start_ref, q_ref, key_ref, value_ref, out_ref, score_ref, weight_ref):
    rows = q_ref.shape[0]
    heads = q_ref.shape[1] // DH
    kv_dev = key_ref.shape[1] // DH
    group = heads // kv_dev
    scale = 1.0 / math.sqrt(DH)
    token0 = first_token + (lax.axis_index(CTX) ^ offset) * rows
    ahead = (
        lax.broadcasted_iota(jnp.int32, (rows, KB), 1)
        - lax.broadcasted_iota(jnp.int32, (rows, KB), 0)
        - token0
    )
    allowed = [ahead + start_ref[slot : slot + 1, :] <= 0 for slot in range(MOST)]
    head_lane = lax.broadcasted_iota(jnp.int32, (rows, LANES), 1)
    peak_tile = jnp.zeros((rows, LANES), F32)
    total_tile = jnp.ones((rows, LANES), F32)
    for kv in range(kv_dev):
        stacked = jnp.concatenate(
            [q_ref[:, (kv * group + h) * DH : (kv * group + h + 1) * DH] for h in range(group)], axis=0
        )
        score_ref[kv] = lax.dot_general(
            stacked,
            key_ref[:, kv * DH : (kv + 1) * DH],
            (((1,), (1,)), ((), ())),
            preferred_element_type=F32,
        )
    for kv in range(kv_dev):
        for h in range(group):
            head = kv * group + h
            span = slice(h * rows, (h + 1) * rows)
            parts = [
                jnp.where(allowed[slot], score_ref[kv, span, slot * KB : (slot + 1) * KB], -1e30)
                for slot in range(MOST)
            ]
            peak = jnp.max(functools.reduce(jnp.maximum, parts), axis=1, keepdims=True)
            parts = [jnp.exp((p - peak) * scale) for p in parts]
            row_total = jnp.sum(functools.reduce(jnp.add, parts), axis=1, keepdims=True)
            for slot, p in enumerate(parts):
                weight_ref[kv, span, slot * KB : (slot + 1) * KB] = p.astype(BF16)
            peak_tile = jnp.where(head_lane == head, peak, peak_tile)
            total_tile = jnp.where(head_lane == head, row_total, total_tile)
    inverse = 1.0 / total_tile
    for kv in range(kv_dev):
        mixture = jnp.dot(
            weight_ref[kv], value_ref[:, kv * DH : (kv + 1) * DH], preferred_element_type=F32
        )
        for h in range(group):
            head = kv * group + h
            out_ref[:, head * DH : (head + 1) * DH] = (
                mixture[h * rows : (h + 1) * rows] * inverse[:, head : head + 1]
            ).astype(BF16)
    lse_tile = peak_tile * scale + jnp.log(total_tile)
    high = lse_tile.astype(BF16).astype(F32)
    rest = lse_tile - high
    mid = rest.astype(BF16).astype(F32)
    low = rest - mid
    tile = high + pltpu.roll(mid, heads, 1) + pltpu.roll(low, 2 * heads, 1)
    out_ref[:, heads * DH :] = tile.astype(BF16)


def first_attend_kernel(
    blocks, first_token, index_ref, q_hbm, key_hbm, value_hbm,
    key_ref, value_ref, start_ref, out_ref, q_ref, score_ref, weight_ref, sems, q_sem,
):
    copies = [pltpu.make_async_copy(q_hbm, q_ref, q_sem)]
    found = slots(index_ref, blocks)
    for slot, (local, _) in enumerate(found):
        rows = pl.ds(pl.multiple_of(local * KB, KB), KB)
        for n, (src, dst) in enumerate(((key_hbm, key_ref), (value_hbm, value_ref))):
            copies.append(
                pltpu.make_async_copy(
                    src.at[rows, :], dst.at[slot * KB : (slot + 1) * KB, :], sems.at[n, slot]
                )
            )
    for copy in copies:
        copy.start()
    row = lax.broadcasted_iota(jnp.int32, start_ref.shape, 0)
    starts = jnp.zeros(start_ref.shape, jnp.int32)
    base = lax.axis_index(CTX) * blocks
    for slot, (local, valid) in enumerate(found):
        starts = jnp.where(row == slot, jnp.where(valid, (base + local) * KB, jnp.int32(1 << 29)), starts)
    start_ref[...] = starts
    for copy in copies:
        copy.wait()
    attend(0, first_token, start_ref, q_ref, key_ref, value_ref, out_ref, score_ref, weight_ref)


def blend_kernel(*refs):
    out_ref = refs[-1]
    parts = refs[:-1]
    heads = out_ref.shape[1] // DH
    logs = []
    for part in parts:
        tile = part[:, heads * DH :].astype(F32)
        logs.append(
            tile + pltpu.roll(tile, LANES - heads, 1) + pltpu.roll(tile, LANES - 2 * heads, 1)
        )
    peak = functools.reduce(jnp.maximum, logs)
    shares = [jnp.exp(log - peak) for log in logs]
    total = functools.reduce(jnp.add, shares)
    shares = [share / total for share in shares]
    for head in range(heads):
        span = slice(head * DH, (head + 1) * DH)
        out_ref[:, span] = functools.reduce(
            jnp.add,
            [share[:, head : head + 1] * part[:, span].astype(F32) for share, part in zip(shares, parts)],
        ).astype(BF16)


def place():
    return lax.axis_index(HEAD) * lax.axis_size(SEC) + lax.axis_index(SEC)


def place_of(n, rows, count):
    n_sec = lax.axis_size(SEC)
    owner = lax.axis_index(CTX) ^ n
    other = ((owner % n_sec) != lax.axis_index(SEC)).astype(jnp.int32)
    return pl.multiple_of(other * (count // n_sec * rows) + owner // n_sec * rows, rows)


def product(rows_ref, weight_ref, source, keep_ref, send_ref, target, width, tile):
    half = rows_ref.shape[0] // 2
    for at in range(0, width, tile):
        size = min(tile, width - at)
        part = jnp.dot(
            rows_ref[...],
            weight_ref[:, source + at : source + at + size],
            preferred_element_type=F32,
        )
        keep_ref[:, target + at : target + at + size] = part[:half]
        send_ref[:, target + at : target + at + size] = part[half:].astype(BF16)


def project_kernel(tile, *refs):
    pieces, (weight_ref, keep_ref, send_ref, rows_ref) = refs[:-4], refs[-4:]
    rows = pieces[0].shape[0]
    for n, piece in enumerate(pieces):
        rows_ref[pl.ds(place_of(n, rows, len(pieces)), rows), :] = piece[...]
    product(rows_ref, weight_ref, 0, keep_ref, send_ref, 0, weight_ref.shape[1], tile)


def fold_kernel(width, keep_ref, got_ref, keep_out, send_out):
    rows = keep_out.shape[0]
    head = lax.axis_index(HEAD)
    mine = pl.ds(pl.multiple_of(head * rows, rows), rows)
    other = pl.ds(pl.multiple_of((1 - head) * rows, rows), rows)
    keep_out[:, :width] = keep_ref[mine, :width] + got_ref[mine, :width].astype(F32)
    send_out[:, :width] = (keep_ref[other, :width] + got_ref[other, :width].astype(F32)).astype(BF16)
    if keep_ref.shape[1] > width:
        keep_out[:, width:] = keep_ref[mine, width:] + take_exact(got_ref[mine, width:])
        put_exact(send_out, slice(None), width, keep_ref[other, width:] + take_exact(got_ref[other, width:]))


def middle_kernel(stream_ref, keep_ref, got_ref, out_ref):
    out_ref[...] = (
        stream_ref[...].astype(F32) + (keep_ref[...] + got_ref[...].astype(F32))
    ).astype(BF16)


def put_exact(ref, rows, at, value):
    high = value.astype(BF16)
    ref[rows, at : at + LANES] = high
    ref[rows, at + LANES : at + 2 * LANES] = (value - high.astype(F32)).astype(BF16)


def take_exact(tile):
    return tile[:, :LANES].astype(F32) + tile[:, LANES:].astype(F32)


def prepare_kernel(piece_ref, gain_ref, row_ref, square_ref):
    model = piece_ref.shape[1]
    gain = gain_ref[:, pl.ds(pl.multiple_of(place() * model, model), model)]
    wide = piece_ref[...].astype(F32)
    row_ref[...] = (wide * gain).astype(BF16)
    square_ref[...] = jnp.broadcast_to(jnp.sum(wide * wide, axis=1, keepdims=True), square_ref.shape)


def first_gate_kernel(width, tile, *refs):
    pieces, squares = refs[:4], refs[4:8]
    gate_ref, up_ref, keep_ref, send_ref, rows_ref = refs[8:]
    rows = pieces[0].shape[0]
    half = rows_ref.shape[0] // 2
    for n, (piece, square) in enumerate(zip(pieces, squares)):
        at = place_of(n, rows, len(pieces))
        rows_ref[pl.ds(at, rows), :] = piece[...]

        @pl.when(at < half)
        def _():
            keep_ref[pl.ds(at, rows), 2 * width :] = square[...]

        @pl.when(at >= half)
        def _():
            put_exact(send_ref, pl.ds(pl.multiple_of(at - half, rows), rows), 2 * width, square[...])

    product(rows_ref, gate_ref, 0, keep_ref, send_ref, 0, width, tile)
    product(rows_ref, up_ref, 0, keep_ref, send_ref, width, width, tile)


def gate_kernel(start, width, tile, rows_ref, gate_ref, up_ref, keep_ref, send_ref):
    product(rows_ref, gate_ref, start, keep_ref, send_ref, 0, width, tile)
    product(rows_ref, up_ref, start, keep_ref, send_ref, width, width, tile)


def scale_kernel(model, keep_ref, got_ref, out_ref):
    at = keep_ref.shape[1] - LANES
    square = keep_ref[:, at:] + take_exact(got_ref[:, at:])
    out_ref[...] = lax.rsqrt(square / model + EPS)


def hidden_kernel(scale_ref, keep_ref, got_ref, out_ref):
    width = out_ref.shape[1]
    scale = scale_ref[...]
    for at in range(0, width, LANES):
        gate = keep_ref[:, at : at + LANES] + got_ref[:, at : at + LANES].astype(F32)
        up = keep_ref[:, width + at : width + at + LANES] + got_ref[
            :, width + at : width + at + LANES
        ].astype(F32)
        gate = gate * scale
        out_ref[:, at : at + LANES] = (
            gate / (1.0 + jnp.exp(-gate)) * (up * scale)
        ).astype(BF16)


def first_hidden_kernel(model, keep_ref, got_ref, out_ref, scale_ref):
    scale_kernel(model, keep_ref, got_ref, scale_ref)
    hidden_kernel(scale_ref, keep_ref, got_ref, out_ref)


def gather_rows(pieces, rows_ref):
    rows = pieces[0].shape[0]
    for n, piece in enumerate(pieces):
        at = pl.ds(pl.multiple_of((lax.axis_index(CTX) ^ place() ^ n) * rows, rows), rows)
        rows_ref[at, :] = piece[...]


def part_down_kernel(tile, start, *refs):
    pieces, weight_ref, so_far = refs[:4], refs[4], refs[5:-2]
    out_ref, rows_ref = refs[-2:]
    gather_rows(pieces, rows_ref)
    depth = rows_ref.shape[1]
    for at in range(0, weight_ref.shape[1], tile):
        columns = slice(at, at + tile)
        part = jnp.dot(
            rows_ref[...], weight_ref[start : start + depth, columns], preferred_element_type=F32
        )
        for ref in so_far:
            part = part + ref[:, columns]
        out_ref[:, columns] = part


def down_kernel(tile, *refs):
    pieces, (weight_ref, so_far_ref, own_ref) = refs[:4], refs[4:7]
    sends, rows_ref = refs[7:-1], refs[-1]
    gather_rows(pieces, rows_ref)
    rows = pieces[0].shape[0]
    depth = rows_ref.shape[1]
    start = weight_ref.shape[0] - depth
    for at in range(0, weight_ref.shape[1], tile):
        columns = slice(at, at + tile)
        part = so_far_ref[:, columns] + jnp.dot(
            rows_ref[...], weight_ref[start:, columns], preferred_element_type=F32
        )
        own_ref[:, columns] = part[:rows]
        for n, send in enumerate(sends):
            send[:, columns] = part[(n + 1) * rows : (n + 2) * rows].astype(send.dtype)


def add_kernel(own_ref, got_ref, out_ref):
    out_ref[...] = (own_ref[...] + got_ref[...].astype(F32)).astype(BF16)


def final_kernel(middle_ref, own_ref, *refs):
    parts, out_ref = refs[:-1], refs[-1]
    total = own_ref[...]
    for part in parts:
        total = total + part[...].astype(F32)
    out_ref[...] = (middle_ref[...].astype(F32) + total).astype(BF16)


def swap(x, axis):
    return lax.ppermute(x, axis, [(0, 1), (1, 0)])


def turn(x, axis, n, offset):
    return lax.ppermute(x, axis, [(i, i ^ offset) for i in range(n)])


def direct_body(
    queries,
    key_cache,
    value_cache,
    block_index,
    stream,
    out_weight,
    norm_gain,
    gate_weight,
    up_weight,
    down_weight,
):
    n_context, n_head, _ = (lax.axis_size(a) for a in ALL)
    rows, heads_width = queries.shape
    context_len = key_cache.shape[0] * n_context
    model = norm_gain.shape[0]
    total = rows * n_context
    blocks = key_cache.shape[0] // KB
    kv_width = key_cache.shape[1]
    order = (3, 2, 1)

    got_q = {m: turn(queries, CTX, n_context, m) for m in (2, 1)}
    got_q[3] = turn(got_q[2], CTX, n_context, 1)
    picked = struct((MOST * KB, kv_width), BF16)
    partial_out = struct((rows, heads_width + LANES), BF16)
    kv_dev = kv_width // DH
    tall = heads_width // kv_width * rows
    scratch = [
        pltpu.VMEM((kv_dev, tall, MOST * KB), F32),
        pltpu.VMEM((kv_dev, tall, MOST * KB), BF16),
    ]
    keys, values, starts, own_partial = call(
        functools.partial(first_attend_kernel, blocks, context_len - total),
        (picked, picked, struct((8, LANES), jnp.int32), partial_out),
        [SM, ANY, ANY, ANY],
        (block_index, in_hbm(queries), in_hbm(key_cache), in_hbm(value_cache)),
        scratch=[pltpu.VMEM((rows, heads_width), BF16)]
        + scratch
        + [pltpu.SemaphoreType.DMA((2, MOST)), pltpu.SemaphoreType.DMA],
    )
    partial = {0: own_partial}
    for m in order:
        partial[m] = call(
            functools.partial(attend, m, context_len - total),
            partial_out,
            [VM] * 4,
            (starts, got_q[m], keys, values),
            scratch=scratch,
        )
    back = {m: turn(partial[m], CTX, n_context, m) for m in order}
    back[0] = partial[0]
    blended = call(
        blend_kernel, struct((rows, heads_width), BF16), [VM] * 4, tuple(back[m] for m in range(4))
    )

    attention = {m: turn(blended, CTX, n_context, m) for m in (2, 1)}
    attention[3] = turn(attention[2], CTX, n_context, 1)
    attention[0] = blended
    width = out_weight.shape[1]
    keep, away = call(
        functools.partial(project_kernel, 512),
        (struct((n_head * rows, width), F32), struct((n_head * rows, width), BF16)),
        [VM] * 5,
        tuple(attention[m] for m in range(4)) + (in_vmem(out_weight),),
        scratch=[pltpu.VMEM((total, heads_width), BF16)],
        cost=6,
    )
    got = swap(away, SEC)
    keep, away = call(
        functools.partial(fold_kernel, width),
        (struct((rows, width), F32), struct((rows, width), BF16)),
        [VM, VM],
        (keep, got),
        cost=6,
    )
    got = swap(away, HEAD)
    middle = call(middle_kernel, struct((rows, width), BF16), [VM] * 3, (stream, keep, got), cost=6)

    all_middle = {
        m: lax.ppermute(
            middle,
            ALL,
            [
                (a * n_context + b, (b ^ m) * n_context + a)
                for a in range(n_context)
                for b in range(n_context)
            ],
        )
        for m in (3, 0, 1, 2)
    }
    hidden_width = gate_weight.shape[1]
    first = hidden_width * 2 // 7 // (2 * LANES) * 2 * LANES
    second = (hidden_width - first) // 2 // LANES * LANES
    widths = (first, second, hidden_width - first - second)
    chunks = tuple((sum(widths[:c]), widths[c]) for c in range(len(widths)))
    hidden = []
    gate_vmem, up_vmem = in_vmem(gate_weight), in_vmem(up_weight)
    prepared = [
        call(
            prepare_kernel,
            (struct((rows, width), BF16), struct((rows, LANES), F32)),
            [VM, VM],
            (all_middle[m], norm_gain[None]),
            cost=0,
        )
        for m in range(4)
    ]
    scale = None
    for c, (start, chunk) in enumerate(chunks):
        extra = LANES if c == 0 else 0
        out = (
            struct((n_head * rows, 2 * chunk + extra), F32),
            struct((n_head * rows, 2 * chunk + 2 * extra), BF16),
        )
        if c == 0:
            keep, away, all_rows = call(
                functools.partial(first_gate_kernel, chunk, 512),
                out + (struct((total, width), BF16),),
                [VM] * 10,
                tuple(p[0] for p in prepared)
                + tuple(p[1] for p in prepared)
                + (gate_vmem, up_vmem),
            )
        else:
            keep, away = call(
                functools.partial(gate_kernel, start, chunk, 512),
                out,
                [VM] * 3,
                (all_rows, gate_vmem, up_vmem),
            )
        keep, away = call(
            functools.partial(fold_kernel, 2 * chunk),
            (
                struct((rows, 2 * chunk + extra), F32),
                struct((rows, 2 * chunk + 2 * extra), BF16),
            ),
            [VM, VM],
            (keep, swap(away, SEC)),
        )
        got = swap(away, HEAD)
        if c == 0:
            own, scale = call(
                functools.partial(first_hidden_kernel, model),
                (struct((rows, chunk), BF16), struct((rows, LANES), F32)),
                [VM] * 2,
                (keep, got),
            )
        else:
            own = call(hidden_kernel, struct((rows, chunk), BF16), [VM] * 3, (scale, keep, got))
        across = swap(own, HEAD)
        beside = swap(own, SEC)
        hidden.append((own, beside, across, swap(across, SEC)))
    out_width = down_weight.shape[1]
    down_vmem = in_vmem(down_weight)
    so_far = ()
    for c, (start, chunk) in enumerate(chunks[:-1]):
        so_far = (
            call(
                functools.partial(part_down_kernel, 512, start),
                struct((total, out_width), F32),
                [VM] * (5 + len(so_far)),
                hidden[c] + (down_vmem,) + so_far,
                scratch=[pltpu.VMEM((total, chunk), BF16)],
            ),
        )
    res = call(
        functools.partial(down_kernel, 512),
        tuple(struct((rows, out_width), t) for t in (F32, BF16, F32, BF16)),
        [VM] * 6,
        hidden[-1] + (down_vmem,) + so_far,
        scratch=[pltpu.VMEM((total, chunks[-1][1]), BF16)],
    )
    beside = turn(res[3], CTX, n_context, 1)
    near = turn(res[1], CTX, n_context, 1)
    pair = call(add_kernel, struct((rows, out_width), BF16), [VM] * 2, (res[2], beside))
    far = turn(pair, CTX, n_context, 2)
    return call(
        final_kernel, struct((rows, out_width), BF16), [VM] * 4, (all_middle[0], res[0], near, far)
    )


def local_attention(gathered, key_cache, value_cache, block_index, context_index, context_len):
    group_size = HQ // KVH
    kv_dev = key_cache.shape[1] // DH
    blocks_dev = key_cache.shape[0] // KB
    total_tokens = gathered.shape[0]
    key_blocks = key_cache.reshape(blocks_dev, KB, kv_dev, DH)
    value_blocks = value_cache.reshape(blocks_dev, KB, kv_dev, DH)
    local_ids = context_index * blocks_dev + jnp.arange(blocks_dev, dtype=jnp.int32)
    member = jnp.any(block_index[:, :, None] == local_ids[None, None, :], axis=1)
    member_rank = jnp.cumsum(member.astype(jnp.int32), axis=1) - 1
    slot_hit = member[:, None, :] & (
        member_rank[:, None, :] == jnp.arange(MOST, dtype=jnp.int32)[None, :, None]
    )
    slot_block = jnp.sum(
        jnp.where(slot_hit, jnp.arange(blocks_dev, dtype=jnp.int32)[None, None, :], 0), axis=2
    )
    slot_valid = jnp.any(slot_hit, axis=2)
    picked_keys = jnp.take(key_blocks, slot_block[0], axis=0).reshape(MOST * KB, kv_dev, DH)
    picked_values = jnp.take(value_blocks, slot_block[0], axis=0).reshape(MOST * KB, kv_dev, DH)
    key_pos = (
        (local_ids[0] + slot_block[0])[:, None] * KB + jnp.arange(KB, dtype=jnp.int32)[None, :]
    ).reshape(-1)
    live_keys = jnp.broadcast_to(slot_valid[0][:, None], (MOST, KB)).reshape(-1)
    query_pos = context_len - total_tokens + jnp.arange(KB, dtype=jnp.int32)
    allowed = live_keys[None, :] & (key_pos[None, :] <= query_pos[:, None])
    query_block = gathered.reshape(KB, kv_dev, group_size, DH)
    scores = jnp.einsum(
        "qhgd,phd->hgqp", query_block, picked_keys, preferred_element_type=jnp.float32
    ) / math.sqrt(DH)
    scores = jnp.where(allowed[None, None], scores, -jnp.inf)
    peak_score = jnp.max(scores, axis=-1, keepdims=True)
    unnormed = jnp.exp(scores - peak_score)
    row_total = jnp.sum(unnormed, axis=-1)
    mixture = jnp.einsum(
        "hgqp,phd->qhgd",
        unnormed.astype(jnp.bfloat16),
        picked_values,
        preferred_element_type=jnp.float32,
    )
    result = mixture / jnp.transpose(row_total, (2, 0, 1))[..., None]
    log_total = jnp.transpose(peak_score[..., 0] + jnp.log(row_total), (2, 0, 1))
    out_list = result.reshape(KB, -1)
    lse_list = log_total.reshape(KB, -1)
    return (out_list, lse_list)


def general_body(
    queries,
    key_cache,
    value_cache,
    block_index,
    stream,
    out_weight,
    norm_gain,
    gate_weight,
    up_weight,
    down_weight,
):
    n_context = lax.axis_size(CTX)
    context_index = lax.axis_index(CTX)
    context_len = key_cache.shape[0] * n_context
    gathered = lax.all_gather(queries, CTX, axis=0, tiled=True)
    part_out, part_lse = local_attention(
        gathered, key_cache, value_cache, block_index, context_index, context_len
    )
    spread_out, spread_lse = (
        lax.all_to_all(part_out[:, None, :], CTX, split_axis=0, concat_axis=1, tiled=True),
        lax.all_to_all(part_lse[:, None, :], CTX, split_axis=0, concat_axis=1, tiled=True),
    )
    share_rows = spread_out.shape[0]
    head_count = spread_lse.shape[2]
    peak_value = jnp.max(spread_lse, axis=1, keepdims=True)
    share_weight = jnp.exp(spread_lse - peak_value)
    blended = jnp.sum(
        spread_out.reshape(share_rows, n_context, head_count, -1) * share_weight[..., None], axis=1
    )
    blended = blended / jnp.sum(share_weight, axis=1)[..., None]
    attention = lax.all_gather(
        blended.reshape(share_rows, -1).astype(jnp.bfloat16), CTX, axis=0, tiled=True
    )
    row_piece = attention
    projected = lax.psum_scatter(
        jnp.dot(row_piece, out_weight, preferred_element_type=jnp.float32),
        HS,
        scatter_dimension=0,
        tiled=True,
    )
    middle = (stream.astype(jnp.float32) + projected).astype(jnp.bfloat16)
    full_middle = lax.all_gather(middle, CTX, axis=1, tiled=True)
    middle_wide = full_middle.astype(jnp.float32)
    mean_square = jnp.mean(middle_wide * middle_wide, axis=-1, keepdims=True)
    normed = (middle_wide * lax.rsqrt(mean_square + 1e-05) * norm_gain).astype(jnp.bfloat16)
    normed_cols, middle_cols = (
        lax.all_to_all(normed, HS, split_axis=1, concat_axis=0, tiled=True),
        lax.all_to_all(full_middle, HS, split_axis=1, concat_axis=0, tiled=True),
    )
    row_piece = normed_cols
    gate_up = lax.psum_scatter(
        jnp.concatenate(
            [
                jnp.dot(row_piece, gate_weight, preferred_element_type=jnp.float32),
                jnp.dot(row_piece, up_weight, preferred_element_type=jnp.float32),
            ],
            axis=1,
        ),
        HS,
        scatter_dimension=0,
        tiled=True,
    )
    hidden_width = gate_weight.shape[1]
    hidden = (jax.nn.silu(gate_up[:, :hidden_width]) * gate_up[:, hidden_width:]).astype(
        jnp.bfloat16
    )
    all_hidden = lax.all_gather(hidden, HS, axis=0, tiled=True)
    row_piece = all_hidden
    down_part = lax.psum_scatter(
        jnp.dot(row_piece, down_weight, preferred_element_type=jnp.float32),
        CTX,
        scatter_dimension=0,
        tiled=True,
    )
    own_middle = lax.dynamic_slice_in_dim(
        middle_cols, context_index * down_part.shape[0], down_part.shape[0], 0
    )
    return (own_middle.astype(jnp.float32) + down_part).astype(jnp.bfloat16)


def solution(mesh):
    size = dict(mesh.shape)
    direct = size[CTX] == 4 and size[HEAD] == 2 and size[SEC] == 2
    return jax.shard_map(
        direct_body if direct else general_body,
        mesh=mesh,
        in_specs=(
            P(ROWS, HS),
            P(ROWS, HS),
            P(ROWS, HS),
            P("groups", None),
            P(("groups",) + HS, CTX),
            P(HS, CTX),
            P(),
            P(HS, CTX),
            P(HS, CTX),
            P(CTX, HS),
        ),
        out_specs=P(ROWS, HS),
        check_vma=False,
    )
```

```python
import functools
import math

import jax
import jax.numpy as jnp
from jax import lax
from jax.experimental import pallas as pl
from jax.experimental.pallas import tpu as pltpu
from jax.sharding import PartitionSpec as P


HQ = 64
KVH = 8
DH = 128
KB = 128
MOST = 4
LANES = 128
EPS = 1e-05
CTX, HEAD, SEC = "ctx", "head", "sec"
ALL = (CTX, HEAD, SEC)
HS = (HEAD, SEC)
ROWS = ("groups", CTX)


VM = pl.BlockSpec(memory_space=pltpu.VMEM)
SM = pl.BlockSpec(memory_space=pltpu.SMEM)
ANY = pl.BlockSpec(memory_space=pl.ANY)
F32 = jnp.float32
BF16 = jnp.bfloat16


def struct(shape, dtype):
    return jax.ShapeDtypeStruct(shape, dtype)


def call(kernel, out, in_specs, args, cost=3, scratch=(), vmem=8):
    outs = out if isinstance(out, (tuple, list)) else (out,)
    nbytes = sum(math.prod(a.shape) * a.dtype.itemsize for a in args)
    nbytes += sum(math.prod(o.shape) * o.dtype.itemsize for o in outs)
    return pl.pallas_call(
        kernel,
        out_shape=out,
        in_specs=in_specs,
        out_specs=jax.tree.map(lambda _: VM, out),
        scratch_shapes=scratch,
        compiler_params=pltpu.CompilerParams(vmem_limit_bytes=vmem << 20),
        cost_estimate=pl.CostEstimate(flops=cost * 10**9, bytes_accessed=nbytes, transcendentals=0),
    )(*args)


def in_vmem(x):
    return pltpu.with_memory_space_constraint(x, pltpu.VMEM)


def in_hbm(x):
    return pltpu.with_memory_space_constraint(x, pltpu.HBM)


def slots(index_ref, blocks):
    entries = index_ref.shape[1]
    base = lax.axis_index(CTX) * blocks
    first = jnp.int32(0)
    end = jnp.int32(0)
    for n in range(entries):
        block = index_ref[0, n]
        first += (block < base).astype(jnp.int32)
        end += (block < base + blocks).astype(jnp.int32)
    found = []
    for slot in range(MOST):
        entry = jnp.minimum(first + slot, entries - 1)
        local = jnp.clip(index_ref[0, entry] - base, 0, blocks - 1)
        found.append((local, first + slot < end))
    return found


def attend(offset, first_token, start_ref, q_ref, key_ref, value_ref, out_ref, score_ref, weight_ref):
    rows = q_ref.shape[0]
    heads = q_ref.shape[1] // DH
    kv_dev = key_ref.shape[1] // DH
    group = heads // kv_dev
    scale = 1.0 / math.sqrt(DH)
    token0 = first_token + (lax.axis_index(CTX) ^ offset) * rows
    ahead = (
        lax.broadcasted_iota(jnp.int32, (rows, KB), 1)
        - lax.broadcasted_iota(jnp.int32, (rows, KB), 0)
        - token0
    )
    allowed = [ahead + start_ref[slot : slot + 1, :] <= 0 for slot in range(MOST)]
    head_lane = lax.broadcasted_iota(jnp.int32, (rows, LANES), 1)
    peak_tile = jnp.zeros((rows, LANES), F32)
    total_tile = jnp.ones((rows, LANES), F32)
    for kv in range(kv_dev):
        stacked = jnp.concatenate(
            [q_ref[:, (kv * group + h) * DH : (kv * group + h + 1) * DH] for h in range(group)], axis=0
        )
        score_ref[kv] = lax.dot_general(
            stacked,
            key_ref[:, kv * DH : (kv + 1) * DH],
            (((1,), (1,)), ((), ())),
            preferred_element_type=F32,
        )
    for kv in range(kv_dev):
        for h in range(group):
            head = kv * group + h
            span = slice(h * rows, (h + 1) * rows)
            parts = [
                jnp.where(allowed[slot], score_ref[kv, span, slot * KB : (slot + 1) * KB], -1e30)
                for slot in range(MOST)
            ]
            peak = jnp.max(functools.reduce(jnp.maximum, parts), axis=1, keepdims=True)
            parts = [jnp.exp((p - peak) * scale) for p in parts]
            row_total = jnp.sum(functools.reduce(jnp.add, parts), axis=1, keepdims=True)
            for slot, p in enumerate(parts):
                weight_ref[kv, span, slot * KB : (slot + 1) * KB] = p.astype(BF16)
            peak_tile = jnp.where(head_lane == head, peak, peak_tile)
            total_tile = jnp.where(head_lane == head, row_total, total_tile)
    inverse = 1.0 / total_tile
    for kv in range(kv_dev):
        mixture = jnp.dot(
            weight_ref[kv], value_ref[:, kv * DH : (kv + 1) * DH], preferred_element_type=F32
        )
        for h in range(group):
            head = kv * group + h
            out_ref[:, head * DH : (head + 1) * DH] = (
                mixture[h * rows : (h + 1) * rows] * inverse[:, head : head + 1]
            ).astype(BF16)
    lse_tile = peak_tile * scale + jnp.log(total_tile)
    high = lse_tile.astype(BF16).astype(F32)
    rest = lse_tile - high
    mid = rest.astype(BF16).astype(F32)
    low = rest - mid
    tile = high + pltpu.roll(mid, heads, 1) + pltpu.roll(low, 2 * heads, 1)
    out_ref[:, heads * DH :] = tile.astype(BF16)


def first_attend_kernel(
    blocks, first_token, index_ref, q_hbm, key_hbm, value_hbm,
    key_ref, value_ref, start_ref, out_ref, q_ref, score_ref, weight_ref, sems, q_sem,
):
    copies = [pltpu.make_async_copy(q_hbm, q_ref, q_sem)]
    found = slots(index_ref, blocks)
    for slot, (local, _) in enumerate(found):
        rows = pl.ds(pl.multiple_of(local * KB, KB), KB)
        for n, (src, dst) in enumerate(((key_hbm, key_ref), (value_hbm, value_ref))):
            copies.append(
                pltpu.make_async_copy(
                    src.at[rows, :], dst.at[slot * KB : (slot + 1) * KB, :], sems.at[n, slot]
                )
            )
    for copy in copies:
        copy.start()
    row = lax.broadcasted_iota(jnp.int32, start_ref.shape, 0)
    starts = jnp.zeros(start_ref.shape, jnp.int32)
    base = lax.axis_index(CTX) * blocks
    for slot, (local, valid) in enumerate(found):
        starts = jnp.where(row == slot, jnp.where(valid, (base + local) * KB, jnp.int32(1 << 29)), starts)
    start_ref[...] = starts
    for copy in copies:
        copy.wait()
    attend(0, first_token, start_ref, q_ref, key_ref, value_ref, out_ref, score_ref, weight_ref)


def blend_kernel(*refs):
    parts, (out_ref, low_ref, high_ref) = refs[:-3], refs[-3:]
    heads = out_ref.shape[1] // DH
    logs = []
    for part in parts:
        tile = part[:, heads * DH :].astype(F32)
        logs.append(
            tile + pltpu.roll(tile, LANES - heads, 1) + pltpu.roll(tile, LANES - 2 * heads, 1)
        )
    peak = functools.reduce(jnp.maximum, logs)
    shares = [jnp.exp(log - peak) for log in logs]
    total = functools.reduce(jnp.add, shares)
    shares = [share / total for share in shares]
    for head in range(heads):
        span = slice(head * DH, (head + 1) * DH)
        value = functools.reduce(
            jnp.add,
            [share[:, head : head + 1] * part[:, span].astype(F32) for share, part in zip(shares, parts)],
        ).astype(BF16)
        out_ref[:, span] = value
        at = head * DH % low_ref.shape[1]
        (low_ref if head * 2 < heads else high_ref)[:, at : at + DH] = value


def place():
    return lax.axis_index(HEAD) * lax.axis_size(SEC) + lax.axis_index(SEC)


def place_of(n, rows, count):
    n_sec = lax.axis_size(SEC)
    owner = lax.axis_index(CTX) ^ n
    other = ((owner % n_sec) != lax.axis_index(SEC)).astype(jnp.int32)
    return pl.multiple_of(other * (count // n_sec * rows) + owner // n_sec * rows, rows)


def product(rows_ref, weight_ref, source, keep_ref, send_ref, target, width, tile):
    half = rows_ref.shape[0] // 2
    for at in range(0, width, tile):
        size = min(tile, width - at)
        part = jnp.dot(
            rows_ref[...],
            weight_ref[:, source + at : source + at + size],
            preferred_element_type=F32,
        )
        keep_ref[:, target + at : target + at + size] = part[:half]
        send_ref[:, target + at : target + at + size] = part[half:].astype(BF16)


def project_kernel(tile, *refs):
    pieces, (weight_ref, keep_ref, send_ref, rows_ref) = refs[:-4], refs[-4:]
    rows = pieces[0].shape[0]
    half = pieces[2].shape[1]
    for n, parts in enumerate((pieces[:1], pieces[1:2], pieces[2:4], pieces[4:6])):
        at = pl.ds(place_of(n, rows, 4), rows)
        for i, part in enumerate(parts):
            rows_ref[at, i * half : i * half + part.shape[1]] = part[...]
    product(rows_ref, weight_ref, 0, keep_ref, send_ref, 0, weight_ref.shape[1], tile)


def fold_kernel(width, keep_ref, got_ref, keep_out, send_out):
    rows = keep_out.shape[0]
    head = lax.axis_index(HEAD)
    mine = pl.ds(pl.multiple_of(head * rows, rows), rows)
    other = pl.ds(pl.multiple_of((1 - head) * rows, rows), rows)
    keep_out[:, :width] = keep_ref[mine, :width] + got_ref[mine, :width].astype(F32)
    send_out[:, :width] = (keep_ref[other, :width] + got_ref[other, :width].astype(F32)).astype(BF16)
    if keep_ref.shape[1] > width:
        keep_out[:, width:] = keep_ref[mine, width:] + take_exact(got_ref[mine, width:])
        put_exact(send_out, slice(None), width, keep_ref[other, width:] + take_exact(got_ref[other, width:]))


def middle_kernel(stream_ref, keep_ref, got_ref, out_ref):
    out_ref[...] = (
        stream_ref[...].astype(F32) + (keep_ref[...] + got_ref[...].astype(F32))
    ).astype(BF16)


def put_exact(ref, rows, at, value):
    high = value.astype(BF16)
    ref[rows, at : at + LANES] = high
    ref[rows, at + LANES : at + 2 * LANES] = (value - high.astype(F32)).astype(BF16)


def take_exact(tile):
    return tile[:, :LANES].astype(F32) + tile[:, LANES:].astype(F32)


def prepare_kernel(piece_ref, gain_ref, row_ref, square_ref):
    model = piece_ref.shape[1]
    gain = gain_ref[:, pl.ds(pl.multiple_of(place() * model, model), model)]
    wide = piece_ref[...].astype(F32)
    row_ref[...] = (wide * gain).astype(BF16)
    square_ref[...] = jnp.broadcast_to(jnp.sum(wide * wide, axis=1, keepdims=True), square_ref.shape)


def first_gate_kernel(width, tile, *refs):
    pieces, squares = refs[:4], refs[4:8]
    gate_ref, up_ref, keep_ref, send_ref, rows_ref = refs[8:]
    rows = pieces[0].shape[0]
    half = rows_ref.shape[0] // 2
    for n, (piece, square) in enumerate(zip(pieces, squares)):
        at = place_of(n, rows, len(pieces))
        rows_ref[pl.ds(at, rows), :] = piece[...]

        @pl.when(at < half)
        def _():
            keep_ref[pl.ds(at, rows), 2 * width :] = square[...]

        @pl.when(at >= half)
        def _():
            put_exact(send_ref, pl.ds(pl.multiple_of(at - half, rows), rows), 2 * width, square[...])

    product(rows_ref, gate_ref, 0, keep_ref, send_ref, 0, width, tile)
    product(rows_ref, up_ref, 0, keep_ref, send_ref, width, width, tile)


def gate_kernel(start, width, tile, rows_ref, gate_ref, up_ref, keep_ref, send_ref):
    product(rows_ref, gate_ref, start, keep_ref, send_ref, 0, width, tile)
    product(rows_ref, up_ref, start, keep_ref, send_ref, width, width, tile)


def scale_kernel(model, keep_ref, got_ref, out_ref):
    at = keep_ref.shape[1] - LANES
    square = keep_ref[:, at:] + take_exact(got_ref[:, at:])
    out_ref[...] = lax.rsqrt(square / model + EPS)


def hidden_kernel(scale_ref, keep_ref, got_ref, out_ref):
    width = out_ref.shape[1]
    scale = scale_ref[...]
    for at in range(0, width, LANES):
        gate = keep_ref[:, at : at + LANES] + got_ref[:, at : at + LANES].astype(F32)
        up = keep_ref[:, width + at : width + at + LANES] + got_ref[
            :, width + at : width + at + LANES
        ].astype(F32)
        gate = gate * scale
        out_ref[:, at : at + LANES] = (
            gate / (1.0 + jnp.exp(-gate)) * (up * scale)
        ).astype(BF16)


def first_hidden_kernel(model, keep_ref, got_ref, out_ref, scale_ref):
    scale_kernel(model, keep_ref, got_ref, scale_ref)
    hidden_kernel(scale_ref, keep_ref, got_ref, out_ref)


def gather_rows(pieces, rows_ref):
    rows = pieces[0].shape[0]
    for n, piece in enumerate(pieces):
        at = pl.ds(pl.multiple_of((lax.axis_index(CTX) ^ place() ^ n) * rows, rows), rows)
        rows_ref[at, :] = piece[...]


def part_down_kernel(tile, start, *refs):
    pieces, weight_ref, so_far = refs[:4], refs[4], refs[5:-2]
    out_ref, rows_ref = refs[-2:]
    gather_rows(pieces, rows_ref)
    depth = rows_ref.shape[1]
    for at in range(0, weight_ref.shape[1], tile):
        columns = slice(at, at + tile)
        part = jnp.dot(
            rows_ref[...], weight_ref[start : start + depth, columns], preferred_element_type=F32
        )
        for ref in so_far:
            part = part + ref[:, columns]
        out_ref[:, columns] = part


def down_kernel(tile, first, *refs):
    pieces, (weight_ref, so_far_ref) = refs[:4], refs[4:6]
    given, (own_ref, *sends, rows_ref) = refs[6:-5], refs[-5:]
    for ref in given:
        sends[0][:, :first] = ref[...]
    gather_rows(pieces, rows_ref)
    rows = pieces[0].shape[0]
    depth = rows_ref.shape[1]
    start = weight_ref.shape[0] - depth
    for at in range(0, own_ref.shape[1], tile):
        source = slice(first + at, first + at + tile)
        target = slice(at, at + tile)
        part = so_far_ref[:, source] + jnp.dot(
            rows_ref[...], weight_ref[start:, source], preferred_element_type=F32
        )
        own_ref[:, target] = part[:rows]
        for n, send in enumerate(sends):
            place_at = source if send.shape[1] > own_ref.shape[1] else target
            send[:, place_at] = part[(n + 1) * rows : (n + 2) * rows].astype(send.dtype)


def add_kernel(own_ref, got_ref, out_ref):
    out_ref[...] = (own_ref[...] + got_ref[...].astype(F32)).astype(BF16)


def final_kernel(middle_ref, near_ref, *refs):
    owns, fars, out_ref = refs[:2], refs[2:4], refs[4]
    start = 0
    for own, far in zip(owns, fars):
        columns = slice(start, start + own.shape[1])
        total = own[...] + near_ref[:, columns].astype(F32) + far[...].astype(F32)
        out_ref[:, columns] = (middle_ref[:, columns].astype(F32) + total).astype(BF16)
        start += own.shape[1]


def swap(x, axis):
    return lax.ppermute(x, axis, [(0, 1), (1, 0)])


def turn(x, axis, n, offset):
    return lax.ppermute(x, axis, [(i, i ^ offset) for i in range(n)])


def direct_body(
    queries,
    key_cache,
    value_cache,
    block_index,
    stream,
    out_weight,
    norm_gain,
    gate_weight,
    up_weight,
    down_weight,
):
    n_context, n_head, _ = (lax.axis_size(a) for a in ALL)
    rows, heads_width = queries.shape
    context_len = key_cache.shape[0] * n_context
    model = norm_gain.shape[0]
    total = rows * n_context
    blocks = key_cache.shape[0] // KB
    kv_width = key_cache.shape[1]
    order = (3, 2, 1)

    got_q = {m: turn(queries, CTX, n_context, m) for m in (2, 1)}
    got_q[3] = turn(got_q[2], CTX, n_context, 1)
    picked = struct((MOST * KB, kv_width), BF16)
    partial_out = struct((rows, heads_width + LANES), BF16)
    kv_dev = kv_width // DH
    tall = heads_width // kv_width * rows
    scratch = [
        pltpu.VMEM((kv_dev, tall, MOST * KB), F32),
        pltpu.VMEM((kv_dev, tall, MOST * KB), BF16),
    ]
    keys, values, starts, own_partial = call(
        functools.partial(first_attend_kernel, blocks, context_len - total),
        (picked, picked, struct((8, LANES), jnp.int32), partial_out),
        [SM, ANY, ANY, ANY],
        (block_index, in_hbm(queries), in_hbm(key_cache), in_hbm(value_cache)),
        scratch=[pltpu.VMEM((rows, heads_width), BF16)]
        + scratch
        + [pltpu.SemaphoreType.DMA((2, MOST)), pltpu.SemaphoreType.DMA],
    )
    partial = {0: own_partial}
    for m in order:
        partial[m] = call(
            functools.partial(attend, m, context_len - total),
            partial_out,
            [VM] * 4,
            (starts, got_q[m], keys, values),
            scratch=scratch,
        )
    back = {m: turn(partial[m], CTX, n_context, m) for m in order}
    back[0] = partial[0]
    low = struct((rows, heads_width // 2), BF16)
    blended, *halves = call(
        blend_kernel,
        (struct((rows, heads_width), BF16), low, low),
        [VM] * 4,
        tuple(back[m] for m in range(4)),
    )

    beside = turn(blended, CTX, n_context, 1)
    across = [turn(h, CTX, n_context, 2) for h in halves]
    relayed = [turn(h, CTX, n_context, 1) for h in across]
    attention = (blended, beside, *across, *relayed)
    width = out_weight.shape[1]
    keep, away = call(
        functools.partial(project_kernel, 512),
        (struct((n_head * rows, width), F32), struct((n_head * rows, width), BF16)),
        [VM] * 7,
        attention + (in_vmem(out_weight),),
        scratch=[pltpu.VMEM((total, heads_width), BF16)],
        cost=6,
    )
    got = swap(away, SEC)
    keep, away = call(
        functools.partial(fold_kernel, width),
        (struct((rows, width), F32), struct((rows, width), BF16)),
        [VM, VM],
        (keep, got),
        cost=6,
    )
    got = swap(away, HEAD)
    middle = call(middle_kernel, struct((rows, width), BF16), [VM] * 3, (stream, keep, got), cost=6)

    all_middle = {
        m: lax.ppermute(
            middle,
            ALL,
            [
                (a * n_context + b, (b ^ m) * n_context + a)
                for a in range(n_context)
                for b in range(n_context)
            ],
        )
        for m in (3, 0, 1, 2)
    }
    hidden_width = gate_weight.shape[1]
    first = hidden_width * 2 // 7 // (2 * LANES) * 2 * LANES
    second = (hidden_width - first) // 2 // LANES * LANES
    widths = (first, second, hidden_width - first - second)
    chunks = tuple((sum(widths[:c]), widths[c]) for c in range(len(widths)))
    hidden = []
    gate_vmem, up_vmem = in_vmem(gate_weight), in_vmem(up_weight)
    prepared = [
        call(
            prepare_kernel,
            (struct((rows, width), BF16), struct((rows, LANES), F32)),
            [VM, VM],
            (all_middle[m], norm_gain[None]),
            cost=0,
        )
        for m in range(4)
    ]
    scale = None
    for c, (start, chunk) in enumerate(chunks):
        extra = LANES if c == 0 else 0
        out = (
            struct((n_head * rows, 2 * chunk + extra), F32),
            struct((n_head * rows, 2 * chunk + 2 * extra), BF16),
        )
        if c == 0:
            keep, away, all_rows = call(
                functools.partial(first_gate_kernel, chunk, 512),
                out + (struct((total, width), BF16),),
                [VM] * 10,
                tuple(p[0] for p in prepared)
                + tuple(p[1] for p in prepared)
                + (gate_vmem, up_vmem),
            )
        else:
            keep, away = call(
                functools.partial(gate_kernel, start, chunk, 512),
                out,
                [VM] * 3,
                (all_rows, gate_vmem, up_vmem),
            )
        keep, away = call(
            functools.partial(fold_kernel, 2 * chunk),
            (
                struct((rows, 2 * chunk + extra), F32),
                struct((rows, 2 * chunk + 2 * extra), BF16),
            ),
            [VM, VM],
            (keep, swap(away, SEC)),
        )
        got = swap(away, HEAD)
        if c == 0:
            own, scale = call(
                functools.partial(first_hidden_kernel, model),
                (struct((rows, chunk), BF16), struct((rows, LANES), F32)),
                [VM] * 2,
                (keep, got),
            )
        else:
            own = call(hidden_kernel, struct((rows, chunk), BF16), [VM] * 3, (scale, keep, got))
        across = swap(own, HEAD)
        beside = swap(own, SEC)
        hidden.append((own, beside, across, swap(across, SEC)))
    out_width = down_weight.shape[1]
    down_vmem = in_vmem(down_weight)
    so_far = ()
    for c, (start, chunk) in enumerate(chunks[:-1]):
        so_far = (
            call(
                functools.partial(part_down_kernel, 512, start),
                struct((total, out_width), F32),
                [VM] * (5 + len(so_far)),
                hidden[c] + (down_vmem,) + so_far,
                scratch=[pltpu.VMEM((total, chunk), BF16)],
            ),
        )
    half = out_width // 2
    owns, fars = [], []
    near = ()
    for n in range(2):
        own, beside, two, three = call(
            functools.partial(down_kernel, 512, n * half),
            tuple(
                struct((rows, w), t)
                for w, t in ((half, F32), ((n + 1) * half, BF16), (half, F32), (half, BF16))
            ),
            [VM] * (6 + n),
            hidden[-1] + (down_vmem,) + so_far + near,
            scratch=[pltpu.VMEM((total, chunks[-1][1]), BF16)],
        )
        near = (beside,)
        pair = call(
            add_kernel, struct((rows, half), BF16), [VM] * 2, (two, turn(three, CTX, n_context, 1))
        )
        owns.append(own)
        fars.append(turn(pair, CTX, n_context, 2))
    return call(
        final_kernel,
        struct((rows, out_width), BF16),
        [VM] * 6,
        (all_middle[0], turn(near[0], CTX, n_context, 1), *owns, *fars),
    )


def local_attention(gathered, key_cache, value_cache, block_index, context_index, context_len):
    group_size = HQ // KVH
    kv_dev = key_cache.shape[1] // DH
    blocks_dev = key_cache.shape[0] // KB
    total_tokens = gathered.shape[0]
    key_blocks = key_cache.reshape(blocks_dev, KB, kv_dev, DH)
    value_blocks = value_cache.reshape(blocks_dev, KB, kv_dev, DH)
    local_ids = context_index * blocks_dev + jnp.arange(blocks_dev, dtype=jnp.int32)
    member = jnp.any(block_index[:, :, None] == local_ids[None, None, :], axis=1)
    member_rank = jnp.cumsum(member.astype(jnp.int32), axis=1) - 1
    slot_hit = member[:, None, :] & (
        member_rank[:, None, :] == jnp.arange(MOST, dtype=jnp.int32)[None, :, None]
    )
    slot_block = jnp.sum(
        jnp.where(slot_hit, jnp.arange(blocks_dev, dtype=jnp.int32)[None, None, :], 0), axis=2
    )
    slot_valid = jnp.any(slot_hit, axis=2)
    picked_keys = jnp.take(key_blocks, slot_block[0], axis=0).reshape(MOST * KB, kv_dev, DH)
    picked_values = jnp.take(value_blocks, slot_block[0], axis=0).reshape(MOST * KB, kv_dev, DH)
    key_pos = (
        (local_ids[0] + slot_block[0])[:, None] * KB + jnp.arange(KB, dtype=jnp.int32)[None, :]
    ).reshape(-1)
    live_keys = jnp.broadcast_to(slot_valid[0][:, None], (MOST, KB)).reshape(-1)
    query_pos = context_len - total_tokens + jnp.arange(KB, dtype=jnp.int32)
    allowed = live_keys[None, :] & (key_pos[None, :] <= query_pos[:, None])
    query_block = gathered.reshape(KB, kv_dev, group_size, DH)
    scores = jnp.einsum(
        "qhgd,phd->hgqp", query_block, picked_keys, preferred_element_type=jnp.float32
    ) / math.sqrt(DH)
    scores = jnp.where(allowed[None, None], scores, -jnp.inf)
    peak_score = jnp.max(scores, axis=-1, keepdims=True)
    unnormed = jnp.exp(scores - peak_score)
    row_total = jnp.sum(unnormed, axis=-1)
    mixture = jnp.einsum(
        "hgqp,phd->qhgd",
        unnormed.astype(jnp.bfloat16),
        picked_values,
        preferred_element_type=jnp.float32,
    )
    result = mixture / jnp.transpose(row_total, (2, 0, 1))[..., None]
    log_total = jnp.transpose(peak_score[..., 0] + jnp.log(row_total), (2, 0, 1))
    out_list = result.reshape(KB, -1)
    lse_list = log_total.reshape(KB, -1)
    return (out_list, lse_list)


def general_body(
    queries,
    key_cache,
    value_cache,
    block_index,
    stream,
    out_weight,
    norm_gain,
    gate_weight,
    up_weight,
    down_weight,
):
    n_context = lax.axis_size(CTX)
    context_index = lax.axis_index(CTX)
    context_len = key_cache.shape[0] * n_context
    gathered = lax.all_gather(queries, CTX, axis=0, tiled=True)
    part_out, part_lse = local_attention(
        gathered, key_cache, value_cache, block_index, context_index, context_len
    )
    spread_out, spread_lse = (
        lax.all_to_all(part_out[:, None, :], CTX, split_axis=0, concat_axis=1, tiled=True),
        lax.all_to_all(part_lse[:, None, :], CTX, split_axis=0, concat_axis=1, tiled=True),
    )
    share_rows = spread_out.shape[0]
    head_count = spread_lse.shape[2]
    peak_value = jnp.max(spread_lse, axis=1, keepdims=True)
    share_weight = jnp.exp(spread_lse - peak_value)
    blended = jnp.sum(
        spread_out.reshape(share_rows, n_context, head_count, -1) * share_weight[..., None], axis=1
    )
    blended = blended / jnp.sum(share_weight, axis=1)[..., None]
    attention = lax.all_gather(
        blended.reshape(share_rows, -1).astype(jnp.bfloat16), CTX, axis=0, tiled=True
    )
    row_piece = attention
    projected = lax.psum_scatter(
        jnp.dot(row_piece, out_weight, preferred_element_type=jnp.float32),
        HS,
        scatter_dimension=0,
        tiled=True,
    )
    middle = (stream.astype(jnp.float32) + projected).astype(jnp.bfloat16)
    full_middle = lax.all_gather(middle, CTX, axis=1, tiled=True)
    middle_wide = full_middle.astype(jnp.float32)
    mean_square = jnp.mean(middle_wide * middle_wide, axis=-1, keepdims=True)
    normed = (middle_wide * lax.rsqrt(mean_square + 1e-05) * norm_gain).astype(jnp.bfloat16)
    normed_cols, middle_cols = (
        lax.all_to_all(normed, HS, split_axis=1, concat_axis=0, tiled=True),
        lax.all_to_all(full_middle, HS, split_axis=1, concat_axis=0, tiled=True),
    )
    row_piece = normed_cols
    gate_up = lax.psum_scatter(
        jnp.concatenate(
            [
                jnp.dot(row_piece, gate_weight, preferred_element_type=jnp.float32),
                jnp.dot(row_piece, up_weight, preferred_element_type=jnp.float32),
            ],
            axis=1,
        ),
        HS,
        scatter_dimension=0,
        tiled=True,
    )
    hidden_width = gate_weight.shape[1]
    hidden = (jax.nn.silu(gate_up[:, :hidden_width]) * gate_up[:, hidden_width:]).astype(
        jnp.bfloat16
    )
    all_hidden = lax.all_gather(hidden, HS, axis=0, tiled=True)
    row_piece = all_hidden
    down_part = lax.psum_scatter(
        jnp.dot(row_piece, down_weight, preferred_element_type=jnp.float32),
        CTX,
        scatter_dimension=0,
        tiled=True,
    )
    own_middle = lax.dynamic_slice_in_dim(
        middle_cols, context_index * down_part.shape[0], down_part.shape[0], 0
    )
    return (own_middle.astype(jnp.float32) + down_part).astype(jnp.bfloat16)


def solution(mesh):
    size = dict(mesh.shape)
    direct = size[CTX] == 4 and size[HEAD] == 2 and size[SEC] == 2
    return jax.shard_map(
        direct_body if direct else general_body,
        mesh=mesh,
        in_specs=(
            P(ROWS, HS),
            P(ROWS, HS),
            P(ROWS, HS),
            P("groups", None),
            P(("groups",) + HS, CTX),
            P(HS, CTX),
            P(),
            P(HS, CTX),
            P(HS, CTX),
            P(CTX, HS),
        ),
        out_specs=P(ROWS, HS),
        check_vma=False,
    )
```

```python
import functools
import math

import jax
import jax.numpy as jnp
from jax import lax
from jax.experimental import pallas as pl
from jax.experimental.pallas import tpu as pltpu
from jax.sharding import PartitionSpec as P


HQ = 64
KVH = 8
DH = 128
KB = 128
MOST = 4
LANES = 128
EPS = 1e-05
CTX, HEAD, SEC = "ctx", "head", "sec"
ALL = (CTX, HEAD, SEC)
HS = (HEAD, SEC)
ROWS = ("groups", CTX)


VM = pl.BlockSpec(memory_space=pltpu.VMEM)
SM = pl.BlockSpec(memory_space=pltpu.SMEM)
ANY = pl.BlockSpec(memory_space=pl.ANY)
F32 = jnp.float32
BF16 = jnp.bfloat16


def struct(shape, dtype):
    return jax.ShapeDtypeStruct(shape, dtype)


def call(kernel, out, in_specs, args, cost=3, scratch=(), vmem=8):
    outs = out if isinstance(out, (tuple, list)) else (out,)
    nbytes = sum(math.prod(a.shape) * a.dtype.itemsize for a in args)
    nbytes += sum(math.prod(o.shape) * o.dtype.itemsize for o in outs)
    return pl.pallas_call(
        kernel,
        out_shape=out,
        in_specs=in_specs,
        out_specs=jax.tree.map(lambda _: VM, out),
        scratch_shapes=scratch,
        compiler_params=pltpu.CompilerParams(vmem_limit_bytes=vmem << 20),
        cost_estimate=pl.CostEstimate(flops=cost * 10**9, bytes_accessed=nbytes, transcendentals=0),
    )(*args)


def in_vmem(x):
    return pltpu.with_memory_space_constraint(x, pltpu.VMEM)


def in_hbm(x):
    return pltpu.with_memory_space_constraint(x, pltpu.HBM)


def slots(index_ref, blocks):
    entries = index_ref.shape[1]
    base = lax.axis_index(CTX) * blocks
    first = jnp.int32(0)
    end = jnp.int32(0)
    for n in range(entries):
        block = index_ref[0, n]
        first += (block < base).astype(jnp.int32)
        end += (block < base + blocks).astype(jnp.int32)
    found = []
    for slot in range(MOST):
        entry = jnp.minimum(first + slot, entries - 1)
        local = jnp.clip(index_ref[0, entry] - base, 0, blocks - 1)
        found.append((local, first + slot < end))
    return found


def attend(offset, first_token, start_ref, q_ref, key_ref, value_ref, out_ref, score_ref, weight_ref):
    rows = q_ref.shape[0]
    heads = q_ref.shape[1] // DH
    kv_dev = key_ref.shape[1] // DH
    group = heads // kv_dev
    scale = 1.0 / math.sqrt(DH)
    token0 = first_token + (lax.axis_index(CTX) ^ offset) * rows
    ahead = (
        lax.broadcasted_iota(jnp.int32, (rows, KB), 1)
        - lax.broadcasted_iota(jnp.int32, (rows, KB), 0)
        - token0
    )
    allowed = [ahead + start_ref[slot : slot + 1, :] <= 0 for slot in range(MOST)]
    head_lane = lax.broadcasted_iota(jnp.int32, (rows, LANES), 1)
    peak_tile = jnp.zeros((rows, LANES), F32)
    total_tile = jnp.ones((rows, LANES), F32)
    for kv in range(kv_dev):
        stacked = jnp.concatenate(
            [q_ref[:, (kv * group + h) * DH : (kv * group + h + 1) * DH] for h in range(group)], axis=0
        )
        score_ref[kv] = lax.dot_general(
            stacked,
            key_ref[:, kv * DH : (kv + 1) * DH],
            (((1,), (1,)), ((), ())),
            preferred_element_type=F32,
        )
    for kv in range(kv_dev):
        for h in range(group):
            head = kv * group + h
            span = slice(h * rows, (h + 1) * rows)
            parts = [
                jnp.where(allowed[slot], score_ref[kv, span, slot * KB : (slot + 1) * KB], -1e30)
                for slot in range(MOST)
            ]
            peak = jnp.max(functools.reduce(jnp.maximum, parts), axis=1, keepdims=True)
            parts = [jnp.exp((p - peak) * scale) for p in parts]
            row_total = jnp.sum(functools.reduce(jnp.add, parts), axis=1, keepdims=True)
            for slot, p in enumerate(parts):
                weight_ref[kv, span, slot * KB : (slot + 1) * KB] = p.astype(BF16)
            peak_tile = jnp.where(head_lane == head, peak, peak_tile)
            total_tile = jnp.where(head_lane == head, row_total, total_tile)
    inverse = 1.0 / total_tile
    for kv in range(kv_dev):
        mixture = jnp.dot(
            weight_ref[kv], value_ref[:, kv * DH : (kv + 1) * DH], preferred_element_type=F32
        )
        for h in range(group):
            head = kv * group + h
            out_ref[:, head * DH : (head + 1) * DH] = (
                mixture[h * rows : (h + 1) * rows] * inverse[:, head : head + 1]
            ).astype(BF16)
    lse_tile = peak_tile * scale + jnp.log(total_tile)
    high = lse_tile.astype(BF16).astype(F32)
    rest = lse_tile - high
    mid = rest.astype(BF16).astype(F32)
    low = rest - mid
    tile = high + pltpu.roll(mid, heads, 1) + pltpu.roll(low, 2 * heads, 1)
    out_ref[:, heads * DH :] = tile.astype(BF16)


def first_attend_kernel(
    blocks, first_token, index_ref, q_hbm, key_hbm, value_hbm,
    key_ref, value_ref, start_ref, out_ref, q_ref, score_ref, weight_ref, sems, q_sem,
):
    copies = [pltpu.make_async_copy(q_hbm, q_ref, q_sem)]
    found = slots(index_ref, blocks)
    for slot, (local, _) in enumerate(found):
        rows = pl.ds(pl.multiple_of(local * KB, KB), KB)
        for n, (src, dst) in enumerate(((key_hbm, key_ref), (value_hbm, value_ref))):
            copies.append(
                pltpu.make_async_copy(
                    src.at[rows, :], dst.at[slot * KB : (slot + 1) * KB, :], sems.at[n, slot]
                )
            )
    for copy in copies:
        copy.start()
    row = lax.broadcasted_iota(jnp.int32, start_ref.shape, 0)
    starts = jnp.zeros(start_ref.shape, jnp.int32)
    base = lax.axis_index(CTX) * blocks
    for slot, (local, valid) in enumerate(found):
        starts = jnp.where(row == slot, jnp.where(valid, (base + local) * KB, jnp.int32(1 << 29)), starts)
    start_ref[...] = starts
    for copy in copies:
        copy.wait()
    attend(0, first_token, start_ref, q_ref, key_ref, value_ref, out_ref, score_ref, weight_ref)


def blend_kernel(*refs):
    parts, (out_ref, low_ref, high_ref) = refs[:-3], refs[-3:]
    heads = out_ref.shape[1] // DH
    logs = []
    for part in parts:
        tile = part[:, heads * DH :].astype(F32)
        logs.append(
            tile + pltpu.roll(tile, LANES - heads, 1) + pltpu.roll(tile, LANES - 2 * heads, 1)
        )
    peak = functools.reduce(jnp.maximum, logs)
    shares = [jnp.exp(log - peak) for log in logs]
    total = functools.reduce(jnp.add, shares)
    shares = [share / total for share in shares]
    for head in range(heads):
        span = slice(head * DH, (head + 1) * DH)
        value = functools.reduce(
            jnp.add,
            [share[:, head : head + 1] * part[:, span].astype(F32) for share, part in zip(shares, parts)],
        ).astype(BF16)
        out_ref[:, span] = value
        at = head * DH % low_ref.shape[1]
        (low_ref if head * 2 < heads else high_ref)[:, at : at + DH] = value


def place():
    return lax.axis_index(HEAD) * lax.axis_size(SEC) + lax.axis_index(SEC)


def place_of(n, rows, count):
    n_sec = lax.axis_size(SEC)
    owner = lax.axis_index(CTX) ^ n
    other = ((owner % n_sec) != lax.axis_index(SEC)).astype(jnp.int32)
    return pl.multiple_of(other * (count // n_sec * rows) + owner // n_sec * rows, rows)


def product(rows_ref, weight_ref, source, keep_ref, send_ref, target, width, tile):
    half = rows_ref.shape[0] // 2
    for at in range(0, width, tile):
        size = min(tile, width - at)
        part = jnp.dot(
            rows_ref[...],
            weight_ref[:, source + at : source + at + size],
            preferred_element_type=F32,
        )
        keep_ref[:, target + at : target + at + size] = part[:half]
        send_ref[:, target + at : target + at + size] = part[half:].astype(BF16)


def project_kernel(tile, *refs):
    pieces, (weight_ref, keep_ref, send_ref, rows_ref) = refs[:-4], refs[-4:]
    rows = pieces[0].shape[0]
    half = pieces[2].shape[1]
    for n, parts in enumerate((pieces[:1], pieces[1:2], pieces[2:4], pieces[4:6])):
        at = pl.ds(place_of(n, rows, 4), rows)
        for i, part in enumerate(parts):
            rows_ref[at, i * half : i * half + part.shape[1]] = part[...]
    product(rows_ref, weight_ref, 0, keep_ref, send_ref, 0, weight_ref.shape[1], tile)


def fold_kernel(width, keep_ref, got_ref, keep_out, send_out):
    rows = keep_out.shape[0]
    head = lax.axis_index(HEAD)
    mine = pl.ds(pl.multiple_of(head * rows, rows), rows)
    other = pl.ds(pl.multiple_of((1 - head) * rows, rows), rows)
    keep_out[:, :width] = keep_ref[mine, :width] + got_ref[mine, :width].astype(F32)
    send_out[:, :width] = (keep_ref[other, :width] + got_ref[other, :width].astype(F32)).astype(BF16)
    if keep_ref.shape[1] > width:
        keep_out[:, width:] = keep_ref[mine, width:] + take_exact(got_ref[mine, width:])
        put_exact(send_out, slice(None), width, keep_ref[other, width:] + take_exact(got_ref[other, width:]))


def middle_kernel(stream_ref, keep_ref, got_ref, out_ref):
    out_ref[...] = (
        stream_ref[...].astype(F32) + (keep_ref[...] + got_ref[...].astype(F32))
    ).astype(BF16)


def put_exact(ref, rows, at, value):
    high = value.astype(BF16)
    ref[rows, at : at + LANES] = high
    ref[rows, at + LANES : at + 2 * LANES] = (value - high.astype(F32)).astype(BF16)


def take_exact(tile):
    return tile[:, :LANES].astype(F32) + tile[:, LANES:].astype(F32)


def prepare_kernel(piece_ref, gain_ref, row_ref, square_ref):
    model = piece_ref.shape[1]
    gain = gain_ref[:, pl.ds(pl.multiple_of(place() * model, model), model)]
    wide = piece_ref[...].astype(F32)
    row_ref[...] = (wide * gain).astype(BF16)
    square_ref[...] = jnp.broadcast_to(jnp.sum(wide * wide, axis=1, keepdims=True), square_ref.shape)


def first_gate_kernel(width, tile, *refs):
    pieces, squares = refs[:4], refs[4:8]
    gate_ref, up_ref, keep_ref, send_ref, rows_ref = refs[8:]
    rows = pieces[0].shape[0]
    half = rows_ref.shape[0] // 2
    for n, (piece, square) in enumerate(zip(pieces, squares)):
        at = place_of(n, rows, len(pieces))
        rows_ref[pl.ds(at, rows), :] = piece[...]

        @pl.when(at < half)
        def _():
            keep_ref[pl.ds(at, rows), 2 * width :] = square[...]

        @pl.when(at >= half)
        def _():
            put_exact(send_ref, pl.ds(pl.multiple_of(at - half, rows), rows), 2 * width, square[...])

    product(rows_ref, gate_ref, 0, keep_ref, send_ref, 0, width, tile)
    product(rows_ref, up_ref, 0, keep_ref, send_ref, width, width, tile)


def gate_kernel(start, width, tile, rows_ref, gate_ref, up_ref, keep_ref, send_ref):
    product(rows_ref, gate_ref, start, keep_ref, send_ref, 0, width, tile)
    product(rows_ref, up_ref, start, keep_ref, send_ref, width, width, tile)


def scale_kernel(model, keep_ref, got_ref, out_ref):
    at = keep_ref.shape[1] - LANES
    square = keep_ref[:, at:] + take_exact(got_ref[:, at:])
    out_ref[...] = lax.rsqrt(square / model + EPS)


def hidden_kernel(scale_ref, keep_ref, got_ref, out_ref):
    width = out_ref.shape[1]
    scale = scale_ref[...]
    for at in range(0, width, LANES):
        gate = keep_ref[:, at : at + LANES] + got_ref[:, at : at + LANES].astype(F32)
        up = keep_ref[:, width + at : width + at + LANES] + got_ref[
            :, width + at : width + at + LANES
        ].astype(F32)
        gate = gate * scale
        out_ref[:, at : at + LANES] = (
            gate / (1.0 + jnp.exp(-gate)) * (up * scale)
        ).astype(BF16)


def first_hidden_kernel(model, keep_ref, got_ref, out_ref, scale_ref):
    scale_kernel(model, keep_ref, got_ref, scale_ref)
    hidden_kernel(scale_ref, keep_ref, got_ref, out_ref)


def gather_rows(pieces, rows_ref):
    rows = pieces[0].shape[0]
    for n, piece in enumerate(pieces):
        at = pl.ds(pl.multiple_of((lax.axis_index(CTX) ^ place() ^ n) * rows, rows), rows)
        rows_ref[at, :] = piece[...]


def part_down_kernel(tile, start, *refs):
    pieces, weight_ref, so_far = refs[:4], refs[4], refs[5:-2]
    out_ref, rows_ref = refs[-2:]
    gather_rows(pieces, rows_ref)
    depth = rows_ref.shape[1]
    for at in range(0, weight_ref.shape[1], tile):
        columns = slice(at, at + tile)
        part = jnp.dot(
            rows_ref[...], weight_ref[start : start + depth, columns], preferred_element_type=F32
        )
        for ref in so_far:
            part = part + ref[:, columns]
        out_ref[:, columns] = part


def down_kernel(tile, first, *refs):
    pieces, (weight_ref, so_far_ref, own_ref) = refs[:4], refs[4:7]
    sends, rows_ref = refs[7:-1], refs[-1]
    gather_rows(pieces, rows_ref)
    rows = pieces[0].shape[0]
    depth = rows_ref.shape[1]
    start = weight_ref.shape[0] - depth
    for at in range(0, own_ref.shape[1], tile):
        source = slice(first + at, first + at + tile)
        target = slice(at, at + tile)
        part = so_far_ref[:, source] + jnp.dot(
            rows_ref[...], weight_ref[start:, source], preferred_element_type=F32
        )
        own_ref[:, target] = part[:rows]
        for n, send in enumerate(sends):
            send[:, target] = part[(n + 1) * rows : (n + 2) * rows].astype(send.dtype)


def add_kernel(own_ref, got_ref, out_ref):
    out_ref[...] = (own_ref[...] + got_ref[...].astype(F32)).astype(BF16)


def final_kernel(middle_ref, *refs):
    parts, out_ref = refs[:-1], refs[-1]
    width = out_ref.shape[1] * 3 // len(parts)
    for n in range(0, len(parts), 3):
        columns = slice(n // 3 * width, (n // 3 + 1) * width)
        own, near, far = parts[n : n + 3]
        total = own[...] + near[...].astype(F32) + far[...].astype(F32)
        out_ref[:, columns] = (middle_ref[:, columns].astype(F32) + total).astype(BF16)


def swap(x, axis):
    return lax.ppermute(x, axis, [(0, 1), (1, 0)])


def turn(x, axis, n, offset):
    return lax.ppermute(x, axis, [(i, i ^ offset) for i in range(n)])


def direct_body(
    queries,
    key_cache,
    value_cache,
    block_index,
    stream,
    out_weight,
    norm_gain,
    gate_weight,
    up_weight,
    down_weight,
):
    n_context, n_head, _ = (lax.axis_size(a) for a in ALL)
    rows, heads_width = queries.shape
    context_len = key_cache.shape[0] * n_context
    model = norm_gain.shape[0]
    total = rows * n_context
    blocks = key_cache.shape[0] // KB
    kv_width = key_cache.shape[1]
    order = (3, 2, 1)

    got_q = {m: turn(queries, CTX, n_context, m) for m in (2, 1)}
    got_q[3] = turn(got_q[2], CTX, n_context, 1)
    picked = struct((MOST * KB, kv_width), BF16)
    partial_out = struct((rows, heads_width + LANES), BF16)
    kv_dev = kv_width // DH
    tall = heads_width // kv_width * rows
    scratch = [
        pltpu.VMEM((kv_dev, tall, MOST * KB), F32),
        pltpu.VMEM((kv_dev, tall, MOST * KB), BF16),
    ]
    keys, values, starts, own_partial = call(
        functools.partial(first_attend_kernel, blocks, context_len - total),
        (picked, picked, struct((8, LANES), jnp.int32), partial_out),
        [SM, ANY, ANY, ANY],
        (block_index, in_hbm(queries), in_hbm(key_cache), in_hbm(value_cache)),
        scratch=[pltpu.VMEM((rows, heads_width), BF16)]
        + scratch
        + [pltpu.SemaphoreType.DMA((2, MOST)), pltpu.SemaphoreType.DMA],
    )
    partial = {0: own_partial}
    for m in order:
        partial[m] = call(
            functools.partial(attend, m, context_len - total),
            partial_out,
            [VM] * 4,
            (starts, got_q[m], keys, values),
            scratch=scratch,
        )
    back = {m: turn(partial[m], CTX, n_context, m) for m in order}
    back[0] = partial[0]
    low = struct((rows, heads_width // 2), BF16)
    blended, *halves = call(
        blend_kernel,
        (struct((rows, heads_width), BF16), low, low),
        [VM] * 4,
        tuple(back[m] for m in range(4)),
    )

    beside = turn(blended, CTX, n_context, 1)
    across = [turn(h, CTX, n_context, 2) for h in halves]
    relayed = [turn(h, CTX, n_context, 1) for h in across]
    attention = (blended, beside, *across, *relayed)
    width = out_weight.shape[1]
    keep, away = call(
        functools.partial(project_kernel, 512),
        (struct((n_head * rows, width), F32), struct((n_head * rows, width), BF16)),
        [VM] * 7,
        attention + (in_vmem(out_weight),),
        scratch=[pltpu.VMEM((total, heads_width), BF16)],
        cost=6,
    )
    got = swap(away, SEC)
    keep, away = call(
        functools.partial(fold_kernel, width),
        (struct((rows, width), F32), struct((rows, width), BF16)),
        [VM, VM],
        (keep, got),
        cost=6,
    )
    got = swap(away, HEAD)
    middle = call(middle_kernel, struct((rows, width), BF16), [VM] * 3, (stream, keep, got), cost=6)

    all_middle = {
        m: lax.ppermute(
            middle,
            ALL,
            [
                (a * n_context + b, (b ^ m) * n_context + a)
                for a in range(n_context)
                for b in range(n_context)
            ],
        )
        for m in (3, 0, 1, 2)
    }
    hidden_width = gate_weight.shape[1]
    first = hidden_width * 2 // 7 // (2 * LANES) * 2 * LANES
    second = (hidden_width - first) // 2 // LANES * LANES
    widths = (first, second, hidden_width - first - second)
    chunks = tuple((sum(widths[:c]), widths[c]) for c in range(len(widths)))
    hidden = []
    gate_vmem, up_vmem = in_vmem(gate_weight), in_vmem(up_weight)
    prepared = [
        call(
            prepare_kernel,
            (struct((rows, width), BF16), struct((rows, LANES), F32)),
            [VM, VM],
            (all_middle[m], norm_gain[None]),
            cost=0,
        )
        for m in range(4)
    ]
    scale = None
    for c, (start, chunk) in enumerate(chunks):
        extra = LANES if c == 0 else 0
        out = (
            struct((n_head * rows, 2 * chunk + extra), F32),
            struct((n_head * rows, 2 * chunk + 2 * extra), BF16),
        )
        if c == 0:
            keep, away, all_rows = call(
                functools.partial(first_gate_kernel, chunk, 512),
                out + (struct((total, width), BF16),),
                [VM] * 10,
                tuple(p[0] for p in prepared)
                + tuple(p[1] for p in prepared)
                + (gate_vmem, up_vmem),
            )
        else:
            keep, away = call(
                functools.partial(gate_kernel, start, chunk, 512),
                out,
                [VM] * 3,
                (all_rows, gate_vmem, up_vmem),
            )
        keep, away = call(
            functools.partial(fold_kernel, 2 * chunk),
            (
                struct((rows, 2 * chunk + extra), F32),
                struct((rows, 2 * chunk + 2 * extra), BF16),
            ),
            [VM, VM],
            (keep, swap(away, SEC)),
        )
        got = swap(away, HEAD)
        if c == 0:
            own, scale = call(
                functools.partial(first_hidden_kernel, model),
                (struct((rows, chunk), BF16), struct((rows, LANES), F32)),
                [VM] * 2,
                (keep, got),
            )
        else:
            own = call(hidden_kernel, struct((rows, chunk), BF16), [VM] * 3, (scale, keep, got))
        across = swap(own, HEAD)
        beside = swap(own, SEC)
        hidden.append((own, beside, across, swap(across, SEC)))
    out_width = down_weight.shape[1]
    down_vmem = in_vmem(down_weight)
    so_far = ()
    for c, (start, chunk) in enumerate(chunks[:-1]):
        so_far = (
            call(
                functools.partial(part_down_kernel, 512, start),
                struct((total, out_width), F32),
                [VM] * (5 + len(so_far)),
                hidden[c] + (down_vmem,) + so_far,
                scratch=[pltpu.VMEM((total, chunk), BF16)],
            ),
        )
    half = out_width // 2
    results = []
    for n in range(2):
        own, near, two, three = call(
            functools.partial(down_kernel, 512, n * half),
            tuple(struct((rows, half), t) for t in (F32, BF16, F32, BF16)),
            [VM] * 6,
            hidden[-1] + (down_vmem,) + so_far,
            scratch=[pltpu.VMEM((total, chunks[-1][1]), BF16)],
        )
        beside = turn(three, CTX, n_context, 1)
        pair = call(add_kernel, struct((rows, half), BF16), [VM] * 2, (two, beside))
        far = turn(pair, CTX, n_context, 2)
        results += [own, turn(near, CTX, n_context, 1), far]
    return call(
        final_kernel, struct((rows, out_width), BF16), [VM] * 7, (all_middle[0],) + tuple(results)
    )


def local_attention(gathered, key_cache, value_cache, block_index, context_index, context_len):
    group_size = HQ // KVH
    kv_dev = key_cache.shape[1] // DH
    blocks_dev = key_cache.shape[0] // KB
    total_tokens = gathered.shape[0]
    key_blocks = key_cache.reshape(blocks_dev, KB, kv_dev, DH)
    value_blocks = value_cache.reshape(blocks_dev, KB, kv_dev, DH)
    local_ids = context_index * blocks_dev + jnp.arange(blocks_dev, dtype=jnp.int32)
    member = jnp.any(block_index[:, :, None] == local_ids[None, None, :], axis=1)
    member_rank = jnp.cumsum(member.astype(jnp.int32), axis=1) - 1
    slot_hit = member[:, None, :] & (
        member_rank[:, None, :] == jnp.arange(MOST, dtype=jnp.int32)[None, :, None]
    )
    slot_block = jnp.sum(
        jnp.where(slot_hit, jnp.arange(blocks_dev, dtype=jnp.int32)[None, None, :], 0), axis=2
    )
    slot_valid = jnp.any(slot_hit, axis=2)
    picked_keys = jnp.take(key_blocks, slot_block[0], axis=0).reshape(MOST * KB, kv_dev, DH)
    picked_values = jnp.take(value_blocks, slot_block[0], axis=0).reshape(MOST * KB, kv_dev, DH)
    key_pos = (
        (local_ids[0] + slot_block[0])[:, None] * KB + jnp.arange(KB, dtype=jnp.int32)[None, :]
    ).reshape(-1)
    live_keys = jnp.broadcast_to(slot_valid[0][:, None], (MOST, KB)).reshape(-1)
    query_pos = context_len - total_tokens + jnp.arange(KB, dtype=jnp.int32)
    allowed = live_keys[None, :] & (key_pos[None, :] <= query_pos[:, None])
    query_block = gathered.reshape(KB, kv_dev, group_size, DH)
    scores = jnp.einsum(
        "qhgd,phd->hgqp", query_block, picked_keys, preferred_element_type=jnp.float32
    ) / math.sqrt(DH)
    scores = jnp.where(allowed[None, None], scores, -jnp.inf)
    peak_score = jnp.max(scores, axis=-1, keepdims=True)
    unnormed = jnp.exp(scores - peak_score)
    row_total = jnp.sum(unnormed, axis=-1)
    mixture = jnp.einsum(
        "hgqp,phd->qhgd",
        unnormed.astype(jnp.bfloat16),
        picked_values,
        preferred_element_type=jnp.float32,
    )
    result = mixture / jnp.transpose(row_total, (2, 0, 1))[..., None]
    log_total = jnp.transpose(peak_score[..., 0] + jnp.log(row_total), (2, 0, 1))
    out_list = result.reshape(KB, -1)
    lse_list = log_total.reshape(KB, -1)
    return (out_list, lse_list)


def general_body(
    queries,
    key_cache,
    value_cache,
    block_index,
    stream,
    out_weight,
    norm_gain,
    gate_weight,
    up_weight,
    down_weight,
):
    n_context = lax.axis_size(CTX)
    context_index = lax.axis_index(CTX)
    context_len = key_cache.shape[0] * n_context
    gathered = lax.all_gather(queries, CTX, axis=0, tiled=True)
    part_out, part_lse = local_attention(
        gathered, key_cache, value_cache, block_index, context_index, context_len
    )
    spread_out, spread_lse = (
        lax.all_to_all(part_out[:, None, :], CTX, split_axis=0, concat_axis=1, tiled=True),
        lax.all_to_all(part_lse[:, None, :], CTX, split_axis=0, concat_axis=1, tiled=True),
    )
    share_rows = spread_out.shape[0]
    head_count = spread_lse.shape[2]
    peak_value = jnp.max(spread_lse, axis=1, keepdims=True)
    share_weight = jnp.exp(spread_lse - peak_value)
    blended = jnp.sum(
        spread_out.reshape(share_rows, n_context, head_count, -1) * share_weight[..., None], axis=1
    )
    blended = blended / jnp.sum(share_weight, axis=1)[..., None]
    attention = lax.all_gather(
        blended.reshape(share_rows, -1).astype(jnp.bfloat16), CTX, axis=0, tiled=True
    )
    row_piece = attention
    projected = lax.psum_scatter(
        jnp.dot(row_piece, out_weight, preferred_element_type=jnp.float32),
        HS,
        scatter_dimension=0,
        tiled=True,
    )
    middle = (stream.astype(jnp.float32) + projected).astype(jnp.bfloat16)
    full_middle = lax.all_gather(middle, CTX, axis=1, tiled=True)
    middle_wide = full_middle.astype(jnp.float32)
    mean_square = jnp.mean(middle_wide * middle_wide, axis=-1, keepdims=True)
    normed = (middle_wide * lax.rsqrt(mean_square + 1e-05) * norm_gain).astype(jnp.bfloat16)
    normed_cols, middle_cols = (
        lax.all_to_all(normed, HS, split_axis=1, concat_axis=0, tiled=True),
        lax.all_to_all(full_middle, HS, split_axis=1, concat_axis=0, tiled=True),
    )
    row_piece = normed_cols
    gate_up = lax.psum_scatter(
        jnp.concatenate(
            [
                jnp.dot(row_piece, gate_weight, preferred_element_type=jnp.float32),
                jnp.dot(row_piece, up_weight, preferred_element_type=jnp.float32),
            ],
            axis=1,
        ),
        HS,
        scatter_dimension=0,
        tiled=True,
    )
    hidden_width = gate_weight.shape[1]
    hidden = (jax.nn.silu(gate_up[:, :hidden_width]) * gate_up[:, hidden_width:]).astype(
        jnp.bfloat16
    )
    all_hidden = lax.all_gather(hidden, HS, axis=0, tiled=True)
    row_piece = all_hidden
    down_part = lax.psum_scatter(
        jnp.dot(row_piece, down_weight, preferred_element_type=jnp.float32),
        CTX,
        scatter_dimension=0,
        tiled=True,
    )
    own_middle = lax.dynamic_slice_in_dim(
        middle_cols, context_index * down_part.shape[0], down_part.shape[0], 0
    )
    return (own_middle.astype(jnp.float32) + down_part).astype(jnp.bfloat16)


def solution(mesh):
    size = dict(mesh.shape)
    direct = size[CTX] == 4 and size[HEAD] == 2 and size[SEC] == 2
    return jax.shard_map(
        direct_body if direct else general_body,
        mesh=mesh,
        in_specs=(
            P(ROWS, HS),
            P(ROWS, HS),
            P(ROWS, HS),
            P("groups", None),
            P(("groups",) + HS, CTX),
            P(HS, CTX),
            P(),
            P(HS, CTX),
            P(HS, CTX),
            P(CTX, HS),
        ),
        out_specs=P(ROWS, HS),
        check_vma=False,
    )
```

```python
import functools
import math

import jax
import jax.numpy as jnp
from jax import lax
from jax.experimental import pallas as pl
from jax.experimental.pallas import tpu as pltpu
from jax.sharding import PartitionSpec as P


HQ = 64
KVH = 8
DH = 128
KB = 128
MOST = 4
LANES = 128
EPS = 1e-05
CTX, HEAD, SEC = "ctx", "head", "sec"
ALL = (CTX, HEAD, SEC)
HS = (HEAD, SEC)
ROWS = ("groups", CTX)


VM = pl.BlockSpec(memory_space=pltpu.VMEM)
SM = pl.BlockSpec(memory_space=pltpu.SMEM)
ANY = pl.BlockSpec(memory_space=pl.ANY)
F32 = jnp.float32
BF16 = jnp.bfloat16


def struct(shape, dtype):
    return jax.ShapeDtypeStruct(shape, dtype)


def call(kernel, out, in_specs, args, cost=3, scratch=(), vmem=8):
    outs = out if isinstance(out, (tuple, list)) else (out,)
    nbytes = sum(math.prod(a.shape) * a.dtype.itemsize for a in args)
    nbytes += sum(math.prod(o.shape) * o.dtype.itemsize for o in outs)
    return pl.pallas_call(
        kernel,
        out_shape=out,
        in_specs=in_specs,
        out_specs=jax.tree.map(lambda _: VM, out),
        scratch_shapes=scratch,
        compiler_params=pltpu.CompilerParams(vmem_limit_bytes=vmem << 20),
        cost_estimate=pl.CostEstimate(flops=cost * 10**9, bytes_accessed=nbytes, transcendentals=0),
    )(*args)


def in_vmem(x):
    return pltpu.with_memory_space_constraint(x, pltpu.VMEM)


def in_hbm(x):
    return pltpu.with_memory_space_constraint(x, pltpu.HBM)


def slots(index_ref, blocks):
    entries = index_ref.shape[1]
    base = lax.axis_index(CTX) * blocks
    first = jnp.int32(0)
    end = jnp.int32(0)
    for n in range(entries):
        block = index_ref[0, n]
        first += (block < base).astype(jnp.int32)
        end += (block < base + blocks).astype(jnp.int32)
    found = []
    for slot in range(MOST):
        entry = jnp.minimum(first + slot, entries - 1)
        local = jnp.clip(index_ref[0, entry] - base, 0, blocks - 1)
        found.append((local, first + slot < end))
    return found


def attend(offset, first_token, start_ref, q_ref, key_ref, value_ref, out_ref, score_ref, weight_ref):
    rows = q_ref.shape[0]
    heads = q_ref.shape[1] // DH
    kv_dev = key_ref.shape[1] // DH
    group = heads // kv_dev
    scale = 1.0 / math.sqrt(DH)
    token0 = first_token + (lax.axis_index(CTX) ^ offset) * rows
    ahead = (
        lax.broadcasted_iota(jnp.int32, (rows, KB), 1)
        - lax.broadcasted_iota(jnp.int32, (rows, KB), 0)
        - token0
    )
    allowed = [ahead + start_ref[slot : slot + 1, :] <= 0 for slot in range(MOST)]
    head_lane = lax.broadcasted_iota(jnp.int32, (rows, LANES), 1)
    peak_tile = jnp.zeros((rows, LANES), F32)
    total_tile = jnp.ones((rows, LANES), F32)
    for kv in range(kv_dev):
        stacked = jnp.concatenate(
            [q_ref[:, (kv * group + h) * DH : (kv * group + h + 1) * DH] for h in range(group)], axis=0
        )
        score_ref[kv] = lax.dot_general(
            stacked,
            key_ref[:, kv * DH : (kv + 1) * DH],
            (((1,), (1,)), ((), ())),
            preferred_element_type=F32,
        )
    for kv in range(kv_dev):
        for h in range(group):
            head = kv * group + h
            span = slice(h * rows, (h + 1) * rows)
            parts = [
                jnp.where(allowed[slot], score_ref[kv, span, slot * KB : (slot + 1) * KB], -1e30)
                for slot in range(MOST)
            ]
            peak = jnp.max(functools.reduce(jnp.maximum, parts), axis=1, keepdims=True)
            parts = [jnp.exp((p - peak) * scale) for p in parts]
            row_total = jnp.sum(functools.reduce(jnp.add, parts), axis=1, keepdims=True)
            for slot, p in enumerate(parts):
                weight_ref[kv, span, slot * KB : (slot + 1) * KB] = p.astype(BF16)
            peak_tile = jnp.where(head_lane == head, peak, peak_tile)
            total_tile = jnp.where(head_lane == head, row_total, total_tile)
    inverse = 1.0 / total_tile
    for kv in range(kv_dev):
        mixture = jnp.dot(
            weight_ref[kv], value_ref[:, kv * DH : (kv + 1) * DH], preferred_element_type=F32
        )
        for h in range(group):
            head = kv * group + h
            out_ref[:, head * DH : (head + 1) * DH] = (
                mixture[h * rows : (h + 1) * rows] * inverse[:, head : head + 1]
            ).astype(BF16)
    lse_tile = peak_tile * scale + jnp.log(total_tile)
    high = lse_tile.astype(BF16).astype(F32)
    rest = lse_tile - high
    mid = rest.astype(BF16).astype(F32)
    low = rest - mid
    tile = high + pltpu.roll(mid, heads, 1) + pltpu.roll(low, 2 * heads, 1)
    out_ref[:, heads * DH :] = tile.astype(BF16)


def first_attend_kernel(
    blocks, first_token, index_ref, q_hbm, key_hbm, value_hbm,
    key_ref, value_ref, start_ref, out_ref, q_ref, score_ref, weight_ref, sems, q_sem,
):
    copies = [pltpu.make_async_copy(q_hbm, q_ref, q_sem)]
    found = slots(index_ref, blocks)
    for slot, (local, _) in enumerate(found):
        rows = pl.ds(pl.multiple_of(local * KB, KB), KB)
        for n, (src, dst) in enumerate(((key_hbm, key_ref), (value_hbm, value_ref))):
            copies.append(
                pltpu.make_async_copy(
                    src.at[rows, :], dst.at[slot * KB : (slot + 1) * KB, :], sems.at[n, slot]
                )
            )
    for copy in copies:
        copy.start()
    row = lax.broadcasted_iota(jnp.int32, start_ref.shape, 0)
    starts = jnp.zeros(start_ref.shape, jnp.int32)
    base = lax.axis_index(CTX) * blocks
    for slot, (local, valid) in enumerate(found):
        starts = jnp.where(row == slot, jnp.where(valid, (base + local) * KB, jnp.int32(1 << 29)), starts)
    start_ref[...] = starts
    for copy in copies:
        copy.wait()
    attend(0, first_token, start_ref, q_ref, key_ref, value_ref, out_ref, score_ref, weight_ref)


def blend_kernel(*refs):
    out_ref = refs[-1]
    parts = refs[:-1]
    heads = out_ref.shape[1] // DH
    logs = []
    for part in parts:
        tile = part[:, heads * DH :].astype(F32)
        logs.append(
            tile + pltpu.roll(tile, LANES - heads, 1) + pltpu.roll(tile, LANES - 2 * heads, 1)
        )
    peak = functools.reduce(jnp.maximum, logs)
    shares = [jnp.exp(log - peak) for log in logs]
    total = functools.reduce(jnp.add, shares)
    shares = [share / total for share in shares]
    for head in range(heads):
        span = slice(head * DH, (head + 1) * DH)
        out_ref[:, span] = functools.reduce(
            jnp.add,
            [share[:, head : head + 1] * part[:, span].astype(F32) for share, part in zip(shares, parts)],
        ).astype(BF16)


def place():
    return lax.axis_index(HEAD) * lax.axis_size(SEC) + lax.axis_index(SEC)


def place_of(n, rows, count):
    n_sec = lax.axis_size(SEC)
    owner = lax.axis_index(CTX) ^ n
    other = ((owner % n_sec) != lax.axis_index(SEC)).astype(jnp.int32)
    return pl.multiple_of(other * (count // n_sec * rows) + owner // n_sec * rows, rows)


def product(rows_ref, weight_ref, source, keep_ref, send_ref, target, width, tile):
    half = rows_ref.shape[0] // 2
    for at in range(0, width, tile):
        size = min(tile, width - at)
        part = jnp.dot(
            rows_ref[...],
            weight_ref[:, source + at : source + at + size],
            preferred_element_type=F32,
        )
        keep_ref[:, target + at : target + at + size] = part[:half]
        send_ref[:, target + at : target + at + size] = part[half:].astype(BF16)


def project_kernel(tile, *refs):
    pieces, (weight_ref, keep_ref, send_ref, rows_ref) = refs[:-4], refs[-4:]
    rows = pieces[0].shape[0]
    for n, piece in enumerate(pieces):
        rows_ref[pl.ds(place_of(n, rows, len(pieces)), rows), :] = piece[...]
    product(rows_ref, weight_ref, 0, keep_ref, send_ref, 0, weight_ref.shape[1], tile)


def fold_kernel(width, keep_ref, got_ref, keep_out, send_out):
    rows = keep_out.shape[0]
    head = lax.axis_index(HEAD)
    mine = pl.ds(pl.multiple_of(head * rows, rows), rows)
    other = pl.ds(pl.multiple_of((1 - head) * rows, rows), rows)
    keep_out[:, :width] = keep_ref[mine, :width] + got_ref[mine, :width].astype(F32)
    send_out[:, :width] = (keep_ref[other, :width] + got_ref[other, :width].astype(F32)).astype(BF16)
    if keep_ref.shape[1] > width:
        keep_out[:, width:] = keep_ref[mine, width:] + take_exact(got_ref[mine, width:])
        put_exact(send_out, slice(None), width, keep_ref[other, width:] + take_exact(got_ref[other, width:]))


def middle_kernel(stream_ref, keep_ref, got_ref, out_ref):
    out_ref[...] = (
        stream_ref[...].astype(F32) + (keep_ref[...] + got_ref[...].astype(F32))
    ).astype(BF16)


def put_exact(ref, rows, at, value):
    high = value.astype(BF16)
    ref[rows, at : at + LANES] = high
    ref[rows, at + LANES : at + 2 * LANES] = (value - high.astype(F32)).astype(BF16)


def take_exact(tile):
    return tile[:, :LANES].astype(F32) + tile[:, LANES:].astype(F32)


def prepare_kernel(piece_ref, gain_ref, row_ref, square_ref):
    model = piece_ref.shape[1]
    gain = gain_ref[:, pl.ds(pl.multiple_of(place() * model, model), model)]
    wide = piece_ref[...].astype(F32)
    row_ref[...] = (wide * gain).astype(BF16)
    square_ref[...] = jnp.broadcast_to(jnp.sum(wide * wide, axis=1, keepdims=True), square_ref.shape)


def first_gate_kernel(width, tile, *refs):
    pieces, squares = refs[:4], refs[4:8]
    gate_ref, up_ref, keep_ref, send_ref, rows_ref = refs[8:]
    rows = pieces[0].shape[0]
    half = rows_ref.shape[0] // 2
    for n, (piece, square) in enumerate(zip(pieces, squares)):
        at = place_of(n, rows, len(pieces))
        rows_ref[pl.ds(at, rows), :] = piece[...]

        @pl.when(at < half)
        def _():
            keep_ref[pl.ds(at, rows), 2 * width :] = square[...]

        @pl.when(at >= half)
        def _():
            put_exact(send_ref, pl.ds(pl.multiple_of(at - half, rows), rows), 2 * width, square[...])

    product(rows_ref, gate_ref, 0, keep_ref, send_ref, 0, width, tile)
    product(rows_ref, up_ref, 0, keep_ref, send_ref, width, width, tile)


def gate_kernel(start, width, tile, rows_ref, gate_ref, up_ref, keep_ref, send_ref):
    product(rows_ref, gate_ref, start, keep_ref, send_ref, 0, width, tile)
    product(rows_ref, up_ref, start, keep_ref, send_ref, width, width, tile)


def scale_kernel(model, keep_ref, got_ref, out_ref):
    at = keep_ref.shape[1] - LANES
    square = keep_ref[:, at:] + take_exact(got_ref[:, at:])
    out_ref[...] = lax.rsqrt(square / model + EPS)


def hidden_kernel(scale_ref, keep_ref, got_ref, out_ref):
    width = out_ref.shape[1]
    scale = scale_ref[...]
    for at in range(0, width, LANES):
        gate = keep_ref[:, at : at + LANES] + got_ref[:, at : at + LANES].astype(F32)
        up = keep_ref[:, width + at : width + at + LANES] + got_ref[
            :, width + at : width + at + LANES
        ].astype(F32)
        gate = gate * scale
        out_ref[:, at : at + LANES] = (
            gate / (1.0 + jnp.exp(-gate)) * (up * scale)
        ).astype(BF16)


def first_hidden_kernel(model, keep_ref, got_ref, out_ref, scale_ref):
    scale_kernel(model, keep_ref, got_ref, scale_ref)
    hidden_kernel(scale_ref, keep_ref, got_ref, out_ref)


def gather_rows(pieces, rows_ref):
    rows = pieces[0].shape[0]
    for n, piece in enumerate(pieces):
        at = pl.ds(pl.multiple_of((lax.axis_index(CTX) ^ place() ^ n) * rows, rows), rows)
        rows_ref[at, :] = piece[...]


def part_down_kernel(tile, start, *refs):
    pieces, weight_ref, so_far = refs[:4], refs[4], refs[5:-2]
    out_ref, rows_ref = refs[-2:]
    gather_rows(pieces, rows_ref)
    depth = rows_ref.shape[1]
    for at in range(0, weight_ref.shape[1], tile):
        columns = slice(at, at + tile)
        part = jnp.dot(
            rows_ref[...], weight_ref[start : start + depth, columns], preferred_element_type=F32
        )
        for ref in so_far:
            part = part + ref[:, columns]
        out_ref[:, columns] = part


def down_kernel(tile, first, *refs):
    pieces, (weight_ref, so_far_ref, own_ref) = refs[:4], refs[4:7]
    sends, rows_ref = refs[7:-1], refs[-1]
    gather_rows(pieces, rows_ref)
    rows = pieces[0].shape[0]
    depth = rows_ref.shape[1]
    start = weight_ref.shape[0] - depth
    for at in range(0, own_ref.shape[1], tile):
        source = slice(first + at, first + at + tile)
        target = slice(at, at + tile)
        part = so_far_ref[:, source] + jnp.dot(
            rows_ref[...], weight_ref[start:, source], preferred_element_type=F32
        )
        own_ref[:, target] = part[:rows]
        for n, send in enumerate(sends):
            send[:, target] = part[(n + 1) * rows : (n + 2) * rows].astype(send.dtype)


def add_kernel(own_ref, got_ref, out_ref):
    out_ref[...] = (own_ref[...] + got_ref[...].astype(F32)).astype(BF16)


def final_kernel(middle_ref, *refs):
    parts, out_ref = refs[:-1], refs[-1]
    width = out_ref.shape[1] * 3 // len(parts)
    for n in range(0, len(parts), 3):
        columns = slice(n // 3 * width, (n // 3 + 1) * width)
        own, near, far = parts[n : n + 3]
        total = own[...] + near[...].astype(F32) + far[...].astype(F32)
        out_ref[:, columns] = (middle_ref[:, columns].astype(F32) + total).astype(BF16)


def swap(x, axis):
    return lax.ppermute(x, axis, [(0, 1), (1, 0)])


def turn(x, axis, n, offset):
    return lax.ppermute(x, axis, [(i, i ^ offset) for i in range(n)])


def direct_body(
    queries,
    key_cache,
    value_cache,
    block_index,
    stream,
    out_weight,
    norm_gain,
    gate_weight,
    up_weight,
    down_weight,
):
    n_context, n_head, _ = (lax.axis_size(a) for a in ALL)
    rows, heads_width = queries.shape
    context_len = key_cache.shape[0] * n_context
    model = norm_gain.shape[0]
    total = rows * n_context
    blocks = key_cache.shape[0] // KB
    kv_width = key_cache.shape[1]
    order = (3, 2, 1)

    got_q = {m: turn(queries, CTX, n_context, m) for m in (2, 1)}
    got_q[3] = turn(got_q[2], CTX, n_context, 1)
    picked = struct((MOST * KB, kv_width), BF16)
    partial_out = struct((rows, heads_width + LANES), BF16)
    kv_dev = kv_width // DH
    tall = heads_width // kv_width * rows
    scratch = [
        pltpu.VMEM((kv_dev, tall, MOST * KB), F32),
        pltpu.VMEM((kv_dev, tall, MOST * KB), BF16),
    ]
    keys, values, starts, own_partial = call(
        functools.partial(first_attend_kernel, blocks, context_len - total),
        (picked, picked, struct((8, LANES), jnp.int32), partial_out),
        [SM, ANY, ANY, ANY],
        (block_index, in_hbm(queries), in_hbm(key_cache), in_hbm(value_cache)),
        scratch=[pltpu.VMEM((rows, heads_width), BF16)]
        + scratch
        + [pltpu.SemaphoreType.DMA((2, MOST)), pltpu.SemaphoreType.DMA],
    )
    partial = {0: own_partial}
    for m in order:
        partial[m] = call(
            functools.partial(attend, m, context_len - total),
            partial_out,
            [VM] * 4,
            (starts, got_q[m], keys, values),
            scratch=scratch,
        )
    back = {m: turn(partial[m], CTX, n_context, m) for m in order}
    back[0] = partial[0]
    blended = call(
        blend_kernel, struct((rows, heads_width), BF16), [VM] * 4, tuple(back[m] for m in range(4))
    )

    attention = {m: turn(blended, CTX, n_context, m) for m in (2, 1)}
    attention[3] = turn(attention[2], CTX, n_context, 1)
    attention[0] = blended
    width = out_weight.shape[1]
    keep, away = call(
        functools.partial(project_kernel, 512),
        (struct((n_head * rows, width), F32), struct((n_head * rows, width), BF16)),
        [VM] * 5,
        tuple(attention[m] for m in range(4)) + (in_vmem(out_weight),),
        scratch=[pltpu.VMEM((total, heads_width), BF16)],
        cost=6,
    )
    got = swap(away, SEC)
    keep, away = call(
        functools.partial(fold_kernel, width),
        (struct((rows, width), F32), struct((rows, width), BF16)),
        [VM, VM],
        (keep, got),
        cost=6,
    )
    got = swap(away, HEAD)
    middle = call(middle_kernel, struct((rows, width), BF16), [VM] * 3, (stream, keep, got), cost=6)

    all_middle = {
        m: lax.ppermute(
            middle,
            ALL,
            [
                (a * n_context + b, (b ^ m) * n_context + a)
                for a in range(n_context)
                for b in range(n_context)
            ],
        )
        for m in (3, 0, 1, 2)
    }
    hidden_width = gate_weight.shape[1]
    first = hidden_width * 2 // 7 // (2 * LANES) * 2 * LANES
    second = (hidden_width - first) // 2 // LANES * LANES
    widths = (first, second, hidden_width - first - second)
    chunks = tuple((sum(widths[:c]), widths[c]) for c in range(len(widths)))
    hidden = []
    gate_vmem, up_vmem = in_vmem(gate_weight), in_vmem(up_weight)
    prepared = [
        call(
            prepare_kernel,
            (struct((rows, width), BF16), struct((rows, LANES), F32)),
            [VM, VM],
            (all_middle[m], norm_gain[None]),
            cost=0,
        )
        for m in range(4)
    ]
    scale = None
    for c, (start, chunk) in enumerate(chunks):
        extra = LANES if c == 0 else 0
        out = (
            struct((n_head * rows, 2 * chunk + extra), F32),
            struct((n_head * rows, 2 * chunk + 2 * extra), BF16),
        )
        if c == 0:
            keep, away, all_rows = call(
                functools.partial(first_gate_kernel, chunk, 512),
                out + (struct((total, width), BF16),),
                [VM] * 10,
                tuple(p[0] for p in prepared)
                + tuple(p[1] for p in prepared)
                + (gate_vmem, up_vmem),
                cost=0,
            )
        else:
            keep, away = call(
                functools.partial(gate_kernel, start, chunk, 512),
                out,
                [VM] * 3,
                (all_rows, gate_vmem, up_vmem),
                cost=0,
            )
        keep, away = call(
            functools.partial(fold_kernel, 2 * chunk),
            (
                struct((rows, 2 * chunk + extra), F32),
                struct((rows, 2 * chunk + 2 * extra), BF16),
            ),
            [VM, VM],
            (keep, swap(away, SEC)),
            cost=3 if start + chunk == hidden_width else 0,
        )
        got = swap(away, HEAD)
        if c == 0:
            own, scale = call(
                functools.partial(first_hidden_kernel, model),
                (struct((rows, chunk), BF16), struct((rows, LANES), F32)),
                [VM] * 2,
                (keep, got),
            )
        else:
            own = call(hidden_kernel, struct((rows, chunk), BF16), [VM] * 3, (scale, keep, got))
        across = swap(own, HEAD)
        beside = swap(own, SEC)
        hidden.append((own, beside, across, swap(across, SEC)))
    out_width = down_weight.shape[1]
    down_vmem = in_vmem(down_weight)
    so_far = ()
    for c, (start, chunk) in enumerate(chunks[:-1]):
        so_far = (
            call(
                functools.partial(part_down_kernel, 512, start),
                struct((total, out_width), F32),
                [VM] * (5 + len(so_far)),
                hidden[c] + (down_vmem,) + so_far,
                scratch=[pltpu.VMEM((total, chunk), BF16)],
            ),
        )
    half = out_width // 2
    results = []
    for n in range(2):
        own, near, two, three = call(
            functools.partial(down_kernel, 512, n * half),
            tuple(struct((rows, half), t) for t in (F32, BF16, F32, BF16)),
            [VM] * 6,
            hidden[-1] + (down_vmem,) + so_far,
            scratch=[pltpu.VMEM((total, chunks[-1][1]), BF16)],
        )
        beside = turn(three, CTX, n_context, 1)
        pair = call(add_kernel, struct((rows, half), BF16), [VM] * 2, (two, beside))
        far = turn(pair, CTX, n_context, 2)
        results += [own, turn(near, CTX, n_context, 1), far]
    return call(
        final_kernel, struct((rows, out_width), BF16), [VM] * 7, (all_middle[0],) + tuple(results)
    )


def local_attention(gathered, key_cache, value_cache, block_index, context_index, context_len):
    group_size = HQ // KVH
    kv_dev = key_cache.shape[1] // DH
    blocks_dev = key_cache.shape[0] // KB
    total_tokens = gathered.shape[0]
    key_blocks = key_cache.reshape(blocks_dev, KB, kv_dev, DH)
    value_blocks = value_cache.reshape(blocks_dev, KB, kv_dev, DH)
    local_ids = context_index * blocks_dev + jnp.arange(blocks_dev, dtype=jnp.int32)
    member = jnp.any(block_index[:, :, None] == local_ids[None, None, :], axis=1)
    member_rank = jnp.cumsum(member.astype(jnp.int32), axis=1) - 1
    slot_hit = member[:, None, :] & (
        member_rank[:, None, :] == jnp.arange(MOST, dtype=jnp.int32)[None, :, None]
    )
    slot_block = jnp.sum(
        jnp.where(slot_hit, jnp.arange(blocks_dev, dtype=jnp.int32)[None, None, :], 0), axis=2
    )
    slot_valid = jnp.any(slot_hit, axis=2)
    picked_keys = jnp.take(key_blocks, slot_block[0], axis=0).reshape(MOST * KB, kv_dev, DH)
    picked_values = jnp.take(value_blocks, slot_block[0], axis=0).reshape(MOST * KB, kv_dev, DH)
    key_pos = (
        (local_ids[0] + slot_block[0])[:, None] * KB + jnp.arange(KB, dtype=jnp.int32)[None, :]
    ).reshape(-1)
    live_keys = jnp.broadcast_to(slot_valid[0][:, None], (MOST, KB)).reshape(-1)
    query_pos = context_len - total_tokens + jnp.arange(KB, dtype=jnp.int32)
    allowed = live_keys[None, :] & (key_pos[None, :] <= query_pos[:, None])
    query_block = gathered.reshape(KB, kv_dev, group_size, DH)
    scores = jnp.einsum(
        "qhgd,phd->hgqp", query_block, picked_keys, preferred_element_type=jnp.float32
    ) / math.sqrt(DH)
    scores = jnp.where(allowed[None, None], scores, -jnp.inf)
    peak_score = jnp.max(scores, axis=-1, keepdims=True)
    unnormed = jnp.exp(scores - peak_score)
    row_total = jnp.sum(unnormed, axis=-1)
    mixture = jnp.einsum(
        "hgqp,phd->qhgd",
        unnormed.astype(jnp.bfloat16),
        picked_values,
        preferred_element_type=jnp.float32,
    )
    result = mixture / jnp.transpose(row_total, (2, 0, 1))[..., None]
    log_total = jnp.transpose(peak_score[..., 0] + jnp.log(row_total), (2, 0, 1))
    out_list = result.reshape(KB, -1)
    lse_list = log_total.reshape(KB, -1)
    return (out_list, lse_list)


def general_body(
    queries,
    key_cache,
    value_cache,
    block_index,
    stream,
    out_weight,
    norm_gain,
    gate_weight,
    up_weight,
    down_weight,
):
    n_context = lax.axis_size(CTX)
    context_index = lax.axis_index(CTX)
    context_len = key_cache.shape[0] * n_context
    gathered = lax.all_gather(queries, CTX, axis=0, tiled=True)
    part_out, part_lse = local_attention(
        gathered, key_cache, value_cache, block_index, context_index, context_len
    )
    spread_out, spread_lse = (
        lax.all_to_all(part_out[:, None, :], CTX, split_axis=0, concat_axis=1, tiled=True),
        lax.all_to_all(part_lse[:, None, :], CTX, split_axis=0, concat_axis=1, tiled=True),
    )
    share_rows = spread_out.shape[0]
    head_count = spread_lse.shape[2]
    peak_value = jnp.max(spread_lse, axis=1, keepdims=True)
    share_weight = jnp.exp(spread_lse - peak_value)
    blended = jnp.sum(
        spread_out.reshape(share_rows, n_context, head_count, -1) * share_weight[..., None], axis=1
    )
    blended = blended / jnp.sum(share_weight, axis=1)[..., None]
    attention = lax.all_gather(
        blended.reshape(share_rows, -1).astype(jnp.bfloat16), CTX, axis=0, tiled=True
    )
    row_piece = attention
    projected = lax.psum_scatter(
        jnp.dot(row_piece, out_weight, preferred_element_type=jnp.float32),
        HS,
        scatter_dimension=0,
        tiled=True,
    )
    middle = (stream.astype(jnp.float32) + projected).astype(jnp.bfloat16)
    full_middle = lax.all_gather(middle, CTX, axis=1, tiled=True)
    middle_wide = full_middle.astype(jnp.float32)
    mean_square = jnp.mean(middle_wide * middle_wide, axis=-1, keepdims=True)
    normed = (middle_wide * lax.rsqrt(mean_square + 1e-05) * norm_gain).astype(jnp.bfloat16)
    normed_cols, middle_cols = (
        lax.all_to_all(normed, HS, split_axis=1, concat_axis=0, tiled=True),
        lax.all_to_all(full_middle, HS, split_axis=1, concat_axis=0, tiled=True),
    )
    row_piece = normed_cols
    gate_up = lax.psum_scatter(
        jnp.concatenate(
            [
                jnp.dot(row_piece, gate_weight, preferred_element_type=jnp.float32),
                jnp.dot(row_piece, up_weight, preferred_element_type=jnp.float32),
            ],
            axis=1,
        ),
        HS,
        scatter_dimension=0,
        tiled=True,
    )
    hidden_width = gate_weight.shape[1]
    hidden = (jax.nn.silu(gate_up[:, :hidden_width]) * gate_up[:, hidden_width:]).astype(
        jnp.bfloat16
    )
    all_hidden = lax.all_gather(hidden, HS, axis=0, tiled=True)
    row_piece = all_hidden
    down_part = lax.psum_scatter(
        jnp.dot(row_piece, down_weight, preferred_element_type=jnp.float32),
        CTX,
        scatter_dimension=0,
        tiled=True,
    )
    own_middle = lax.dynamic_slice_in_dim(
        middle_cols, context_index * down_part.shape[0], down_part.shape[0], 0
    )
    return (own_middle.astype(jnp.float32) + down_part).astype(jnp.bfloat16)


def solution(mesh):
    size = dict(mesh.shape)
    direct = size[CTX] == 4 and size[HEAD] == 2 and size[SEC] == 2
    return jax.shard_map(
        direct_body if direct else general_body,
        mesh=mesh,
        in_specs=(
            P(ROWS, HS),
            P(ROWS, HS),
            P(ROWS, HS),
            P("groups", None),
            P(("groups",) + HS, CTX),
            P(HS, CTX),
            P(),
            P(HS, CTX),
            P(HS, CTX),
            P(CTX, HS),
        ),
        out_specs=P(ROWS, HS),
        check_vma=False,
    )
```
